32 devices in a mesh: tenant: 2 (over x), store: 16 (over z, y, core).
Axes of the slice: x: 2, y: 2, z: 4, core: 2. Of those that a mesh axis runs over, the one named last changes fastest.
Arguments:
- queries: bfloat16 [4096, 1024], P(('tenant', 'store')), parts along dimension 0, may hold values from -24 to 24
- own_kv: bfloat16 [4096, 256], P(('tenant', 'store')), parts along dimension 0, may hold values from -15 to 15
- store_kv: bfloat16 [1024, 256, 256], P(('tenant', 'store')), parts along dimension 0, may hold values from -15 to 15
- q_start: int32 [32], P(('tenant', 'store')), parts along dimension 0, may hold values from 12288 to 16255
- pop_ids: int32 [8], P('tenant'), parts along dimension 0, may hold values from 0 to 511
- pop_pos: int32 [32, 4], P(('tenant', 'store')), parts along dimension 0, may hold values from 0 to 12287
- rare_ids: int32 [32, 6], P(('tenant', 'store')), parts along dimension 0, may hold values from 0 to 511, as said below
- rare_count: int32 [32], P(('tenant', 'store')), parts along dimension 0, may hold values from 4 to 6, as said below
- rare_pos: int32 [32, 6], P(('tenant', 'store')), parts along dimension 0, may hold values from 0 to 12287
Outputs:
- attended: bfloat16 [4096, 1024], P(('tenant', 'store')), parts along dimension 0
The draws below stay inside these ranges and needn't reach their ends.
There are 2 independent parts, one for each index of `tenant`. The reference program is written for one: setup_inputs(seed, part) draws one part's arguments, and reference() takes and returns one part's arrays. A program takes and returns all parts, laid end to end along the dimension named above; each array names one. Nothing has to cross between parts.
Inputs may be any that keep to these rules, and one draw needn't show every extreme that they name: `rare_ids`: the first rare_count entries of one device's list name blocks of different holders (id // 32); entries after them are ignored. `rare_count`: some device requests exactly 6 blocks and another exactly 4.
All inputs are finite; a program needn't handle non-finite values.
Results may differ from the reference program's by a relative error of at most 0.0085.
The reference program's roundings to bfloat16 on the way count: a program that leaves them out, or rounds other values in their place, can miss the bound.
Values may be sent and summed in bfloat16 or wider, within the bound.
A program may use at most 128 MiB of HBM per device.

```python
import jax
import jax.numpy as jnp
from jax import lax

HD = 128
GROUP = 8
QT = 128
SPAN = 256
CH_DEV = 32
POP = 4
TOKENS = 2048
SPANS = 512
RMAX = 6
RMIN = 4
N_STORE = 16


def shared_direction(key):
    pair_count = max(1, min(4, HD // 16))
    feature = jnp.arange(HD, dtype=jnp.int32)
    chosen = feature % (HD // 2) >= HD // 2 - pair_count
    signs = 2.0 * jax.random.randint(jax.random.fold_in(key, 21), (HD,), 0, 2).astype(jnp.float32) - 1.0
    return jnp.where(chosen, signs, 0.0)


def shape_keys(key, raw, salt):
    direction = shared_direction(key)
    lead_shape = raw.shape[:-1]
    picked = jax.random.randint(jax.random.fold_in(key, salt + 7), lead_shape, 0, 32) == 0
    key_part = raw[..., :HD]
    value_part = raw[..., HD:]
    key_part = jnp.where(picked[..., None], 0.2 * key_part + 3.6 * direction, key_part)
    return jnp.clip(jnp.concatenate([key_part, value_part], axis=-1), -15.0, 15.0).astype(jnp.bfloat16)


def draw_queries(key, part):
    direction = jnp.tile(shared_direction(key), GROUP)
    base = jax.random.normal(key, (TOKENS, GROUP * HD), jnp.float32)
    base = base + 3.0 * direction[None, :]
    return jnp.clip(base, -24.0, 24.0).astype(jnp.bfloat16)


def draw_own_kv(key, part):
    main_key = jax.random.fold_in(key, 42)
    raw = 2.5 * jax.random.normal(main_key, (TOKENS, 2 * HD), jnp.float32)
    return shape_keys(key, raw, 42)


def draw_store_kv(key, part):
    main_key = jax.random.fold_in(key, 41)
    raw = 2.5 * jax.random.normal(main_key, (SPANS, SPAN, 2 * HD), jnp.float32)
    return shape_keys(key, raw, 41)


def rare_tables(key):
    key_hot = jax.random.fold_in(key, 11)
    key_noise = jax.random.fold_in(key, 12)
    key_slot = jax.random.fold_in(key, 13)
    key_count = jax.random.fold_in(key, 14)
    key_peak = jax.random.fold_in(key, 15)
    hot_order = jax.random.permutation(key_hot, N_STORE)
    bias = jnp.where(hot_order < 4, 1 << 22, 0).astype(jnp.int32)
    noise = jax.random.randint(key_noise, (N_STORE, N_STORE), 0, 1 << 20)
    score = (noise + bias[None, :]) * N_STORE + jnp.arange(N_STORE, dtype=jnp.int32)[None, :]
    ranked, holders = lax.top_k(score, RMAX)
    slot_pick = jax.random.randint(key_slot, (N_STORE, RMAX), 0, CH_DEV)
    block_ids = holders.astype(jnp.int32) * CH_DEV + slot_pick
    counts = jax.random.randint(key_count, (N_STORE,), RMIN, RMAX + 1)
    peak_dev = jax.random.randint(key_peak, (), 0, N_STORE)
    device_index = jnp.arange(N_STORE, dtype=jnp.int32)
    counts = jnp.where(device_index == peak_dev, RMAX, counts)
    counts = jnp.where(device_index == (peak_dev + 1) % N_STORE, RMIN, counts)
    return (block_ids.astype(jnp.int32), counts.astype(jnp.int32))


def draw_rare_ids(key, part):
    block_ids, counts = rare_tables(key)
    return block_ids


def draw_rare_count(key, part):
    block_ids, counts = rare_tables(key)
    return counts


def place_ends(drawn, key, smallest, largest):
    index_at = [jax.random.randint(jax.random.fold_in(key, axis), (), 0, length) for axis, length in enumerate(drawn.shape)]
    main_axis = drawn.shape.index(max(drawn.shape))
    neighbour = index_at[:main_axis] + [(index_at[main_axis] + 1) % drawn.shape[main_axis]] + index_at[main_axis + 1:]
    return drawn.at[tuple(index_at)].set(smallest).at[tuple(neighbour)].set(largest)


def setup_inputs(seed: int = 0, part: int = 0) -> dict:
    key_list = jax.random.split(jax.random.key(seed), 10)
    part_keys = jax.random.split(jax.random.fold_in(key_list[9], part), 10)
    return {
        "queries": draw_queries(jax.random.fold_in(jax.random.fold_in(key_list[9], part), 71), part),
        "own_kv": draw_own_kv(jax.random.fold_in(jax.random.fold_in(key_list[9], part), 71), part),
        "store_kv": draw_store_kv(jax.random.fold_in(jax.random.fold_in(key_list[9], part), 71), part),
        "q_start": place_ends(jax.random.randint(part_keys[3], (N_STORE,), 12288, 16384 - QT), jax.random.fold_in(part_keys[3], 1), 12288, (16384 - QT) - 1).astype(jnp.int32),
        "pop_ids": place_ends(jax.random.randint(part_keys[4], (POP,), 0, SPANS), jax.random.fold_in(part_keys[4], 1), 0, SPANS - 1).astype(jnp.int32),
        "pop_pos": place_ends(jax.random.randint(part_keys[5], (N_STORE, POP), 0, 12288), jax.random.fold_in(part_keys[5], 1), 0, 12287).astype(jnp.int32),
        "rare_ids": draw_rare_ids(jax.random.fold_in(jax.random.fold_in(key_list[9], part), 71), part),
        "rare_count": draw_rare_count(jax.random.fold_in(jax.random.fold_in(key_list[9], part), 71), part),
        "rare_pos": place_ends(jax.random.randint(part_keys[8], (N_STORE, RMAX), 0, 12288), jax.random.fold_in(part_keys[8], 1), 0, 12287).astype(jnp.int32),
    }


def rotate(values, positions, head_size):
    half_size = head_size // 2
    freq_table = 500000.0 ** (-(2.0 * jnp.arange(half_size, dtype=jnp.float32)) / head_size)
    angles = positions.astype(jnp.float32)[:, None] * freq_table[None, :]
    cosine = jnp.cos(angles)[:, None, :]
    sine_part = jnp.sin(angles)[:, None, :]
    shaped = values.reshape(values.shape[0], -1, 2, half_size)
    first_half = shaped[:, :, 0, :]
    second_half = shaped[:, :, 1, :]
    turned = jnp.stack([first_half * cosine - second_half * sine_part, second_half * cosine + first_half * sine_part], axis=2)
    return turned.reshape(values.shape)


def block_stats(query_rows, key_rows, value_rows, allowed, scale_factor):
    scores = jnp.dot(query_rows, key_rows.T, preferred_element_type=jnp.float32) * scale_factor
    scores = jnp.where(allowed, scores, -jnp.inf)
    top_score = jnp.max(scores, axis=1)
    weights = jnp.exp(scores - top_score[:, None]).astype(jnp.bfloat16)
    weight_sum = jnp.sum(weights.astype(jnp.float32), axis=1)
    mixed_part = jnp.dot(weights, value_rows, preferred_element_type=jnp.float32)
    return top_score, weight_sum, mixed_part


def reference(queries, own_kv, store_kv, q_start, pop_ids, pop_pos, rare_ids, rare_count, rare_pos):
    scale_factor = HD ** -0.5

    def one_device(inputs):
        query_block, own_block, start_pos, pop_offsets, rare_list, rare_total, rare_offsets = inputs
        positions = start_pos + jnp.arange(QT, dtype=jnp.int32)
        query_rows = rotate(query_block.astype(jnp.float32), positions, HD).astype(jnp.bfloat16).reshape(QT * GROUP, HD)
        own_keys = rotate(own_block[:, :HD].astype(jnp.float32), positions, HD).astype(jnp.bfloat16)
        causal = (jnp.arange(QT * GROUP) // GROUP)[:, None] >= jnp.arange(QT)[None, :]
        own_top, own_sum, own_mixed = block_stats(query_rows, own_keys, own_block[:, HD:], causal, scale_factor)
        span_list = jnp.concatenate([pop_ids, rare_list]).astype(jnp.int32)
        offsets = jnp.concatenate([pop_offsets, rare_offsets]).astype(jnp.int32)
        present = jnp.concatenate([jnp.ones((POP,), jnp.bool_), jnp.arange(RMAX) < rare_total])

        def span_stats(item):
            span_id, offset, is_present = item
            span_kv = lax.dynamic_index_in_dim(store_kv, span_id, 0, keepdims=False)
            span_keys = rotate(span_kv[:, :HD].astype(jnp.float32), offset + jnp.arange(SPAN, dtype=jnp.int32), HD).astype(jnp.bfloat16)
            top_score, weight_sum, mixed_part = block_stats(query_rows, span_keys, span_kv[:, HD:], True, scale_factor)
            return jnp.where(is_present, top_score, -jnp.inf), weight_sum, mixed_part

        tops, sums, mixes = lax.map(span_stats, (span_list, offsets, present))
        tops = jnp.concatenate([own_top[None], tops], axis=0)
        sums = jnp.concatenate([own_sum[None], sums], axis=0)
        mixes = jnp.concatenate([own_mixed[None], mixes], axis=0)
        peak = jnp.max(tops, axis=0)
        factor = jnp.exp(tops - peak[None, :])
        numer = jnp.sum(factor[:, :, None] * mixes, axis=0)
        denom = jnp.sum(factor * sums, axis=0)
        return (numer / denom[:, None]).reshape(QT, GROUP * HD).astype(jnp.bfloat16)

    result = lax.map(one_device, (queries.reshape(N_STORE, QT, GROUP * HD), own_kv.reshape(N_STORE, QT, 2 * HD), q_start, pop_pos, rare_ids, rare_count, rare_pos))
    return result.reshape(N_STORE * QT, GROUP * HD)
```

```python
import functools

import jax
import jax.numpy as jnp
import numpy as np
from jax import lax
from jax.experimental import pallas as pl
from jax.experimental.pallas import tpu as pltpu
from jax.sharding import PartitionSpec as P

MESH = pl.DeviceIdType.MESH
INNER = 4
STRIDE = 5
WINDOW = 7


def direct_kernel(
    n, per_device, requests, pops, chunk, power,
    pop_ref, request_ref, queries_ref, own_ref, store_hbm,
    base_cos, base_sin, step_cos, step_sin, out_ref,
    store, asks, asks_s, stage, recv, query_rows, total, tops,
    one_stage, one_recv, two_stage, two_recv, mid_stage, three_stage, popular,
    local_sem, ask_send, ask_recv, rare_send, rare_recv,
    one_send, one_sem, two_send, two_sem, mid_send, mid_sem, three_send, three_sem,
):
    me = lax.axis_index("store")
    inner, outer = lax.rem(me, INNER), me // INNER
    outers = n // INNER
    head = base_cos.shape[1]
    tokens = queries_ref.shape[0]
    rows = query_rows.shape[0]
    span = stage.shape[1]
    piece = span // INNER

    def ask_copy(slot, target):
        return pltpu.make_async_remote_copy(
            src_ref=request_ref, dst_ref=asks.at[slot],
            send_sem=ask_send.at[target], recv_sem=ask_recv.at[slot],
            device_id={"store": target}, device_id_type=MESH)

    def rare_copy(slot, target):
        return pltpu.make_async_remote_copy(
            src_ref=stage.at[target], dst_ref=recv.at[slot],
            send_sem=rare_send.at[target], recv_sem=rare_recv.at[slot],
            device_id={"store": target}, device_id_type=MESH)

    def one_copy(slot, target):
        return pltpu.make_async_remote_copy(
            src_ref=one_stage.at[target], dst_ref=one_recv.at[slot],
            send_sem=one_send.at[target], recv_sem=one_sem.at[slot],
            device_id={"store": outer * INNER + target}, device_id_type=MESH)

    def two_copy(slot, target):
        return pltpu.make_async_remote_copy(
            src_ref=two_stage.at[target], dst_ref=two_recv.at[slot],
            send_sem=two_send.at[target], recv_sem=two_sem.at[slot],
            device_id={"store": target * INNER + inner}, device_id_type=MESH)

    def mid_copy(slot, target):
        return pltpu.make_async_remote_copy(
            src_ref=mid_stage, dst_ref=three_stage.at[slot],
            send_sem=mid_send.at[target], recv_sem=mid_sem.at[slot],
            device_id={"store": target * INNER + inner}, device_id_type=MESH)

    def three_copy(slot, target):
        return pltpu.make_async_remote_copy(
            src_ref=three_stage, dst_ref=popular.at[slot],
            send_sem=three_send.at[target], recv_sem=three_sem.at[slot],
            device_id={"store": outer * INNER + target}, device_id_type=MESH)

    def peers(act):
        def step(s, carry):
            act(lax.rem(me + s, n))
            return carry
        lax.fori_loop(1, n, step, 0)

    load = pltpu.make_async_copy(store_hbm, store, local_sem.at[0])
    load.start()
    barrier = pltpu.get_barrier_semaphore()
    peers(lambda d: pl.semaphore_signal(
        barrier, inc=1, device_id={"store": d}, device_id_type=MESH))
    pl.semaphore_wait(barrier, n - 1)
    peers(lambda d: ask_copy(me, d).start())
    load.wait()

    for s in range(INNER):
        j = lax.rem(inner + s, INNER)
        begin = pl.multiple_of(j * piece, piece)
        for k in range(pops):
            part = store[lax.rem(pop_ref[k], per_device), pl.ds(begin, piece), :]
            if s == 0:
                one_recv[inner, k] = part
            else:
                one_stage[j, k] = part
        if s:
            one_copy(inner, j).start()

    cos0, sin0 = base_cos[0:1, :], base_sin[0:1, :]
    cos_n, sin_n = step_cos[:tokens, :], step_sin[:tokens, :]
    own_cos = cos0 * cos_n - sin0 * sin_n
    own_sin = sin0 * cos_n + cos0 * sin_n

    def turn(x, cosine, sine):
        x = x.astype(jnp.float32)
        return (x * cosine + pltpu.roll(x, head // 2, 1) * sine).astype(jnp.bfloat16)

    for g in range(rows // tokens):
        query_rows[g * tokens:(g + 1) * tokens, :] = turn(
            queries_ref[:, g * head:(g + 1) * head], own_cos, own_sin)

    pad = total.shape[0] - head

    def attend(keys, values, c, seen):
        at = pl.ds(c * chunk, chunk)
        scores = lax.dot_general(
            keys, query_rows[at, :], (((1,), (1,)), ((), ())),
            preferred_element_type=jnp.float32)
        if seen is not None:
            scores = jnp.where(seen, scores, -jnp.inf)
        top = jnp.max(scores, axis=0, keepdims=True)
        weights = jnp.exp2((scores - top) * power).astype(jnp.bfloat16)
        return top, jnp.dot(values, weights, preferred_element_type=jnp.float32)

    def flip(values):
        return jnp.concatenate(
            [values.T, jnp.ones((pad, values.shape[0]), jnp.bfloat16)], axis=0)

    def fold(block, base, live):
        cos_b, sin_b = base_cos[pl.ds(base, 1), :], base_sin[pl.ds(base, 1), :]
        cos_n, sin_n = step_cos[:span, :], step_sin[:span, :]
        keys = turn(
            block[:, :head], cos_b * cos_n - sin_b * sin_n, sin_b * cos_n + cos_b * sin_n)
        values = flip(block[:, head:])
        for c in range(rows // chunk):
            at = pl.ds(c * chunk, chunk)
            top, mixed = attend(keys, values, c, None)
            top = jnp.where(live, top, -jnp.inf)
            old = tops[:, at]
            diff = top - old
            factor = jnp.exp2(-jnp.abs(diff) * power)
            rises = diff > 0.0
            tops[:, at] = jnp.maximum(old, top)
            total[:, at] = (
                total[:, at] * jnp.where(rises, factor, 1.0)
                + mixed * jnp.where(rises, 1.0, factor))

    peers(lambda d: ask_copy(d, d).wait_recv())
    bring = pltpu.make_async_copy(asks, asks_s, local_sem.at[1])
    asks[me] = request_ref[...]
    bring.start()
    bring.wait()

    def slot_for(d):
        def look(r, slot):
            block_id = asks_s[d, 0, r]
            hit = (block_id // per_device == me) & (r < asks_s[d, 0, requests])
            return jnp.where(hit, lax.rem(block_id, per_device), slot)
        return lax.fori_loop(0, requests, look, jnp.int32(0), unroll=min(requests, 8))

    def reply(first, last):
        def step(s, carry):
            d = lax.rem(me + s * STRIDE, n)
            stage[d] = store[slot_for(d)]
            rare_copy(me, d).start()
            return carry
        lax.fori_loop(first, last, step, 0)

    cuts = [1, 3, 5, WINDOW + 1, n]
    reply(cuts[0], cuts[1])
    recv[me] = store[slot_for(me)]

    for s in range(1, INNER):
        j = lax.rem(inner + s, INNER)
        one_copy(j, j).wait_recv()
    for k in range(pops):
        two_stage[k] = one_recv[lax.rem(pop_ref[k] // per_device, INNER), k]
    for k in range(pops):
        @pl.when(outer != k)
        def _():
            two_copy(outer, k).start()

        @pl.when(outer == k)
        def _():
            two_recv[k] = two_stage[k]

    def rare_fold(h):
        def look(r, found):
            hit = (asks_s[me, 0, r] // per_device == h) & (r < asks_s[me, 0, requests])
            return jnp.where(hit, r, found)
        r = lax.fori_loop(0, requests, look, jnp.int32(-1), unroll=min(requests, 8))
        fold(recv[h], jnp.maximum(r, 0) + 1 + pops, r >= 0)

    def arrivals(first, last):
        def step(s, carry):
            h = lax.rem(me + (n - s) * STRIDE, n)
            rare_copy(h, h).wait_recv()
            rare_fold(h)

            @pl.when(s + WINDOW < n)
            def _():
                reply(s + WINDOW, s + WINDOW + 1)
            return carry
        lax.fori_loop(first, last, step, 0)

    reply(cuts[1], cuts[2])

    own_keys = turn(own_ref[:, :head], own_cos, own_sin)
    own_values = flip(own_ref[:, head:])
    for c in range(rows // chunk):
        at = pl.ds(c * chunk, chunk)
        token = lax.rem(
            lax.broadcasted_iota(jnp.int32, (tokens, chunk), 1) + c * chunk, tokens)
        seen = token >= lax.broadcasted_iota(jnp.int32, (tokens, chunk), 0)
        top, total[:, at] = attend(own_keys, own_values, c, seen)
        tops[:, at] = top

    rare_fold(me)

    @pl.when(outer < pops)
    def _():
        def two_wait(s, carry):
            d = lax.rem(outer + s, outers)
            pltpu.make_async_remote_copy(
                src_ref=mid_stage, dst_ref=two_recv.at[d],
                send_sem=mid_send.at[d], recv_sem=two_sem.at[d],
                device_id={"store": d * INNER + inner}, device_id_type=MESH).wait_recv()
            return carry
        lax.fori_loop(1, outers, two_wait, 0)
        mine = lax.rem(outer, pops)
        mid_stage[...] = two_recv[pop_ref[mine] // (per_device * INNER)]

        def mid_start(s, carry):
            mid_copy(mine, lax.rem(outer + s, outers)).start()
            return carry
        lax.fori_loop(1, outers, mid_start, 0)
        three_stage[mine] = mid_stage[...]

    reply(cuts[2], cuts[3])
    arrivals(cuts[0], cuts[1])
    for k in range(pops):
        @pl.when(outer != k)
        def _():
            mid_copy(k, k).wait_recv()
    for s in range(1, INNER):
        three_copy(inner, lax.rem(inner + s, INNER)).start()
    for k in range(pops):
        popular[inner, k] = three_stage[k]
    arrivals(cuts[1], cuts[3])

    for s in range(1, INNER):
        j = lax.rem(inner + s, INNER)
        three_copy(j, j).wait_recv()

    def popular_fold(k, carry):
        block = jnp.concatenate([popular[j, k] for j in range(INNER)], axis=0)
        fold(block, k + 1, True)
        return carry
    lax.fori_loop(0, pops, popular_fold, 0)

    arrivals(cuts[3], cuts[4])

    for g in range(rows // tokens):
        at = pl.ds(g * tokens, tokens)
        out_ref[:, g * head:(g + 1) * head] = (
            total[:head, at] / total[head:head + 1, at]).T.astype(jnp.bfloat16)

    peers(lambda d: ask_copy(d, d).wait_send())
    peers(lambda d: rare_copy(d, d).wait_send())
    for s in range(1, INNER):
        j = lax.rem(inner + s, INNER)
        one_copy(j, j).wait_send()
        three_copy(j, j).wait_send()

    for k in range(pops):
        @pl.when(outer != k)
        def _():
            two_copy(k, k).wait_send()

    @pl.when(outer < pops)
    def _():
        def mid_done(s, carry):
            d = lax.rem(outer + s, outers)
            mid_copy(lax.rem(outer, pops), d).wait_send()
            return carry
        lax.fori_loop(1, outers, mid_done, 0)


def direct_body(queries, own_kv, store_kv, q_start, pop_ids, pop_pos, rare_ids, rare_count, rare_pos):
    n = lax.axis_size("store")
    tokens = queries.shape[0]
    head = own_kv.shape[1] // 2
    rows = tokens * (queries.shape[1] // head)
    per_device, span, width = store_kv.shape
    requests = rare_ids.shape[1]
    pops = pop_ids.shape[0]
    longest = max(span, tokens)
    lanes = -(-(requests + 1) // 128) * 128
    outers = n // INNER
    piece = span // INNER

    half = np.arange(head) % (head // 2)
    freq = 500000.0 ** (-(2.0 * half) / head)
    sign = np.where(np.arange(head) < head // 2, -1.0, 1.0)
    steps = np.arange(longest)[:, None] * freq[None, :]
    step_cos = np.cos(steps).astype(np.float32)
    step_sin = (np.sin(steps) * sign).astype(np.float32)
    base = jnp.concatenate([q_start, pop_pos[0], rare_pos[0]]).astype(jnp.float32)
    angles = base[:, None] * freq.astype(np.float32)[None, :]
    base_cos = jnp.cos(angles)
    base_sin = jnp.sin(angles) * sign.astype(np.float32)[None, :]
    table = jnp.concatenate([rare_ids[0], rare_count])
    table = jnp.pad(table, (0, lanes - requests - 1))

    vmem = pl.BlockSpec(memory_space=pltpu.VMEM)
    smem = pl.BlockSpec(memory_space=pltpu.SMEM)
    dma = pltpu.SemaphoreType.DMA
    bf16 = jnp.bfloat16
    chunk = min(rows, 512)
    return pl.pallas_call(
        functools.partial(direct_kernel, n, per_device, requests, pops, chunk, head ** -0.5 * np.log2(np.e).item()),
        out_shape=jax.ShapeDtypeStruct(queries.shape, bf16),
        in_specs=[smem, vmem, vmem, vmem, pl.BlockSpec(memory_space=pl.ANY)] + [vmem] * 4,
        out_specs=vmem,
        scratch_shapes=[
            pltpu.VMEM((per_device, span, width), bf16),
            pltpu.VMEM((n, 1, lanes), jnp.int32),
            pltpu.SMEM((n, 1, lanes), jnp.int32),
            pltpu.VMEM((n, span, width), bf16),
            pltpu.VMEM((n, span, width), bf16),
            pltpu.VMEM((rows, head), bf16),
            pltpu.VMEM((head + 16, rows), jnp.float32),
            pltpu.VMEM((1, rows), jnp.float32),
            pltpu.VMEM((INNER, pops, piece, width), bf16),
            pltpu.VMEM((INNER, pops, piece, width), bf16),
            pltpu.VMEM((pops, piece, width), bf16),
            pltpu.VMEM((outers, piece, width), bf16),
            pltpu.VMEM((piece, width), bf16),
            pltpu.VMEM((pops, piece, width), bf16),
            pltpu.VMEM((INNER, pops, piece, width), bf16),
            dma((2,)), dma((n,)), dma((n,)), dma((n,)), dma((n,)),
            dma((INNER,)), dma((INNER,)), dma((outers,)), dma((outers,)), dma((outers,)), dma((pops,)),
            dma((INNER,)), dma((INNER,)),
        ],
        compiler_params=pltpu.CompilerParams(
            collective_id=0, has_side_effects=True, vmem_limit_bytes=60 * 2**20),
    )(pop_ids, table.reshape(1, lanes), queries, own_kv, store_kv,
      base_cos, base_sin, step_cos, step_sin)


PLANES = 4
LANES = 4
SLOTS = 6
SLACK = 2
COARSE = 128


def relay_kernel(
    per_device, requests, pops, power,
    pop_ref, ids_ref, count_ref, rare_pos, pop_pos, start_ref,
    queries_ref, own_ref, store_hbm, coarse_cos, coarse_sin, step_cos, step_sin, out_ref,
    store, row, asks, asks_s, choice, info, query_rows, total, tops,
    far_stage, hop, cand, near_stage, list_stage, recv,
    one_stage, one_recv, two_stage, two_recv, mid_stage, three_stage, popular,
    local_sem, ask_send, ask_recv, far_send, hop_sem, fwd_send, cand_sem, near_send, list_send, recv_sem,
    one_send, one_sem, two_send, two_sem, mid_send, mid_sem, three_send, three_sem,
):
    n = PLANES * LANES
    me = lax.axis_index("store")
    plane, lane = me // LANES, lax.rem(me, LANES)
    half = plane // 2
    inner = jnp.where(half == 0, plane, 3 - plane)
    is_inner, is_outer = inner == 1, inner == 0
    head = step_cos.shape[1]
    tokens = queries_ref.shape[0]
    rows = query_rows.shape[0]
    span = store.shape[1]
    piece = span // LANES

    def device(h, u, t):
        return (u + h * (3 - 2 * u)) * LANES + t

    def place(u, d):
        return (d & 1) + (d >> 1) * 4 + (1 - u) * 2

    def remote(src, dst, send, recv_at, target):
        return pltpu.make_async_remote_copy(
            src_ref=src, dst_ref=dst, send_sem=send, recv_sem=recv_at,
            device_id={"store": target}, device_id_type=MESH)

    def ask_copy(slot, target):
        return remote(row, asks.at[slot], ask_send.at[target], ask_recv.at[slot], target)

    def far_copy(q, d):
        at = q * 4 + d
        return remote(
            far_stage.at[at], cand.at[q * 8 + place(inner, d)], far_send.at[at],
            cand_sem.at[q * 8 + place(inner, d)], device(half, 1, lane ^ d))

    def hop_copy(q, d):
        at = q * 4 + d
        return remote(
            far_stage.at[at], hop.at[q * 2 + d - 2], far_send.at[at],
            hop_sem.at[q * 2 + d - 2], device(half, 0, lane ^ d))

    def forward_copy(q, j):
        at = q * 8 + place(0, 2 + j)
        return remote(
            hop.at[q * 2 + j], cand.at[at], fwd_send.at[q * 2 + j], cand_sem.at[at],
            device(half, 1, lane))

    def near_copy(rel, d):
        at = rel * 4 + d
        return remote(
            near_stage.at[at], recv.at[at], near_send.at[at], recv_sem.at[at],
            device(half, inner ^ rel, lane ^ d))

    def list_copy(q, s):
        at = q * SLOTS + s
        return remote(
            list_stage.at[at], recv.at[8 + s], list_send.at[at], recv_sem.at[8 + s],
            device(1 - half, q, lane))

    def one_copy(d):
        return remote(
            one_stage.at[d], one_recv.at[d], one_send.at[d], one_sem.at[d],
            plane * LANES + (lane ^ d))

    def two_copy(d):
        return remote(
            two_stage.at[plane ^ d], two_recv.at[d], two_send.at[d], two_sem.at[d],
            (plane ^ d) * LANES + lane)

    def mid_copy(d):
        return remote(
            mid_stage, three_stage.at[d], mid_send.at[d], mid_sem.at[d],
            (plane ^ d) * LANES + lane)

    def three_copy(d):
        return remote(
            three_stage, popular.at[d], three_send.at[d], three_sem.at[d],
            plane * LANES + (lane ^ d))

    def peers(act):
        def step(s, carry):
            act(lax.rem(me + s, n))
            return carry
        lax.fori_loop(1, n, step, 0)

    load = pltpu.make_async_copy(store_hbm, store, local_sem.at[0])
    load.start()
    barrier = pltpu.get_barrier_semaphore()
    peers(lambda d: pl.semaphore_signal(
        barrier, inc=1, device_id={"store": d}, device_id_type=MESH))

    spot = lax.broadcasted_iota(jnp.int32, row.shape, 1)
    wanted = jnp.full(row.shape, -1, jnp.int32)
    for r in range(requests):
        block_id = ids_ref[0, r]
        holder = jnp.where(r < count_ref[0], block_id // per_device, -1)
        wanted = jnp.where(spot == holder, lax.rem(block_id, per_device) + r * per_device, wanted)
    row[...] = wanted
    asks[me] = wanted

    def base_of(position):
        a, b = position // COARSE, lax.rem(position, COARSE)
        ca, sa = coarse_cos[pl.ds(a, 1), :], coarse_sin[pl.ds(a, 1), :]
        cb, sb = step_cos[pl.ds(b, 1), :], step_sin[pl.ds(b, 1), :]
        return ca * cb - sa * sb, sa * cb + ca * sb

    def table(position, count):
        cos_b, sin_b = base_of(position)
        cos_n, sin_n = step_cos[:count, :], step_sin[:count, :]
        return cos_b * cos_n - sin_b * sin_n, sin_b * cos_n + cos_b * sin_n

    def turn(x, cosine, sine):
        x = x.astype(jnp.float32)
        return (x * cosine + pltpu.roll(x, head // 2, 1) * sine).astype(jnp.bfloat16)

    own_cos, own_sin = table(start_ref[0], tokens)
    for g in range(rows // tokens):
        query_rows[g * tokens:(g + 1) * tokens, :] = turn(
            queries_ref[:, g * head:(g + 1) * head], own_cos, own_sin)

    pad = total.shape[0] - head

    def attend(keys, values, seen):
        scores = lax.dot_general(
            keys, query_rows[...], (((1,), (1,)), ((), ())),
            preferred_element_type=jnp.float32)
        if seen is not None:
            scores = jnp.where(seen, scores, -jnp.inf)
        top = jnp.max(scores, axis=0, keepdims=True)
        weights = jnp.exp2((scores - top) * power).astype(jnp.bfloat16)
        return top, jnp.dot(values, weights, preferred_element_type=jnp.float32)

    def flip(values):
        return jnp.concatenate(
            [values.T, jnp.ones((pad, values.shape[0]), jnp.bfloat16)], axis=0)

    def fold(block, position, live):
        keys = turn(block[:, :head], *table(position, span))
        values = flip(block[:, head:])
        top, mixed = attend(keys, values, None)
        top = jnp.where(live, top, -jnp.inf)
        old = tops[...]
        diff = top - old
        factor = jnp.exp2(-jnp.abs(diff) * power)
        rises = diff > 0.0
        tops[...] = jnp.maximum(old, top)
        total[...] = (
            total[...] * jnp.where(rises, factor, 1.0)
            + mixed * jnp.where(rises, 1.0, factor))

    load.wait()
    for d in range(LANES):
        begin = pl.multiple_of((lane ^ d) * piece, piece)
        for k in range(pops):
            part = store[lax.rem(pop_ref[k], per_device), pl.ds(begin, piece), :]
            if d == 0:
                one_recv[0, k] = part
            else:
                one_stage[d, k] = part

    pl.semaphore_wait(barrier, n - 1)
    peers(lambda d: ask_copy(me, d).start())
    for d in range(1, LANES):
        one_copy(d).start()

    token = lax.rem(lax.broadcasted_iota(jnp.int32, (tokens, rows), 1), tokens)
    seen = token >= lax.broadcasted_iota(jnp.int32, (tokens, rows), 0)
    top, mixed = attend(
        turn(own_ref[:, :head], own_cos, own_sin), flip(own_ref[:, head:]), seen)
    total[...] = mixed
    tops[...] = top

    peers(lambda d: ask_copy(d, d).wait_recv())
    bring = pltpu.make_async_copy(asks, asks_s, local_sem.at[1])
    bring.start()
    bring.wait()

    def block_for(target):
        return store[lax.rem(jnp.maximum(asks_s[target, 0, me], 0), per_device)]

    def far_block(q, d):
        return block_for(device(1 - half, q, lane ^ d))

    def far_send_to_relay(q, d):
        far_stage[q * 4 + d] = far_block(q, d)
        far_copy(q, d).start()

    def far_send_to_hop(q, d):
        far_stage[q * 4 + d] = far_block(q, d)
        hop_copy(q, d).start()

    def near_send_one(rel, d):
        near_stage[rel * 4 + d] = block_for(device(half, inner ^ rel, lane ^ d))
        near_copy(rel, d).start()

    @pl.when(is_outer)
    def _():
        for d in (0, 1):
            far_send_to_relay(0, d)
        for d in (2, 3):
            far_send_to_hop(0, d)
        for d in (2, 3):
            far_send_to_hop(1, d)

    @pl.when(is_inner)
    def _():
        for q in (0, 1):
            cand[q * 8] = far_block(q, 0)
            for d in (1, 2, 3):
                far_send_to_relay(q, d)

    def assign(requester, h, name):
        found = [jnp.int32(-1)] * SLOTS
        last = jnp.int32(-1)
        for i in range(SLOTS + SLACK):
            d, u = (i & 1) + ((i >> 2) << 1), 1 - ((i >> 1) & 1)
            value = asks_s[requester, 0, device(h, u, lane ^ d)]
            there = value >= 0
            slot = jnp.maximum(last + 1, i - SLACK)
            for s in range(max(0, i - SLACK), min(i, SLOTS - 1) + 1):
                found[s] = jnp.where(there & (slot == s), name(i, value), found[s])
            last = jnp.where(there, slot, last)
        return found

    @pl.when(is_inner)
    def _():
        for q in (0, 1):
            for s, i in enumerate(assign(device(1 - half, q, lane), half, lambda i, value: i)):
                choice[q * SLOTS + s] = i

    for rel in (0, 1):
        for d in range(LANES):
            value = asks_s[me, 0, device(half, inner ^ rel, lane ^ d)]
            info[rel * 4 + d] = jnp.where(value >= 0, value // per_device, -1)
    for s, r in enumerate(assign(me, 1 - half, lambda i, value: value // per_device)):
        info[8 + s] = r

    for d in range(1, LANES):
        one_copy(d).wait_recv()
    for k in range(pops):
        two_stage[k] = one_recv[lane ^ lax.rem(pop_ref[k] // per_device, LANES), k]
    two_recv[0] = two_stage[plane]
    for d in range(1, PLANES):
        two_copy(d).start()

    def wait_cand(at):
        remote(far_stage.at[0], cand.at[at], far_send.at[0], cand_sem.at[at], me ^ 1).wait_recv()

    def relay(q, s):
        at = q * 8 + s
        wait_cand(at + 2)
        pick = choice[q * SLOTS + s]
        list_stage[q * SLOTS + s] = jnp.where(
            pick == s, cand[at], jnp.where(pick == s + 1, cand[at + 1], cand[at + 2]))
        list_copy(q, s).start()

    def start_forward(q, j):
        remote(far_stage.at[0], hop.at[q * 2 + j], far_send.at[0], hop_sem.at[q * 2 + j], me ^ 1).wait_recv()
        forward_copy(q, j).start()

    @pl.when(is_outer)
    def _():
        start_forward(0, 0)
        start_forward(0, 1)
        for d in (0, 1):
            far_send_to_relay(1, d)

    @pl.when(is_inner)
    def _():
        wait_cand(1)
        relay(0, 0)
        relay(0, 1)

    recv[0] = block_for(me)
    for d in range(1, LANES):
        near_send_one(0, d)

    for d in range(1, PLANES):
        two_copy(d).wait_recv()
    mid_stage[...] = two_recv[plane ^ (pop_ref[plane] // (per_device * LANES))]
    for d in range(1, PLANES):
        mid_copy(d).start()
    three_stage[0] = mid_stage[...]

    def rare_fold(i):
        r = info[i]
        fold(recv[i], rare_pos[0, jnp.maximum(r, 0)], r >= 0)

    def wait_block(i):
        remote(near_stage.at[0], recv.at[i], near_send.at[0], recv_sem.at[i], me ^ 1).wait_recv()

    def first(k, carry):
        @pl.when(is_inner)
        def _():
            relay(0, k)

        @pl.when(is_outer & (k < 4))
        def _():
            start_forward(1, k - 2)
        near_send_one(1, k - 2)

        @pl.when(k > 2)
        def _():
            wait_block(k - 2)
        rare_fold(k - 2)
        return carry
    lax.fori_loop(2, SLOTS, first, 0)

    for d in range(1, PLANES):
        mid_copy(d).wait_recv()
    for d in range(1, LANES):
        three_copy(d).start()
    popular[0] = three_stage[...]

    @pl.when(is_inner)
    def _():
        wait_cand(8 + 1)
        relay(1, 0)
        relay(1, 1)

    for d in range(1, LANES):
        three_copy(d).wait_recv()

    def second(k, carry):
        @pl.when(is_inner)
        def _():
            relay(1, k + 2)
        block = jnp.concatenate([popular[lane ^ j, plane ^ k] for j in range(LANES)], axis=0)
        fold(block, pop_pos[0, k], True)
        return carry
    lax.fori_loop(0, pops, second, 0)

    def third(e, carry):
        i = jnp.where(e < 3, 8 + e, jnp.where(e < 7, e + 1, e + 4))
        wait_block(i)
        rare_fold(i)
        return carry
    lax.fori_loop(0, 10, third, 0)

    for g in range(rows // tokens):
        at = pl.ds(g * tokens, tokens)
        out_ref[:, g * head:(g + 1) * head] = (
            total[:head, at] / total[head:head + 1, at]).T.astype(jnp.bfloat16)

    peers(lambda d: ask_copy(d, d).wait_send())
    for rel in (0, 1):
        for d in range(LANES):
            if rel or d:
                near_copy(rel, d).wait_send()
    for q in (0, 1):
        @pl.when(is_outer)
        def _():
            for d in range(LANES):
                (far_copy if d < 2 else hop_copy)(q, d).wait_send()
            for j in (0, 1):
                forward_copy(q, j).wait_send()

        @pl.when(is_inner)
        def _():
            for d in range(1, LANES):
                far_copy(q, d).wait_send()
            for s in range(SLOTS):
                list_copy(q, s).wait_send()
    for d in range(1, LANES):
        one_copy(d).wait_send()
        three_copy(d).wait_send()
    for d in range(1, PLANES):
        two_copy(d).wait_send()
        mid_copy(d).wait_send()


def relay_body(queries, own_kv, store_kv, q_start, pop_ids, pop_pos, rare_ids, rare_count, rare_pos):
    n = lax.axis_size("store")
    tokens = queries.shape[0]
    head = own_kv.shape[1] // 2
    rows = tokens * (queries.shape[1] // head)
    per_device, span, width = store_kv.shape
    requests = rare_ids.shape[1]
    pops = pop_ids.shape[0]
    longest = max(span, tokens, COARSE)
    piece = span // LANES

    half = np.arange(head) % (head // 2)
    freq = 500000.0 ** (-(2.0 * half) / head)
    sign = np.where(np.arange(head) < head // 2, -1.0, 1.0)

    def tables(positions):
        angles = positions[:, None] * freq[None, :]
        return np.cos(angles).astype(np.float32), (np.sin(angles) * sign).astype(np.float32)

    vmem = pl.BlockSpec(memory_space=pltpu.VMEM)
    smem = pl.BlockSpec(memory_space=pltpu.SMEM)
    dma = pltpu.SemaphoreType.DMA
    bf16 = jnp.bfloat16

    def blocks(count):
        return pltpu.VMEM((count, span, width), bf16)

    def pieces(*lead):
        return pltpu.VMEM((*lead, piece, width), bf16)

    return pl.pallas_call(
        functools.partial(relay_kernel, per_device, requests, pops, head ** -0.5 * np.log2(np.e).item()),
        out_shape=jax.ShapeDtypeStruct(queries.shape, bf16),
        in_specs=[smem] * 6 + [vmem, vmem, pl.BlockSpec(memory_space=pl.ANY)] + [vmem] * 4,
        out_specs=vmem,
        scratch_shapes=[
            blocks(per_device),
            pltpu.VMEM((1, 128), jnp.int32),
            pltpu.VMEM((n, 1, 128), jnp.int32),
            pltpu.SMEM((n, 1, 128), jnp.int32),
            pltpu.SMEM((2 * SLOTS,), jnp.int32),
            pltpu.SMEM((8 + SLOTS,), jnp.int32),
            pltpu.VMEM((rows, head), bf16),
            pltpu.VMEM((head + 16, rows), jnp.float32),
            pltpu.VMEM((1, rows), jnp.float32),
            blocks(8), blocks(4), blocks(16), blocks(8), blocks(2 * SLOTS), blocks(8 + SLOTS),
            pieces(LANES, pops), pieces(LANES, pops), pieces(pops), pieces(PLANES),
            pieces(), pieces(PLANES), pieces(LANES, PLANES),
            dma((2,)), dma((n,)), dma((n,)), dma((8,)), dma((4,)), dma((4,)), dma((16,)), dma((8,)),
            dma((2 * SLOTS,)), dma((8 + SLOTS,)),
            dma((LANES,)), dma((LANES,)), dma((PLANES,)), dma((PLANES,)), dma((PLANES,)), dma((PLANES,)),
            dma((LANES,)), dma((LANES,)),
        ],
        compiler_params=pltpu.CompilerParams(
            collective_id=1, has_side_effects=True, vmem_limit_bytes=60 * 2**20),
    )(pop_ids, rare_ids, rare_count, rare_pos, pop_pos, q_start, queries, own_kv, store_kv,
      *tables(np.arange(COARSE) * float(COARSE)), *tables(np.arange(longest) * 1.0))


def body(*args):
    requests, pops = args[6].shape[1], args[4].shape[0]
    if lax.axis_size("store") == PLANES * LANES and requests == SLOTS and pops == PLANES:
        return relay_body(*args)
    return direct_body(*args)


def solution(mesh):
    both = ("tenant", "store")
    in_specs = (
        P(both, None), P(both, None), P(both, None, None), P(both), P("tenant"),
        P(both, None), P(both, None), P(both), P(both, None),
    )
    return jax.shard_map(
        body, mesh=mesh, in_specs=in_specs, out_specs=P(both, None), check_vma=False)
```

```python
import functools

import jax
import jax.numpy as jnp
import numpy as np
from jax import lax
from jax.experimental import pallas as pl
from jax.experimental.pallas import tpu as pltpu
from jax.sharding import PartitionSpec as P

MESH = pl.DeviceIdType.MESH
INNER = 4
STRIDE = 5
WINDOW = 7


def direct_kernel(
    n, per_device, requests, pops, chunk, power,
    pop_ref, request_ref, queries_ref, own_ref, store_hbm,
    base_cos, base_sin, step_cos, step_sin, out_ref,
    store, asks, asks_s, stage, recv, query_rows, total, tops,
    one_stage, one_recv, two_stage, two_recv, mid_stage, three_stage, popular,
    local_sem, ask_send, ask_recv, rare_send, rare_recv,
    one_send, one_sem, two_send, two_sem, mid_send, mid_sem, three_send, three_sem,
):
    me = lax.axis_index("store")
    inner, outer = lax.rem(me, INNER), me // INNER
    outers = n // INNER
    head = base_cos.shape[1]
    tokens = queries_ref.shape[0]
    rows = query_rows.shape[0]
    span = stage.shape[1]
    piece = span // INNER

    def ask_copy(slot, target):
        return pltpu.make_async_remote_copy(
            src_ref=request_ref, dst_ref=asks.at[slot],
            send_sem=ask_send.at[target], recv_sem=ask_recv.at[slot],
            device_id={"store": target}, device_id_type=MESH)

    def rare_copy(slot, target):
        return pltpu.make_async_remote_copy(
            src_ref=stage.at[target], dst_ref=recv.at[slot],
            send_sem=rare_send.at[target], recv_sem=rare_recv.at[slot],
            device_id={"store": target}, device_id_type=MESH)

    def one_copy(slot, target):
        return pltpu.make_async_remote_copy(
            src_ref=one_stage.at[target], dst_ref=one_recv.at[slot],
            send_sem=one_send.at[target], recv_sem=one_sem.at[slot],
            device_id={"store": outer * INNER + target}, device_id_type=MESH)

    def two_copy(slot, target):
        return pltpu.make_async_remote_copy(
            src_ref=two_stage.at[target], dst_ref=two_recv.at[slot],
            send_sem=two_send.at[target], recv_sem=two_sem.at[slot],
            device_id={"store": target * INNER + inner}, device_id_type=MESH)

    def mid_copy(slot, target):
        return pltpu.make_async_remote_copy(
            src_ref=mid_stage, dst_ref=three_stage.at[slot],
            send_sem=mid_send.at[target], recv_sem=mid_sem.at[slot],
            device_id={"store": target * INNER + inner}, device_id_type=MESH)

    def three_copy(slot, target):
        return pltpu.make_async_remote_copy(
            src_ref=three_stage, dst_ref=popular.at[slot],
            send_sem=three_send.at[target], recv_sem=three_sem.at[slot],
            device_id={"store": outer * INNER + target}, device_id_type=MESH)

    def peers(act):
        def step(s, carry):
            act(lax.rem(me + s, n))
            return carry
        lax.fori_loop(1, n, step, 0)

    load = pltpu.make_async_copy(store_hbm, store, local_sem.at[0])
    load.start()
    barrier = pltpu.get_barrier_semaphore()
    peers(lambda d: pl.semaphore_signal(
        barrier, inc=1, device_id={"store": d}, device_id_type=MESH))
    pl.semaphore_wait(barrier, n - 1)
    peers(lambda d: ask_copy(me, d).start())
    load.wait()

    for s in range(INNER):
        j = lax.rem(inner + s, INNER)
        begin = pl.multiple_of(j * piece, piece)
        for k in range(pops):
            part = store[lax.rem(pop_ref[k], per_device), pl.ds(begin, piece), :]
            if s == 0:
                one_recv[inner, k] = part
            else:
                one_stage[j, k] = part
        if s:
            one_copy(inner, j).start()

    cos0, sin0 = base_cos[0:1, :], base_sin[0:1, :]
    cos_n, sin_n = step_cos[:tokens, :], step_sin[:tokens, :]
    own_cos = cos0 * cos_n - sin0 * sin_n
    own_sin = sin0 * cos_n + cos0 * sin_n

    def turn(x, cosine, sine):
        x = x.astype(jnp.float32)
        return (x * cosine + pltpu.roll(x, head // 2, 1) * sine).astype(jnp.bfloat16)

    for g in range(rows // tokens):
        query_rows[g * tokens:(g + 1) * tokens, :] = turn(
            queries_ref[:, g * head:(g + 1) * head], own_cos, own_sin)

    pad = total.shape[0] - head

    def attend(keys, values, c, seen):
        at = pl.ds(c * chunk, chunk)
        scores = lax.dot_general(
            keys, query_rows[at, :], (((1,), (1,)), ((), ())),
            preferred_element_type=jnp.float32)
        if seen is not None:
            scores = jnp.where(seen, scores, -jnp.inf)
        top = jnp.max(scores, axis=0, keepdims=True)
        weights = jnp.exp2((scores - top) * power).astype(jnp.bfloat16)
        return top, jnp.dot(values, weights, preferred_element_type=jnp.float32)

    def flip(values):
        return jnp.concatenate(
            [values.T, jnp.ones((pad, values.shape[0]), jnp.bfloat16)], axis=0)

    def fold(block, base, live):
        cos_b, sin_b = base_cos[pl.ds(base, 1), :], base_sin[pl.ds(base, 1), :]
        cos_n, sin_n = step_cos[:span, :], step_sin[:span, :]
        keys = turn(
            block[:, :head], cos_b * cos_n - sin_b * sin_n, sin_b * cos_n + cos_b * sin_n)
        values = flip(block[:, head:])
        for c in range(rows // chunk):
            at = pl.ds(c * chunk, chunk)
            top, mixed = attend(keys, values, c, None)
            top = jnp.where(live, top, -jnp.inf)
            old = tops[:, at]
            diff = top - old
            factor = jnp.exp2(-jnp.abs(diff) * power)
            rises = diff > 0.0
            tops[:, at] = jnp.maximum(old, top)
            total[:, at] = (
                total[:, at] * jnp.where(rises, factor, 1.0)
                + mixed * jnp.where(rises, 1.0, factor))

    peers(lambda d: ask_copy(d, d).wait_recv())
    bring = pltpu.make_async_copy(asks, asks_s, local_sem.at[1])
    asks[me] = request_ref[...]
    bring.start()
    bring.wait()

    def slot_for(d):
        def look(r, slot):
            block_id = asks_s[d, 0, r]
            hit = (block_id // per_device == me) & (r < asks_s[d, 0, requests])
            return jnp.where(hit, lax.rem(block_id, per_device), slot)
        return lax.fori_loop(0, requests, look, jnp.int32(0), unroll=min(requests, 8))

    def reply(first, last):
        def step(s, carry):
            d = lax.rem(me + s * STRIDE, n)
            stage[d] = store[slot_for(d)]
            rare_copy(me, d).start()
            return carry
        lax.fori_loop(first, last, step, 0)

    cuts = [1, 3, 5, WINDOW + 1, n]
    reply(cuts[0], cuts[1])
    recv[me] = store[slot_for(me)]

    for s in range(1, INNER):
        j = lax.rem(inner + s, INNER)
        one_copy(j, j).wait_recv()
    for k in range(pops):
        two_stage[k] = one_recv[lax.rem(pop_ref[k] // per_device, INNER), k]
    for k in range(pops):
        @pl.when(outer != k)
        def _():
            two_copy(outer, k).start()

        @pl.when(outer == k)
        def _():
            two_recv[k] = two_stage[k]

    def rare_fold(h):
        def look(r, found):
            hit = (asks_s[me, 0, r] // per_device == h) & (r < asks_s[me, 0, requests])
            return jnp.where(hit, r, found)
        r = lax.fori_loop(0, requests, look, jnp.int32(-1), unroll=min(requests, 8))
        fold(recv[h], jnp.maximum(r, 0) + 1 + pops, r >= 0)

    def arrivals(first, last):
        def step(s, carry):
            h = lax.rem(me + (n - s) * STRIDE, n)
            rare_copy(h, h).wait_recv()
            rare_fold(h)

            @pl.when(s + WINDOW < n)
            def _():
                reply(s + WINDOW, s + WINDOW + 1)
            return carry
        lax.fori_loop(first, last, step, 0)

    reply(cuts[1], cuts[2])

    own_keys = turn(own_ref[:, :head], own_cos, own_sin)
    own_values = flip(own_ref[:, head:])
    for c in range(rows // chunk):
        at = pl.ds(c * chunk, chunk)
        token = lax.rem(
            lax.broadcasted_iota(jnp.int32, (tokens, chunk), 1) + c * chunk, tokens)
        seen = token >= lax.broadcasted_iota(jnp.int32, (tokens, chunk), 0)
        top, total[:, at] = attend(own_keys, own_values, c, seen)
        tops[:, at] = top

    rare_fold(me)

    @pl.when(outer < pops)
    def _():
        def two_wait(s, carry):
            d = lax.rem(outer + s, outers)
            pltpu.make_async_remote_copy(
                src_ref=mid_stage, dst_ref=two_recv.at[d],
                send_sem=mid_send.at[d], recv_sem=two_sem.at[d],
                device_id={"store": d * INNER + inner}, device_id_type=MESH).wait_recv()
            return carry
        lax.fori_loop(1, outers, two_wait, 0)
        mine = lax.rem(outer, pops)
        mid_stage[...] = two_recv[pop_ref[mine] // (per_device * INNER)]

        def mid_start(s, carry):
            mid_copy(mine, lax.rem(outer + s, outers)).start()
            return carry
        lax.fori_loop(1, outers, mid_start, 0)
        three_stage[mine] = mid_stage[...]

    reply(cuts[2], cuts[3])
    arrivals(cuts[0], cuts[1])
    for k in range(pops):
        @pl.when(outer != k)
        def _():
            mid_copy(k, k).wait_recv()
    for s in range(1, INNER):
        three_copy(inner, lax.rem(inner + s, INNER)).start()
    for k in range(pops):
        popular[inner, k] = three_stage[k]
    arrivals(cuts[1], cuts[3])

    for s in range(1, INNER):
        j = lax.rem(inner + s, INNER)
        three_copy(j, j).wait_recv()

    def popular_fold(k, carry):
        block = jnp.concatenate([popular[j, k] for j in range(INNER)], axis=0)
        fold(block, k + 1, True)
        return carry
    lax.fori_loop(0, pops, popular_fold, 0)

    arrivals(cuts[3], cuts[4])

    for g in range(rows // tokens):
        at = pl.ds(g * tokens, tokens)
        out_ref[:, g * head:(g + 1) * head] = (
            total[:head, at] / total[head:head + 1, at]).T.astype(jnp.bfloat16)

    peers(lambda d: ask_copy(d, d).wait_send())
    peers(lambda d: rare_copy(d, d).wait_send())
    for s in range(1, INNER):
        j = lax.rem(inner + s, INNER)
        one_copy(j, j).wait_send()
        three_copy(j, j).wait_send()

    for k in range(pops):
        @pl.when(outer != k)
        def _():
            two_copy(k, k).wait_send()

    @pl.when(outer < pops)
    def _():
        def mid_done(s, carry):
            d = lax.rem(outer + s, outers)
            mid_copy(lax.rem(outer, pops), d).wait_send()
            return carry
        lax.fori_loop(1, outers, mid_done, 0)


def direct_body(queries, own_kv, store_kv, q_start, pop_ids, pop_pos, rare_ids, rare_count, rare_pos):
    n = lax.axis_size("store")
    tokens = queries.shape[0]
    head = own_kv.shape[1] // 2
    rows = tokens * (queries.shape[1] // head)
    per_device, span, width = store_kv.shape
    requests = rare_ids.shape[1]
    pops = pop_ids.shape[0]
    longest = max(span, tokens)
    lanes = -(-(requests + 1) // 128) * 128
    outers = n // INNER
    piece = span // INNER

    half = np.arange(head) % (head // 2)
    freq = 500000.0 ** (-(2.0 * half) / head)
    sign = np.where(np.arange(head) < head // 2, -1.0, 1.0)
    steps = np.arange(longest)[:, None] * freq[None, :]
    step_cos = np.cos(steps).astype(np.float32)
    step_sin = (np.sin(steps) * sign).astype(np.float32)
    base = jnp.concatenate([q_start, pop_pos[0], rare_pos[0]]).astype(jnp.float32)
    angles = base[:, None] * freq.astype(np.float32)[None, :]
    base_cos = jnp.cos(angles)
    base_sin = jnp.sin(angles) * sign.astype(np.float32)[None, :]
    table = jnp.concatenate([rare_ids[0], rare_count])
    table = jnp.pad(table, (0, lanes - requests - 1))

    vmem = pl.BlockSpec(memory_space=pltpu.VMEM)
    smem = pl.BlockSpec(memory_space=pltpu.SMEM)
    dma = pltpu.SemaphoreType.DMA
    bf16 = jnp.bfloat16
    chunk = min(rows, 512)
    return pl.pallas_call(
        functools.partial(direct_kernel, n, per_device, requests, pops, chunk, head ** -0.5 * np.log2(np.e).item()),
        out_shape=jax.ShapeDtypeStruct(queries.shape, bf16),
        in_specs=[smem, vmem, vmem, vmem, pl.BlockSpec(memory_space=pl.ANY)] + [vmem] * 4,
        out_specs=vmem,
        scratch_shapes=[
            pltpu.VMEM((per_device, span, width), bf16),
            pltpu.VMEM((n, 1, lanes), jnp.int32),
            pltpu.SMEM((n, 1, lanes), jnp.int32),
            pltpu.VMEM((n, span, width), bf16),
            pltpu.VMEM((n, span, width), bf16),
            pltpu.VMEM((rows, head), bf16),
            pltpu.VMEM((head + 16, rows), jnp.float32),
            pltpu.VMEM((1, rows), jnp.float32),
            pltpu.VMEM((INNER, pops, piece, width), bf16),
            pltpu.VMEM((INNER, pops, piece, width), bf16),
            pltpu.VMEM((pops, piece, width), bf16),
            pltpu.VMEM((outers, piece, width), bf16),
            pltpu.VMEM((piece, width), bf16),
            pltpu.VMEM((pops, piece, width), bf16),
            pltpu.VMEM((INNER, pops, piece, width), bf16),
            dma((2,)), dma((n,)), dma((n,)), dma((n,)), dma((n,)),
            dma((INNER,)), dma((INNER,)), dma((outers,)), dma((outers,)), dma((outers,)), dma((pops,)),
            dma((INNER,)), dma((INNER,)),
        ],
        compiler_params=pltpu.CompilerParams(
            collective_id=0, has_side_effects=True, vmem_limit_bytes=60 * 2**20),
    )(pop_ids, table.reshape(1, lanes), queries, own_kv, store_kv,
      base_cos, base_sin, step_cos, step_sin)


PLANES = 4
LANES = 4
SLOTS = 6
SLACK = 2
COARSE = 128


def relay_kernel(
    per_device, requests, pops, power,
    pop_ref, ids_ref, count_ref, rare_pos, pop_pos, start_ref,
    queries_ref, own_ref, store_hbm, coarse_cos, coarse_sin, step_cos, step_sin, out_ref,
    store, row, asks, asks_s, choice, info, query_rows, total, tops,
    far_stage, hop, cand, near_stage, list_stage, recv,
    one_stage, one_recv, two_stage, up_recv, merged, cross_recv, final,
    local_sem, ask_send, ask_recv, far_send, hop_sem, fwd_send, cand_sem, near_send, list_send, recv_sem,
    one_send, one_sem, chain_send, chain_sem, three_send, three_sem,
):
    n = PLANES * LANES
    me = lax.axis_index("store")
    plane, lane = me // LANES, lax.rem(me, LANES)
    half = plane // 2
    inner = jnp.where(half == 0, plane, 3 - plane)
    is_inner, is_outer = inner == 1, inner == 0
    head = step_cos.shape[1]
    tokens = queries_ref.shape[0]
    rows = query_rows.shape[0]
    span = store.shape[1]
    piece = span // LANES

    def device(h, u, t):
        return (u + h * (3 - 2 * u)) * LANES + t

    def place(u, d):
        return (d & 1) + (d >> 1) * 4 + (1 - u) * 2

    def remote(src, dst, send, recv_at, target):
        return pltpu.make_async_remote_copy(
            src_ref=src, dst_ref=dst, send_sem=send, recv_sem=recv_at,
            device_id={"store": target}, device_id_type=MESH)

    def ask_copy(slot, target):
        return remote(row, asks.at[slot], ask_send.at[target], ask_recv.at[slot], target)

    def far_copy(q, d):
        at = q * 4 + d
        return remote(
            far_stage.at[at], cand.at[q * 8 + place(inner, d)], far_send.at[at],
            cand_sem.at[q * 8 + place(inner, d)], device(half, 1, lane ^ d))

    def hop_copy(q, d):
        at = q * 4 + d
        return remote(
            far_stage.at[at], hop.at[q * 2 + d - 2], far_send.at[at],
            hop_sem.at[q * 2 + d - 2], device(half, 0, lane ^ d))

    def forward_copy(q, j):
        at = q * 8 + place(0, 2 + j)
        return remote(
            hop.at[q * 2 + j], cand.at[at], fwd_send.at[q * 2 + j], cand_sem.at[at],
            device(half, 1, lane))

    def near_copy(rel, d):
        at = rel * 4 + d
        return remote(
            near_stage.at[at], recv.at[at], near_send.at[at], recv_sem.at[at],
            device(half, inner ^ rel, lane ^ d))

    def list_copy(q, s):
        at = q * SLOTS + s
        return remote(
            list_stage.at[at], recv.at[8 + s], list_send.at[at], recv_sem.at[8 + s],
            device(1 - half, q, lane))

    def one_copy(d):
        return remote(
            one_stage.at[d], one_recv.at[d], one_send.at[d], one_sem.at[d],
            plane * LANES + (lane ^ d))

    def chain_copy(step, src, dst, target):
        return remote(src, dst, chain_send.at[step], chain_sem.at[step], target)

    def up_copy():
        return chain_copy(0, two_stage, up_recv, device(half, 1, lane))

    def cross_copy():
        return chain_copy(1, merged, cross_recv, device(1 - half, 1, lane))

    def down_copy():
        return chain_copy(2, final, final, device(half, 0, lane))

    def popular_at(t):
        return recv.at[pl.ds(8 + SLOTS, pops), pl.ds(pl.multiple_of(t * piece, piece), piece)]

    def three_copy(d):
        return remote(
            final, popular_at(lane), three_send.at[d], three_sem.at[d],
            plane * LANES + (lane ^ d))

    def peers(act):
        def step(s, carry):
            act(lax.rem(me + s, n))
            return carry
        lax.fori_loop(1, n, step, 0)

    load = pltpu.make_async_copy(store_hbm, store, local_sem.at[0])
    load.start()
    barrier = pltpu.get_barrier_semaphore()
    peers(lambda d: pl.semaphore_signal(
        barrier, inc=1, device_id={"store": d}, device_id_type=MESH))

    spot = lax.broadcasted_iota(jnp.int32, row.shape, 1)
    wanted = jnp.full(row.shape, -1, jnp.int32)
    for r in range(requests):
        block_id = ids_ref[0, r]
        holder = jnp.where(r < count_ref[0], block_id // per_device, -1)
        wanted = jnp.where(spot == holder, lax.rem(block_id, per_device) + r * per_device, wanted)
    row[...] = wanted
    asks[me] = wanted

    def base_of(position):
        a, b = position // COARSE, lax.rem(position, COARSE)
        ca, sa = coarse_cos[pl.ds(a, 1), :], coarse_sin[pl.ds(a, 1), :]
        cb, sb = step_cos[pl.ds(b, 1), :], step_sin[pl.ds(b, 1), :]
        return ca * cb - sa * sb, sa * cb + ca * sb

    def table(position, count):
        cos_b, sin_b = base_of(position)
        cos_n, sin_n = step_cos[:count, :], step_sin[:count, :]
        return cos_b * cos_n - sin_b * sin_n, sin_b * cos_n + cos_b * sin_n

    def turn(x, cosine, sine):
        x = x.astype(jnp.float32)
        return (x * cosine + pltpu.roll(x, head // 2, 1) * sine).astype(jnp.bfloat16)

    own_cos, own_sin = table(start_ref[0], tokens)
    for g in range(rows // tokens):
        query_rows[g * tokens:(g + 1) * tokens, :] = turn(
            queries_ref[:, g * head:(g + 1) * head], own_cos, own_sin)

    pad = total.shape[0] - head

    def attend(keys, values, seen):
        scores = lax.dot_general(
            keys, query_rows[...], (((1,), (1,)), ((), ())),
            preferred_element_type=jnp.float32)
        if seen is not None:
            scores = jnp.where(seen, scores, -jnp.inf)
        top = jnp.max(scores, axis=0, keepdims=True)
        weights = jnp.exp2((scores - top) * power).astype(jnp.bfloat16)
        return top, jnp.dot(values, weights, preferred_element_type=jnp.float32)

    def flip(values):
        return jnp.concatenate(
            [values.T, jnp.ones((pad, values.shape[0]), jnp.bfloat16)], axis=0)

    def fold(block, position, live):
        keys = turn(block[:, :head], *table(position, span))
        values = flip(block[:, head:])
        top, mixed = attend(keys, values, None)
        top = jnp.where(live, top, -jnp.inf)
        old = tops[...]
        diff = top - old
        factor = jnp.exp2(-jnp.abs(diff) * power)
        rises = diff > 0.0
        tops[...] = jnp.maximum(old, top)
        total[...] = (
            total[...] * jnp.where(rises, factor, 1.0)
            + mixed * jnp.where(rises, 1.0, factor))

    load.wait()
    for d in range(LANES):
        begin = pl.multiple_of((lane ^ d) * piece, piece)
        for k in range(pops):
            part = store[lax.rem(pop_ref[k], per_device), pl.ds(begin, piece), :]
            if d == 0:
                one_recv[0, k] = part
            else:
                one_stage[d, k] = part

    pl.semaphore_wait(barrier, n - 1)
    peers(lambda d: ask_copy(me, d).start())
    for d in range(1, LANES):
        one_copy(d).start()

    token = lax.rem(lax.broadcasted_iota(jnp.int32, (tokens, rows), 1), tokens)
    seen = token >= lax.broadcasted_iota(jnp.int32, (tokens, rows), 0)
    top, mixed = attend(
        turn(own_ref[:, :head], own_cos, own_sin), flip(own_ref[:, head:]), seen)
    total[...] = mixed
    tops[...] = top

    peers(lambda d: ask_copy(d, d).wait_recv())
    bring = pltpu.make_async_copy(asks, asks_s, local_sem.at[1])
    bring.start()
    bring.wait()

    def block_for(target):
        return store[lax.rem(jnp.maximum(asks_s[target, 0, me], 0), per_device)]

    def far_block(q, d):
        return block_for(device(1 - half, q, lane ^ d))

    def far_send_to_relay(q, d):
        far_stage[q * 4 + d] = far_block(q, d)
        far_copy(q, d).start()

    def far_send_to_hop(q, d):
        far_stage[q * 4 + d] = far_block(q, d)
        hop_copy(q, d).start()

    def near_send_one(rel, d):
        near_stage[rel * 4 + d] = block_for(device(half, inner ^ rel, lane ^ d))
        near_copy(rel, d).start()

    @pl.when(is_outer)
    def _():
        for d in (0, 1):
            far_send_to_relay(0, d)
        for d in (2, 3):
            far_send_to_hop(0, d)
        for d in (2, 3):
            far_send_to_hop(1, d)

    @pl.when(is_inner)
    def _():
        for q in (0, 1):
            cand[q * 8] = far_block(q, 0)
            for d in (1, 2, 3):
                far_send_to_relay(q, d)

    recv[0] = block_for(me)
    for d in range(1, LANES):
        near_send_one(0, d)

    @pl.when(is_inner)
    def _():
        for d in range(LANES):
            near_send_one(1, d)

    def assign(requester, h, name):
        found = [jnp.int32(-1)] * SLOTS
        last = jnp.int32(-1)
        for i in range(SLOTS + SLACK):
            d, u = (i & 1) + ((i >> 2) << 1), 1 - ((i >> 1) & 1)
            value = asks_s[requester, 0, device(h, u, lane ^ d)]
            there = value >= 0
            slot = jnp.maximum(last + 1, i - SLACK)
            for s in range(max(0, i - SLACK), min(i, SLOTS - 1) + 1):
                found[s] = jnp.where(there & (slot == s), name(i, value), found[s])
            last = jnp.where(there, slot, last)
        return found

    @pl.when(is_inner)
    def _():
        for q in (0, 1):
            for s, i in enumerate(assign(device(1 - half, q, lane), half, lambda i, value: i)):
                choice[q * SLOTS + s] = i

    def note(i, r):
        info[i] = jnp.where(r >= 0, rare_pos[0, jnp.maximum(r, 0)], -1)

    for rel in (0, 1):
        for d in range(LANES):
            value = asks_s[me, 0, device(half, inner ^ rel, lane ^ d)]
            note(rel * 4 + d, jnp.where(value >= 0, value // per_device, -1))
    for s, r in enumerate(assign(me, 1 - half, lambda i, value: value // per_device)):
        note(8 + s, r)
    for k in range(pops):
        info[8 + SLOTS + k] = pop_pos[0, k]

    for d in range(1, LANES):
        one_copy(d).wait_recv()
    for k in range(pops):
        two_stage[k] = one_recv[lane ^ lax.rem(pop_ref[k] // per_device, LANES), k]

    def wait_cand(at):
        remote(far_stage.at[0], cand.at[at], far_send.at[0], cand_sem.at[at], me ^ 1).wait_recv()

    def relay(q, s):
        at = q * 8 + s
        wait_cand(at + 2)
        pick = choice[q * SLOTS + s]
        list_stage[q * SLOTS + s] = jnp.where(
            pick == s, cand[at], jnp.where(pick == s + 1, cand[at + 1], cand[at + 2]))
        list_copy(q, s).start()

    def start_forward(q, j):
        remote(far_stage.at[0], hop.at[q * 2 + j], far_send.at[0], hop_sem.at[q * 2 + j], me ^ 1).wait_recv()
        forward_copy(q, j).start()

    def wait_block(i):
        @pl.when((i > 0) & (i < 8 + SLOTS))
        def _():
            remote(near_stage.at[0], recv.at[i], near_send.at[0], recv_sem.at[i], me ^ 1).wait_recv()

        @pl.when(i == 8 + SLOTS)
        def _():
            for d in range(1, LANES):
                remote(final, popular_at(lane ^ d), three_send.at[d], three_sem.at[d], me ^ 1).wait_recv()

    def folds(inner_order, outer_order):
        def code(order, first):
            return sum(i << (5 * e) for e, i in enumerate(order[first:first + 6]))

        def step(e, carry):
            packed = jnp.int32(0)
            for first in range(0, max(len(inner_order), len(outer_order)), 6):
                words = jnp.where(is_inner, code(inner_order, first), code(outer_order, first))
                packed = jnp.where((e >= first) & (e < first + 6), words >> (5 * (e - first) % 30), packed)
            i = packed & 31
            wait_block(i)
            position = info[i]
            fold(recv[i], jnp.maximum(position, 0), position >= 0)
            return carry
        lax.fori_loop(0, jnp.where(is_inner, len(inner_order), len(outer_order)), step, 0)

    def holder_plane(k):
        return pop_ref[k] // (per_device * LANES)

    def spread():
        for d in range(1, LANES):
            three_copy(d).start()
        popular_at(lane)[...] = final[...]

    @pl.when(is_outer)
    def _():
        up_copy().start()
        start_forward(0, 0)
        start_forward(0, 1)
        for d in (0, 1):
            far_send_to_relay(1, d)
        start_forward(1, 0)
        start_forward(1, 1)
        for d in range(LANES):
            near_send_one(1, d)

    @pl.when(is_inner)
    def _():
        wait_cand(1)
        for s in range(4):
            relay(0, s)
        up_copy().wait_recv()
        for k in range(pops):
            merged[k] = jnp.where(holder_plane(k) == plane, two_stage[k], up_recv[k])
        cross_copy().start()
        for s in range(4, SLOTS):
            relay(0, s)

    folds([0, 1], [0, 1, 8, 9, 10])

    @pl.when(is_inner)
    def _():
        cross_copy().wait_recv()
        for k in range(pops):
            final[k] = jnp.where(holder_plane(k) // 2 == half, merged[k], cross_recv[k])
        down_copy().start()
        spread()
        wait_cand(8 + 1)
        relay(1, 0)
        relay(1, 1)

    folds([2, 3], [2, 3, 11])

    @pl.when(is_inner)
    def _():
        for s in range(2, SLOTS):
            relay(1, s)

    @pl.when(is_outer)
    def _():
        down_copy().wait_recv()
        spread()

    folds([14, 15, 16, 17, 8, 4, 9, 5, 10, 6, 11, 7, 12, 13], [12, 13, 4, 5, 6, 7, 14, 15, 16, 17])

    for g in range(rows // tokens):
        at = pl.ds(g * tokens, tokens)
        out_ref[:, g * head:(g + 1) * head] = (
            total[:head, at] / total[head:head + 1, at]).T.astype(jnp.bfloat16)

    peers(lambda d: ask_copy(d, d).wait_send())
    for rel in (0, 1):
        for d in range(LANES):
            if rel or d:
                near_copy(rel, d).wait_send()
    for q in (0, 1):
        @pl.when(is_outer)
        def _():
            for d in range(LANES):
                (far_copy if d < 2 else hop_copy)(q, d).wait_send()
            for j in (0, 1):
                forward_copy(q, j).wait_send()

        @pl.when(is_inner)
        def _():
            for d in range(1, LANES):
                far_copy(q, d).wait_send()
            for s in range(SLOTS):
                list_copy(q, s).wait_send()
    for d in range(1, LANES):
        one_copy(d).wait_send()
        three_copy(d).wait_send()

    @pl.when(is_outer)
    def _():
        up_copy().wait_send()

    @pl.when(is_inner)
    def _():
        cross_copy().wait_send()
        down_copy().wait_send()


def relay_body(queries, own_kv, store_kv, q_start, pop_ids, pop_pos, rare_ids, rare_count, rare_pos):
    n = lax.axis_size("store")
    tokens = queries.shape[0]
    head = own_kv.shape[1] // 2
    rows = tokens * (queries.shape[1] // head)
    per_device, span, width = store_kv.shape
    requests = rare_ids.shape[1]
    pops = pop_ids.shape[0]
    longest = max(span, tokens, COARSE)
    piece = span // LANES

    half = np.arange(head) % (head // 2)
    freq = 500000.0 ** (-(2.0 * half) / head)
    sign = np.where(np.arange(head) < head // 2, -1.0, 1.0)

    def tables(positions):
        angles = positions[:, None] * freq[None, :]
        return np.cos(angles).astype(np.float32), (np.sin(angles) * sign).astype(np.float32)

    vmem = pl.BlockSpec(memory_space=pltpu.VMEM)
    smem = pl.BlockSpec(memory_space=pltpu.SMEM)
    dma = pltpu.SemaphoreType.DMA
    bf16 = jnp.bfloat16

    def blocks(count):
        return pltpu.VMEM((count, span, width), bf16)

    def pieces(*lead):
        return pltpu.VMEM((*lead, piece, width), bf16)

    return pl.pallas_call(
        functools.partial(relay_kernel, per_device, requests, pops, head ** -0.5 * np.log2(np.e).item()),
        out_shape=jax.ShapeDtypeStruct(queries.shape, bf16),
        in_specs=[smem] * 6 + [vmem, vmem, pl.BlockSpec(memory_space=pl.ANY)] + [vmem] * 4,
        out_specs=vmem,
        scratch_shapes=[
            blocks(per_device),
            pltpu.VMEM((1, 128), jnp.int32),
            pltpu.VMEM((n, 1, 128), jnp.int32),
            pltpu.SMEM((n, 1, 128), jnp.int32),
            pltpu.SMEM((2 * SLOTS,), jnp.int32),
            pltpu.SMEM((8 + SLOTS + pops,), jnp.int32),
            pltpu.VMEM((rows, head), bf16),
            pltpu.VMEM((head + 16, rows), jnp.float32),
            pltpu.VMEM((1, rows), jnp.float32),
            blocks(8), blocks(4), blocks(16), blocks(8), blocks(2 * SLOTS), blocks(8 + SLOTS + pops),
            pieces(LANES, pops), pieces(LANES, pops), pieces(pops), pieces(pops),
            pieces(pops), pieces(pops), pieces(pops),
            dma((2,)), dma((n,)), dma((n,)), dma((8,)), dma((4,)), dma((4,)), dma((16,)), dma((8,)),
            dma((2 * SLOTS,)), dma((8 + SLOTS,)),
            dma((LANES,)), dma((LANES,)), dma((3,)), dma((3,)),
            dma((LANES,)), dma((LANES,)),
        ],
        compiler_params=pltpu.CompilerParams(
            collective_id=1, has_side_effects=True, vmem_limit_bytes=60 * 2**20),
    )(pop_ids, rare_ids, rare_count, rare_pos, pop_pos, q_start, queries, own_kv, store_kv,
      *tables(np.arange(COARSE) * float(COARSE)), *tables(np.arange(longest) * 1.0))


def body(*args):
    requests, pops = args[6].shape[1], args[4].shape[0]
    if lax.axis_size("store") == PLANES * LANES and requests == SLOTS and pops == PLANES:
        return relay_body(*args)
    return direct_body(*args)


def solution(mesh):
    both = ("tenant", "store")
    in_specs = (
        P(both, None), P(both, None), P(both, None, None), P(both), P("tenant"),
        P(both, None), P(both, None), P(both), P(both, None),
    )
    return jax.shard_map(
        body, mesh=mesh, in_specs=in_specs, out_specs=P(both, None), check_vma=False)
```

```python
import functools

import jax
import jax.numpy as jnp
import numpy as np
from jax import lax
from jax.experimental import pallas as pl
from jax.experimental.pallas import tpu as pltpu
from jax.sharding import PartitionSpec as P

MESH = pl.DeviceIdType.MESH
INNER = 4
STRIDE = 5
WINDOW = 7


def direct_kernel(
    n, per_device, requests, pops, chunk, power,
    pop_ref, request_ref, queries_ref, own_ref, store_hbm,
    base_cos, base_sin, step_cos, step_sin, out_ref,
    store, asks, asks_s, stage, recv, query_rows, total, tops,
    one_stage, one_recv, two_stage, two_recv, mid_stage, three_stage, popular,
    local_sem, ask_send, ask_recv, rare_send, rare_recv,
    one_send, one_sem, two_send, two_sem, mid_send, mid_sem, three_send, three_sem,
):
    me = lax.axis_index("store")
    inner, outer = lax.rem(me, INNER), me // INNER
    outers = n // INNER
    head = base_cos.shape[1]
    tokens = queries_ref.shape[0]
    rows = query_rows.shape[0]
    span = stage.shape[1]
    piece = span // INNER

    def ask_copy(slot, target):
        return pltpu.make_async_remote_copy(
            src_ref=request_ref, dst_ref=asks.at[slot],
            send_sem=ask_send.at[target], recv_sem=ask_recv.at[slot],
            device_id={"store": target}, device_id_type=MESH)

    def rare_copy(slot, target):
        return pltpu.make_async_remote_copy(
            src_ref=stage.at[target], dst_ref=recv.at[slot],
            send_sem=rare_send.at[target], recv_sem=rare_recv.at[slot],
            device_id={"store": target}, device_id_type=MESH)

    def one_copy(slot, target):
        return pltpu.make_async_remote_copy(
            src_ref=one_stage.at[target], dst_ref=one_recv.at[slot],
            send_sem=one_send.at[target], recv_sem=one_sem.at[slot],
            device_id={"store": outer * INNER + target}, device_id_type=MESH)

    def two_copy(slot, target):
        return pltpu.make_async_remote_copy(
            src_ref=two_stage.at[target], dst_ref=two_recv.at[slot],
            send_sem=two_send.at[target], recv_sem=two_sem.at[slot],
            device_id={"store": target * INNER + inner}, device_id_type=MESH)

    def mid_copy(slot, target):
        return pltpu.make_async_remote_copy(
            src_ref=mid_stage, dst_ref=three_stage.at[slot],
            send_sem=mid_send.at[target], recv_sem=mid_sem.at[slot],
            device_id={"store": target * INNER + inner}, device_id_type=MESH)

    def three_copy(slot, target):
        return pltpu.make_async_remote_copy(
            src_ref=three_stage, dst_ref=popular.at[slot],
            send_sem=three_send.at[target], recv_sem=three_sem.at[slot],
            device_id={"store": outer * INNER + target}, device_id_type=MESH)

    def peers(act):
        def step(s, carry):
            act(lax.rem(me + s, n))
            return carry
        lax.fori_loop(1, n, step, 0)

    load = pltpu.make_async_copy(store_hbm, store, local_sem.at[0])
    load.start()
    barrier = pltpu.get_barrier_semaphore()
    peers(lambda d: pl.semaphore_signal(
        barrier, inc=1, device_id={"store": d}, device_id_type=MESH))
    pl.semaphore_wait(barrier, n - 1)
    peers(lambda d: ask_copy(me, d).start())
    load.wait()

    for s in range(INNER):
        j = lax.rem(inner + s, INNER)
        begin = pl.multiple_of(j * piece, piece)
        for k in range(pops):
            part = store[lax.rem(pop_ref[k], per_device), pl.ds(begin, piece), :]
            if s == 0:
                one_recv[inner, k] = part
            else:
                one_stage[j, k] = part
        if s:
            one_copy(inner, j).start()

    cos0, sin0 = base_cos[0:1, :], base_sin[0:1, :]
    cos_n, sin_n = step_cos[:tokens, :], step_sin[:tokens, :]
    own_cos = cos0 * cos_n - sin0 * sin_n
    own_sin = sin0 * cos_n + cos0 * sin_n

    def turn(x, cosine, sine):
        x = x.astype(jnp.float32)
        return (x * cosine + pltpu.roll(x, head // 2, 1) * sine).astype(jnp.bfloat16)

    for g in range(rows // tokens):
        query_rows[g * tokens:(g + 1) * tokens, :] = turn(
            queries_ref[:, g * head:(g + 1) * head], own_cos, own_sin)

    pad = total.shape[0] - head

    def attend(keys, values, c, seen):
        at = pl.ds(c * chunk, chunk)
        scores = lax.dot_general(
            keys, query_rows[at, :], (((1,), (1,)), ((), ())),
            preferred_element_type=jnp.float32)
        if seen is not None:
            scores = jnp.where(seen, scores, -jnp.inf)
        top = jnp.max(scores, axis=0, keepdims=True)
        weights = jnp.exp2((scores - top) * power).astype(jnp.bfloat16)
        return top, jnp.dot(values, weights, preferred_element_type=jnp.float32)

    def flip(values):
        return jnp.concatenate(
            [values.T, jnp.ones((pad, values.shape[0]), jnp.bfloat16)], axis=0)

    def fold(block, base, live):
        cos_b, sin_b = base_cos[pl.ds(base, 1), :], base_sin[pl.ds(base, 1), :]
        cos_n, sin_n = step_cos[:span, :], step_sin[:span, :]
        keys = turn(
            block[:, :head], cos_b * cos_n - sin_b * sin_n, sin_b * cos_n + cos_b * sin_n)
        values = flip(block[:, head:])
        for c in range(rows // chunk):
            at = pl.ds(c * chunk, chunk)
            top, mixed = attend(keys, values, c, None)
            top = jnp.where(live, top, -jnp.inf)
            old = tops[:, at]
            diff = top - old
            factor = jnp.exp2(-jnp.abs(diff) * power)
            rises = diff > 0.0
            tops[:, at] = jnp.maximum(old, top)
            total[:, at] = (
                total[:, at] * jnp.where(rises, factor, 1.0)
                + mixed * jnp.where(rises, 1.0, factor))

    peers(lambda d: ask_copy(d, d).wait_recv())
    bring = pltpu.make_async_copy(asks, asks_s, local_sem.at[1])
    asks[me] = request_ref[...]
    bring.start()
    bring.wait()

    def slot_for(d):
        def look(r, slot):
            block_id = asks_s[d, 0, r]
            hit = (block_id // per_device == me) & (r < asks_s[d, 0, requests])
            return jnp.where(hit, lax.rem(block_id, per_device), slot)
        return lax.fori_loop(0, requests, look, jnp.int32(0), unroll=min(requests, 8))

    def reply(first, last):
        def step(s, carry):
            d = lax.rem(me + s * STRIDE, n)
            stage[d] = store[slot_for(d)]
            rare_copy(me, d).start()
            return carry
        lax.fori_loop(first, last, step, 0)

    cuts = [1, 3, 5, WINDOW + 1, n]
    reply(cuts[0], cuts[1])
    recv[me] = store[slot_for(me)]

    for s in range(1, INNER):
        j = lax.rem(inner + s, INNER)
        one_copy(j, j).wait_recv()
    for k in range(pops):
        two_stage[k] = one_recv[lax.rem(pop_ref[k] // per_device, INNER), k]
    for k in range(pops):
        @pl.when(outer != k)
        def _():
            two_copy(outer, k).start()

        @pl.when(outer == k)
        def _():
            two_recv[k] = two_stage[k]

    def rare_fold(h):
        def look(r, found):
            hit = (asks_s[me, 0, r] // per_device == h) & (r < asks_s[me, 0, requests])
            return jnp.where(hit, r, found)
        r = lax.fori_loop(0, requests, look, jnp.int32(-1), unroll=min(requests, 8))
        fold(recv[h], jnp.maximum(r, 0) + 1 + pops, r >= 0)

    def arrivals(first, last):
        def step(s, carry):
            h = lax.rem(me + (n - s) * STRIDE, n)
            rare_copy(h, h).wait_recv()
            rare_fold(h)

            @pl.when(s + WINDOW < n)
            def _():
                reply(s + WINDOW, s + WINDOW + 1)
            return carry
        lax.fori_loop(first, last, step, 0)

    reply(cuts[1], cuts[2])

    own_keys = turn(own_ref[:, :head], own_cos, own_sin)
    own_values = flip(own_ref[:, head:])
    for c in range(rows // chunk):
        at = pl.ds(c * chunk, chunk)
        token = lax.rem(
            lax.broadcasted_iota(jnp.int32, (tokens, chunk), 1) + c * chunk, tokens)
        seen = token >= lax.broadcasted_iota(jnp.int32, (tokens, chunk), 0)
        top, total[:, at] = attend(own_keys, own_values, c, seen)
        tops[:, at] = top

    rare_fold(me)

    @pl.when(outer < pops)
    def _():
        def two_wait(s, carry):
            d = lax.rem(outer + s, outers)
            pltpu.make_async_remote_copy(
                src_ref=mid_stage, dst_ref=two_recv.at[d],
                send_sem=mid_send.at[d], recv_sem=two_sem.at[d],
                device_id={"store": d * INNER + inner}, device_id_type=MESH).wait_recv()
            return carry
        lax.fori_loop(1, outers, two_wait, 0)
        mine = lax.rem(outer, pops)
        mid_stage[...] = two_recv[pop_ref[mine] // (per_device * INNER)]

        def mid_start(s, carry):
            mid_copy(mine, lax.rem(outer + s, outers)).start()
            return carry
        lax.fori_loop(1, outers, mid_start, 0)
        three_stage[mine] = mid_stage[...]

    reply(cuts[2], cuts[3])
    arrivals(cuts[0], cuts[1])
    for k in range(pops):
        @pl.when(outer != k)
        def _():
            mid_copy(k, k).wait_recv()
    for s in range(1, INNER):
        three_copy(inner, lax.rem(inner + s, INNER)).start()
    for k in range(pops):
        popular[inner, k] = three_stage[k]
    arrivals(cuts[1], cuts[3])

    for s in range(1, INNER):
        j = lax.rem(inner + s, INNER)
        three_copy(j, j).wait_recv()

    def popular_fold(k, carry):
        block = jnp.concatenate([popular[j, k] for j in range(INNER)], axis=0)
        fold(block, k + 1, True)
        return carry
    lax.fori_loop(0, pops, popular_fold, 0)

    arrivals(cuts[3], cuts[4])

    for g in range(rows // tokens):
        at = pl.ds(g * tokens, tokens)
        out_ref[:, g * head:(g + 1) * head] = (
            total[:head, at] / total[head:head + 1, at]).T.astype(jnp.bfloat16)

    peers(lambda d: ask_copy(d, d).wait_send())
    peers(lambda d: rare_copy(d, d).wait_send())
    for s in range(1, INNER):
        j = lax.rem(inner + s, INNER)
        one_copy(j, j).wait_send()
        three_copy(j, j).wait_send()

    for k in range(pops):
        @pl.when(outer != k)
        def _():
            two_copy(k, k).wait_send()

    @pl.when(outer < pops)
    def _():
        def mid_done(s, carry):
            d = lax.rem(outer + s, outers)
            mid_copy(lax.rem(outer, pops), d).wait_send()
            return carry
        lax.fori_loop(1, outers, mid_done, 0)


def direct_body(queries, own_kv, store_kv, q_start, pop_ids, pop_pos, rare_ids, rare_count, rare_pos):
    n = lax.axis_size("store")
    tokens = queries.shape[0]
    head = own_kv.shape[1] // 2
    rows = tokens * (queries.shape[1] // head)
    per_device, span, width = store_kv.shape
    requests = rare_ids.shape[1]
    pops = pop_ids.shape[0]
    longest = max(span, tokens)
    lanes = -(-(requests + 1) // 128) * 128
    outers = n // INNER
    piece = span // INNER

    half = np.arange(head) % (head // 2)
    freq = 500000.0 ** (-(2.0 * half) / head)
    sign = np.where(np.arange(head) < head // 2, -1.0, 1.0)
    steps = np.arange(longest)[:, None] * freq[None, :]
    step_cos = np.cos(steps).astype(np.float32)
    step_sin = (np.sin(steps) * sign).astype(np.float32)
    base = jnp.concatenate([q_start, pop_pos[0], rare_pos[0]]).astype(jnp.float32)
    angles = base[:, None] * freq.astype(np.float32)[None, :]
    base_cos = jnp.cos(angles)
    base_sin = jnp.sin(angles) * sign.astype(np.float32)[None, :]
    table = jnp.concatenate([rare_ids[0], rare_count])
    table = jnp.pad(table, (0, lanes - requests - 1))

    vmem = pl.BlockSpec(memory_space=pltpu.VMEM)
    smem = pl.BlockSpec(memory_space=pltpu.SMEM)
    dma = pltpu.SemaphoreType.DMA
    bf16 = jnp.bfloat16
    chunk = min(rows, 512)
    return pl.pallas_call(
        functools.partial(direct_kernel, n, per_device, requests, pops, chunk, head ** -0.5 * np.log2(np.e).item()),
        out_shape=jax.ShapeDtypeStruct(queries.shape, bf16),
        in_specs=[smem, vmem, vmem, vmem, pl.BlockSpec(memory_space=pl.ANY)] + [vmem] * 4,
        out_specs=vmem,
        scratch_shapes=[
            pltpu.VMEM((per_device, span, width), bf16),
            pltpu.VMEM((n, 1, lanes), jnp.int32),
            pltpu.SMEM((n, 1, lanes), jnp.int32),
            pltpu.VMEM((n, span, width), bf16),
            pltpu.VMEM((n, span, width), bf16),
            pltpu.VMEM((rows, head), bf16),
            pltpu.VMEM((head + 16, rows), jnp.float32),
            pltpu.VMEM((1, rows), jnp.float32),
            pltpu.VMEM((INNER, pops, piece, width), bf16),
            pltpu.VMEM((INNER, pops, piece, width), bf16),
            pltpu.VMEM((pops, piece, width), bf16),
            pltpu.VMEM((outers, piece, width), bf16),
            pltpu.VMEM((piece, width), bf16),
            pltpu.VMEM((pops, piece, width), bf16),
            pltpu.VMEM((INNER, pops, piece, width), bf16),
            dma((2,)), dma((n,)), dma((n,)), dma((n,)), dma((n,)),
            dma((INNER,)), dma((INNER,)), dma((outers,)), dma((outers,)), dma((outers,)), dma((pops,)),
            dma((INNER,)), dma((INNER,)),
        ],
        compiler_params=pltpu.CompilerParams(
            collective_id=0, has_side_effects=True, vmem_limit_bytes=60 * 2**20),
    )(pop_ids, table.reshape(1, lanes), queries, own_kv, store_kv,
      base_cos, base_sin, step_cos, step_sin)


PLANES = 4
LANES = 4
PARTS = 2
COARSE = 128
PLACE = 64
LOWEST = -1e30
TINY = 1e-30


def plane_kernel(
    per_device, requests, pops, power,
    pop_ref, ids_ref, count_ref, rare_pos, pop_pos, start_ref,
    queries_ref, own_ref, store_hbm, coarse_cos, coarse_sin, step_cos, step_sin, out_ref,
    store, row, asks, asks_s, info, rows_of, total, tops,
    stage, cand, part_out, part_in, log_out, log_in,
    one_stage, one_recv, two_stage, up_recv, merged, cross_recv, final, popular,
    local_sem, ask_send, ask_recv, query_send, query_sem, block_send, block_sem,
    part_send, part_sem, log_send, log_sem,
    one_send, one_sem, chain_send, chain_sem, three_send, three_sem,
):
    n = PLANES * LANES
    me = lax.axis_index("store")
    plane, lane = me // LANES, lax.rem(me, LANES)
    half = plane // 2
    near, across = plane ^ 1, plane ^ 3
    is_inner = (plane == 1) | (plane == 2)
    is_outer = jnp.logical_not(is_inner)
    far_inner, far_outer = 2 - half, 3 - 3 * half
    asker = (far_inner, far_outer, near, plane)
    head = step_cos.shape[1]
    tokens = queries_ref.shape[0]
    rows = rows_of.shape[1]
    span = store.shape[1]
    piece = span // LANES
    part = rows // PARTS
    pad = total.shape[1] - head

    def remote(src, dst, send, recv_at, target):
        return pltpu.make_async_remote_copy(
            src_ref=src, dst_ref=dst, send_sem=send, recv_sem=recv_at,
            device_id={"store": target}, device_id_type=MESH)

    def ask_copy(slot, target):
        return remote(row, asks.at[slot], ask_send.at[target], ask_recv.at[slot], target)

    def query_copy(number, src, dst, p, target_plane):
        at = pl.ds(p * part, part)
        return remote(
            rows_of.at[src, at], rows_of.at[dst, at], query_send.at[number * PARTS + p],
            query_sem.at[dst * PARTS + p], target_plane * LANES + lane)

    def own_to_near(p):
        return query_copy(0, 3, 2, p, near)

    def own_across(p):
        return query_copy(1, 3, 0, p, across)

    def near_across(p):
        return query_copy(2, 2, 1, p, across)

    def far_to_near(s, p):
        return query_copy(3 + s, s, s, p, near)

    def block_copy(i, d):
        at = i * LANES + d
        return remote(
            stage.at[at], cand.at[at], block_send.at[at], block_sem.at[at],
            plane * LANES + (lane ^ d))

    def part_copies(i, j, target_plane):
        target = target_plane * LANES + lane
        return (
            remote(log_out.at[i], log_in.at[j], log_send.at[i], log_sem.at[j], target),
            remote(part_out.at[i], part_in.at[j], part_send.at[i], part_sem.at[j], target))

    def one_copy(d):
        return remote(
            one_stage.at[d], one_recv.at[d], one_send.at[d], one_sem.at[d],
            plane * LANES + (lane ^ d))

    def chain_copy(step, src, dst, target_plane):
        return remote(src, dst, chain_send.at[step], chain_sem.at[step], target_plane * LANES + lane)

    def up_copy():
        return chain_copy(0, two_stage, up_recv, near)

    def cross_copy():
        return chain_copy(1, merged, cross_recv, across)

    def down_copy():
        return chain_copy(2, final, final, near)

    def popular_at(t):
        return popular.at[:, pl.ds(pl.multiple_of(t * piece, piece), piece)]

    def three_copy(d):
        return remote(
            final, popular_at(lane), three_send.at[d], three_sem.at[d],
            plane * LANES + (lane ^ d))

    def peers(act):
        def step(s, carry):
            act(lax.rem(me + s, n))
            return carry
        lax.fori_loop(1, n, step, 0)

    load = pltpu.make_async_copy(store_hbm, store, local_sem.at[0])
    load.start()
    barrier = pltpu.get_barrier_semaphore()
    peers(lambda d: pl.semaphore_signal(
        barrier, inc=1, device_id={"store": d}, device_id_type=MESH))

    spot = lax.broadcasted_iota(jnp.int32, row.shape, 1)
    wanted = jnp.full(row.shape, -1, jnp.int32)
    for r in range(requests):
        block_id = ids_ref[0, r]
        holder = jnp.where(r < count_ref[0], block_id // per_device, -1)
        wanted = jnp.where(spot == holder, lax.rem(block_id, per_device) + r * per_device, wanted)
        wanted = jnp.where(spot == PLACE + r, rare_pos[0, r], wanted)
    row[...] = wanted
    asks[me] = wanted

    def base_of(position):
        a, b = position // COARSE, lax.rem(position, COARSE)
        ca, sa = coarse_cos[pl.ds(a, 1), :], coarse_sin[pl.ds(a, 1), :]
        cb, sb = step_cos[pl.ds(b, 1), :], step_sin[pl.ds(b, 1), :]
        return ca * cb - sa * sb, sa * cb + ca * sb

    def table(position, count):
        cos_b, sin_b = base_of(position)
        cos_n, sin_n = step_cos[:count, :], step_sin[:count, :]
        return cos_b * cos_n - sin_b * sin_n, sin_b * cos_n + cos_b * sin_n

    def turn(x, cosine, sine):
        x = x.astype(jnp.float32)
        return (x * cosine + pltpu.roll(x, head // 2, 1) * sine).astype(jnp.bfloat16)

    own_cos, own_sin = table(start_ref[0], tokens)
    for g in range(rows // tokens):
        rows_of[3, g * tokens:(g + 1) * tokens, :] = turn(
            queries_ref[:, g * head:(g + 1) * head], own_cos, own_sin)

    def attend(i, keys, values, seen):
        scores = lax.dot_general(
            keys, rows_of[i], (((1,), (1,)), ((), ())),
            preferred_element_type=jnp.float32)
        if seen is not None:
            scores = jnp.where(seen, scores, -jnp.inf)
        top = jnp.max(scores, axis=0, keepdims=True)
        weights = jnp.exp2((scores - top) * power).astype(jnp.bfloat16)
        return top, jnp.dot(values, weights, preferred_element_type=jnp.float32)

    def flip(values):
        return jnp.concatenate(
            [values.T, jnp.ones((pad, values.shape[0]), jnp.bfloat16)], axis=0)

    def blend(i, top, mixed):
        old = tops[i]
        diff = top - old
        factor = jnp.exp2(-jnp.abs(diff) * power)
        rises = diff > 0.0
        tops[i] = jnp.maximum(old, top)
        total[i] = (
            total[i] * jnp.where(rises, factor, 1.0)
            + mixed * jnp.where(rises, 1.0, factor))

    def fold(i, block, position):
        keys = turn(block[:, :head], *table(jnp.maximum(position, 0), span))
        top, mixed = attend(i, keys, flip(block[:, head:]), None)
        blend(i, jnp.where(position >= 0, top, -jnp.inf), mixed)

    load.wait()
    for d in range(LANES):
        begin = pl.multiple_of((lane ^ d) * piece, piece)
        for k in range(pops):
            quarter = store[lax.rem(pop_ref[k], per_device), pl.ds(begin, piece), :]
            if d == 0:
                one_recv[0, k] = quarter
            else:
                one_stage[d, k] = quarter

    pl.semaphore_wait(barrier, n - 1)
    peers(lambda d: ask_copy(me, d).start())
    for p in range(PARTS):
        own_to_near(p).start()

        @pl.when(is_inner)
        def _():
            own_across(p).start()
    for d in range(1, LANES):
        one_copy(d).start()

    token = lax.rem(lax.broadcasted_iota(jnp.int32, (tokens, rows), 1), tokens)
    seen = token >= lax.broadcasted_iota(jnp.int32, (tokens, rows), 0)
    top, mixed = attend(
        3, turn(own_ref[:, :head], own_cos, own_sin), flip(own_ref[:, head:]), seen)
    total[3] = mixed
    tops[3] = top
    for i in range(3):
        total[i] = jnp.zeros(total.shape[1:], jnp.float32)
        tops[i] = jnp.full(tops.shape[1:], LOWEST, jnp.float32)

    peers(lambda d: ask_copy(d, d).wait_recv())
    bring = pltpu.make_async_copy(asks, asks_s, local_sem.at[1])
    bring.start()
    bring.wait()

    def block_for(target):
        return store[lax.rem(jnp.maximum(asks_s[target, 0, me], 0), per_device)]

    def send_blocks(i):
        for d in (2, 3, 1):
            stage[i * LANES + d] = block_for(asker[i] * LANES + (lane ^ d))
            block_copy(i, d).start()
        cand[i * LANES] = block_for(asker[i] * LANES + lane)

    for i in range(3):
        send_blocks(i)

    for i in range(4):
        for d in range(LANES):
            requester = asker[i] * LANES + lane
            value = asks_s[requester, 0, plane * LANES + (lane ^ d)]
            position = asks_s[requester, 0, PLACE + jnp.maximum(value, 0) // per_device]
            info[i * LANES + d] = jnp.where(value >= 0, position, -1)

    def query_wait(s, p):
        at = pl.ds(p * part, part)
        remote(
            rows_of.at[s, at], rows_of.at[s, at], query_send.at[0],
            query_sem.at[s * PARTS + p], me ^ 1).wait_recv()

    @pl.when(is_inner)
    def _():
        for p in range(PARTS):
            query_wait(2, p)
            near_across(p).start()
            query_wait(0, p)
            far_to_near(0, p).start()

    for d in range(1, LANES):
        one_copy(d).wait_recv()
    for k in range(pops):
        two_stage[k] = one_recv[lane ^ lax.rem(pop_ref[k] // per_device, LANES), k]

    def holder_plane(k):
        return pop_ref[k] // (per_device * LANES)

    @pl.when(is_inner)
    def _():
        for p in range(PARTS - 1):
            query_wait(1, p)
            far_to_near(1, p).start()
        up_copy().wait_recv()
        for k in range(pops):
            merged[k] = jnp.where(holder_plane(k) == plane, two_stage[k], up_recv[k])
        cross_copy().start()
        query_wait(1, PARTS - 1)
        far_to_near(1, PARTS - 1).start()

    @pl.when(is_outer)
    def _():
        up_copy().start()
        for p in range(PARTS):
            query_wait(0, p)

    def phase(i):
        def step(d, carry):
            at = i * LANES + d

            @pl.when(d > 0)
            def _():
                remote(
                    stage.at[0], cand.at[at], block_send.at[0], block_sem.at[at], me ^ 1).wait_recv()
            fold(i, cand[at], info[at])
            return carry
        lax.fori_loop(0, LANES, step, 0)

    def send_part(i, j, target_plane):
        weight = jnp.maximum(total[i, head:head + 1, :], TINY)
        part_out[i] = (total[i, :head, :] / weight).astype(jnp.bfloat16)
        log_out[i] = tops[i] + jnp.log2(weight) * (1.0 / power)
        for copy in part_copies(i, j, target_plane):
            copy.start()

    def take_part(i, j):
        for copy in part_copies(0, j, near):
            copy.wait_recv()
        ones = jnp.ones((pad, rows), jnp.float32)
        blend(i, log_in[j], jnp.concatenate([part_in[j].astype(jnp.float32), ones], axis=0))

    def spread():
        for d in range(1, LANES):
            three_copy(d).start()
        popular_at(lane)[...] = final[...]
        send_blocks(3)

    phase(0)

    @pl.when(is_outer)
    def _():
        send_part(0, 0, near)
        for p in range(PARTS):
            query_wait(1, p)

    @pl.when(is_inner)
    def _():
        cross_copy().wait_recv()
        for k in range(pops):
            final[k] = jnp.where(holder_plane(k) // 2 == half, merged[k], cross_recv[k])
        down_copy().start()
        spread()

    phase(1)

    @pl.when(is_outer)
    def _():
        send_part(1, 1, near)
        for p in range(PARTS):
            query_wait(2, p)
        down_copy().wait_recv()
        spread()

    @pl.when(is_inner)
    def _():
        take_part(0, 0)
        send_part(0, 3, far_inner)

    phase(2)
    send_part(2, 2, near)

    @pl.when(is_inner)
    def _():
        take_part(1, 1)
        send_part(1, 3, far_outer)

    for d in range(1, LANES):
        remote(final, popular_at(lane ^ d), three_send.at[d], three_sem.at[d], me ^ 1).wait_recv()

    def popular_fold(k, carry):
        fold(3, popular[k], pop_pos[0, k])
        return carry
    lax.fori_loop(0, pops, popular_fold, 0)

    phase(3)
    take_part(3, 2)
    take_part(3, 3)

    for g in range(rows // tokens):
        at = pl.ds(g * tokens, tokens)
        out_ref[:, g * head:(g + 1) * head] = (
            total[3, :head, at] / total[3, head:head + 1, at]).T.astype(jnp.bfloat16)

    peers(lambda d: ask_copy(d, d).wait_send())
    for p in range(PARTS):
        own_to_near(p).wait_send()

        @pl.when(is_inner)
        def _():
            own_across(p).wait_send()
            near_across(p).wait_send()
            far_to_near(0, p).wait_send()
            far_to_near(1, p).wait_send()
    for d in range(1, LANES):
        for i in range(4):
            block_copy(i, d).wait_send()
        one_copy(d).wait_send()
        three_copy(d).wait_send()
    for i in range(3):
        for copy in part_copies(i, i, near):
            copy.wait_send()

    @pl.when(is_outer)
    def _():
        up_copy().wait_send()

    @pl.when(is_inner)
    def _():
        cross_copy().wait_send()
        down_copy().wait_send()


def plane_body(queries, own_kv, store_kv, q_start, pop_ids, pop_pos, rare_ids, rare_count, rare_pos):
    n = lax.axis_size("store")
    tokens = queries.shape[0]
    head = own_kv.shape[1] // 2
    rows = tokens * (queries.shape[1] // head)
    per_device, span, width = store_kv.shape
    requests = rare_ids.shape[1]
    pops = pop_ids.shape[0]
    longest = max(span, tokens, COARSE)
    piece = span // LANES

    half = np.arange(head) % (head // 2)
    freq = 500000.0 ** (-(2.0 * half) / head)
    sign = np.where(np.arange(head) < head // 2, -1.0, 1.0)

    def tables(positions):
        angles = positions[:, None] * freq[None, :]
        return np.cos(angles).astype(np.float32), (np.sin(angles) * sign).astype(np.float32)

    vmem = pl.BlockSpec(memory_space=pltpu.VMEM)
    smem = pl.BlockSpec(memory_space=pltpu.SMEM)
    dma = pltpu.SemaphoreType.DMA
    bf16, f32 = jnp.bfloat16, jnp.float32

    def blocks(count):
        return pltpu.VMEM((count, span, width), bf16)

    def pieces(*lead):
        return pltpu.VMEM((*lead, piece, width), bf16)

    return pl.pallas_call(
        functools.partial(plane_kernel, per_device, requests, pops, head ** -0.5 * np.log2(np.e).item()),
        out_shape=jax.ShapeDtypeStruct(queries.shape, bf16),
        in_specs=[smem] * 6 + [vmem, vmem, pl.BlockSpec(memory_space=pl.ANY)] + [vmem] * 4,
        out_specs=vmem,
        scratch_shapes=[
            blocks(per_device),
            pltpu.VMEM((1, 128), jnp.int32),
            pltpu.VMEM((n, 1, 128), jnp.int32),
            pltpu.SMEM((n, 1, 128), jnp.int32),
            pltpu.SMEM((4 * LANES,), jnp.int32),
            pltpu.VMEM((4, rows, head), bf16),
            pltpu.VMEM((4, head + 16, rows), f32),
            pltpu.VMEM((4, 1, rows), f32),
            blocks(4 * LANES), blocks(4 * LANES),
            pltpu.VMEM((3, head, rows), bf16), pltpu.VMEM((4, head, rows), bf16),
            pltpu.VMEM((3, 1, rows), f32), pltpu.VMEM((4, 1, rows), f32),
            pieces(LANES, pops), pieces(LANES, pops), pieces(pops), pieces(pops),
            pieces(pops), pieces(pops), pieces(pops), blocks(pops),
            dma((2,)), dma((n,)), dma((n,)), dma((5 * PARTS,)), dma((3 * PARTS,)),
            dma((4 * LANES,)), dma((4 * LANES,)),
            dma((3,)), dma((4,)), dma((3,)), dma((4,)),
            dma((LANES,)), dma((LANES,)), dma((3,)), dma((3,)), dma((LANES,)), dma((LANES,)),
        ],
        compiler_params=pltpu.CompilerParams(
            collective_id=1, has_side_effects=True, vmem_limit_bytes=60 * 2**20),
    )(pop_ids, rare_ids, rare_count, rare_pos, pop_pos, q_start, queries, own_kv, store_kv,
      *tables(np.arange(COARSE) * float(COARSE)), *tables(np.arange(longest) * 1.0))


def body(*args):
    requests, pops = args[6].shape[1], args[4].shape[0]
    if lax.axis_size("store") == PLANES * LANES and requests <= PLACE and pops == 4:
        return plane_body(*args)
    return direct_body(*args)


def solution(mesh):
    both = ("tenant", "store")
    in_specs = (
        P(both, None), P(both, None), P(both, None, None), P(both), P("tenant"),
        P(both, None), P(both, None), P(both), P(both, None),
    )
    return jax.shard_map(
        body, mesh=mesh, in_specs=in_specs, out_specs=P(both, None), check_vma=False)
```

```python
import functools

import jax
import jax.numpy as jnp
import numpy as np
from jax import lax
from jax.experimental import pallas as pl
from jax.experimental.pallas import tpu as pltpu
from jax.sharding import PartitionSpec as P

MESH = pl.DeviceIdType.MESH
INNER = 4
STRIDE = 5
WINDOW = 7


def direct_kernel(
    n, per_device, requests, pops, chunk, power,
    pop_ref, request_ref, queries_ref, own_ref, store_hbm,
    base_cos, base_sin, step_cos, step_sin, out_ref,
    store, asks, asks_s, stage, recv, query_rows, total, tops,
    one_stage, one_recv, two_stage, two_recv, mid_stage, three_stage, popular,
    local_sem, ask_send, ask_recv, rare_send, rare_recv,
    one_send, one_sem, two_send, two_sem, mid_send, mid_sem, three_send, three_sem,
):
    me = lax.axis_index("store")
    inner, outer = lax.rem(me, INNER), me // INNER
    outers = n // INNER
    head = base_cos.shape[1]
    tokens = queries_ref.shape[0]
    rows = query_rows.shape[0]
    span = stage.shape[1]
    piece = span // INNER

    def ask_copy(slot, target):
        return pltpu.make_async_remote_copy(
            src_ref=request_ref, dst_ref=asks.at[slot],
            send_sem=ask_send.at[target], recv_sem=ask_recv.at[slot],
            device_id={"store": target}, device_id_type=MESH)

    def rare_copy(slot, target):
        return pltpu.make_async_remote_copy(
            src_ref=stage.at[target], dst_ref=recv.at[slot],
            send_sem=rare_send.at[target], recv_sem=rare_recv.at[slot],
            device_id={"store": target}, device_id_type=MESH)

    def one_copy(slot, target):
        return pltpu.make_async_remote_copy(
            src_ref=one_stage.at[target], dst_ref=one_recv.at[slot],
            send_sem=one_send.at[target], recv_sem=one_sem.at[slot],
            device_id={"store": outer * INNER + target}, device_id_type=MESH)

    def two_copy(slot, target):
        return pltpu.make_async_remote_copy(
            src_ref=two_stage.at[target], dst_ref=two_recv.at[slot],
            send_sem=two_send.at[target], recv_sem=two_sem.at[slot],
            device_id={"store": target * INNER + inner}, device_id_type=MESH)

    def mid_copy(slot, target):
        return pltpu.make_async_remote_copy(
            src_ref=mid_stage, dst_ref=three_stage.at[slot],
            send_sem=mid_send.at[target], recv_sem=mid_sem.at[slot],
            device_id={"store": target * INNER + inner}, device_id_type=MESH)

    def three_copy(slot, target):
        return pltpu.make_async_remote_copy(
            src_ref=three_stage, dst_ref=popular.at[slot],
            send_sem=three_send.at[target], recv_sem=three_sem.at[slot],
            device_id={"store": outer * INNER + target}, device_id_type=MESH)

    def peers(act):
        def step(s, carry):
            act(lax.rem(me + s, n))
            return carry
        lax.fori_loop(1, n, step, 0)

    load = pltpu.make_async_copy(store_hbm, store, local_sem.at[0])
    load.start()
    barrier = pltpu.get_barrier_semaphore()
    peers(lambda d: pl.semaphore_signal(
        barrier, inc=1, device_id={"store": d}, device_id_type=MESH))
    pl.semaphore_wait(barrier, n - 1)
    peers(lambda d: ask_copy(me, d).start())
    load.wait()

    for s in range(INNER):
        j = lax.rem(inner + s, INNER)
        begin = pl.multiple_of(j * piece, piece)
        for k in range(pops):
            part = store[lax.rem(pop_ref[k], per_device), pl.ds(begin, piece), :]
            if s == 0:
                one_recv[inner, k] = part
            else:
                one_stage[j, k] = part
        if s:
            one_copy(inner, j).start()

    cos0, sin0 = base_cos[0:1, :], base_sin[0:1, :]
    cos_n, sin_n = step_cos[:tokens, :], step_sin[:tokens, :]
    own_cos = cos0 * cos_n - sin0 * sin_n
    own_sin = sin0 * cos_n + cos0 * sin_n

    def turn(x, cosine, sine):
        x = x.astype(jnp.float32)
        return (x * cosine + pltpu.roll(x, head // 2, 1) * sine).astype(jnp.bfloat16)

    for g in range(rows // tokens):
        query_rows[g * tokens:(g + 1) * tokens, :] = turn(
            queries_ref[:, g * head:(g + 1) * head], own_cos, own_sin)

    pad = total.shape[0] - head

    def attend(keys, values, c, seen):
        at = pl.ds(c * chunk, chunk)
        scores = lax.dot_general(
            keys, query_rows[at, :], (((1,), (1,)), ((), ())),
            preferred_element_type=jnp.float32)
        if seen is not None:
            scores = jnp.where(seen, scores, -jnp.inf)
        top = jnp.max(scores, axis=0, keepdims=True)
        weights = jnp.exp2((scores - top) * power).astype(jnp.bfloat16)
        return top, jnp.dot(values, weights, preferred_element_type=jnp.float32)

    def flip(values):
        return jnp.concatenate(
            [values.T, jnp.ones((pad, values.shape[0]), jnp.bfloat16)], axis=0)

    def fold(block, base, live):
        cos_b, sin_b = base_cos[pl.ds(base, 1), :], base_sin[pl.ds(base, 1), :]
        cos_n, sin_n = step_cos[:span, :], step_sin[:span, :]
        keys = turn(
            block[:, :head], cos_b * cos_n - sin_b * sin_n, sin_b * cos_n + cos_b * sin_n)
        values = flip(block[:, head:])
        for c in range(rows // chunk):
            at = pl.ds(c * chunk, chunk)
            top, mixed = attend(keys, values, c, None)
            top = jnp.where(live, top, -jnp.inf)
            old = tops[:, at]
            diff = top - old
            factor = jnp.exp2(-jnp.abs(diff) * power)
            rises = diff > 0.0
            tops[:, at] = jnp.maximum(old, top)
            total[:, at] = (
                total[:, at] * jnp.where(rises, factor, 1.0)
                + mixed * jnp.where(rises, 1.0, factor))

    peers(lambda d: ask_copy(d, d).wait_recv())
    bring = pltpu.make_async_copy(asks, asks_s, local_sem.at[1])
    asks[me] = request_ref[...]
    bring.start()
    bring.wait()

    def slot_for(d):
        def look(r, slot):
            block_id = asks_s[d, 0, r]
            hit = (block_id // per_device == me) & (r < asks_s[d, 0, requests])
            return jnp.where(hit, lax.rem(block_id, per_device), slot)
        return lax.fori_loop(0, requests, look, jnp.int32(0), unroll=min(requests, 8))

    def reply(first, last):
        def step(s, carry):
            d = lax.rem(me + s * STRIDE, n)
            stage[d] = store[slot_for(d)]
            rare_copy(me, d).start()
            return carry
        lax.fori_loop(first, last, step, 0)

    cuts = [1, 3, 5, WINDOW + 1, n]
    reply(cuts[0], cuts[1])
    recv[me] = store[slot_for(me)]

    for s in range(1, INNER):
        j = lax.rem(inner + s, INNER)
        one_copy(j, j).wait_recv()
    for k in range(pops):
        two_stage[k] = one_recv[lax.rem(pop_ref[k] // per_device, INNER), k]
    for k in range(pops):
        @pl.when(outer != k)
        def _():
            two_copy(outer, k).start()

        @pl.when(outer == k)
        def _():
            two_recv[k] = two_stage[k]

    def rare_fold(h):
        def look(r, found):
            hit = (asks_s[me, 0, r] // per_device == h) & (r < asks_s[me, 0, requests])
            return jnp.where(hit, r, found)
        r = lax.fori_loop(0, requests, look, jnp.int32(-1), unroll=min(requests, 8))
        fold(recv[h], jnp.maximum(r, 0) + 1 + pops, r >= 0)

    def arrivals(first, last):
        def step(s, carry):
            h = lax.rem(me + (n - s) * STRIDE, n)
            rare_copy(h, h).wait_recv()
            rare_fold(h)

            @pl.when(s + WINDOW < n)
            def _():
                reply(s + WINDOW, s + WINDOW + 1)
            return carry
        lax.fori_loop(first, last, step, 0)

    reply(cuts[1], cuts[2])

    own_keys = turn(own_ref[:, :head], own_cos, own_sin)
    own_values = flip(own_ref[:, head:])
    for c in range(rows // chunk):
        at = pl.ds(c * chunk, chunk)
        token = lax.rem(
            lax.broadcasted_iota(jnp.int32, (tokens, chunk), 1) + c * chunk, tokens)
        seen = token >= lax.broadcasted_iota(jnp.int32, (tokens, chunk), 0)
        top, total[:, at] = attend(own_keys, own_values, c, seen)
        tops[:, at] = top

    rare_fold(me)

    @pl.when(outer < pops)
    def _():
        def two_wait(s, carry):
            d = lax.rem(outer + s, outers)
            pltpu.make_async_remote_copy(
                src_ref=mid_stage, dst_ref=two_recv.at[d],
                send_sem=mid_send.at[d], recv_sem=two_sem.at[d],
                device_id={"store": d * INNER + inner}, device_id_type=MESH).wait_recv()
            return carry
        lax.fori_loop(1, outers, two_wait, 0)
        mine = lax.rem(outer, pops)
        mid_stage[...] = two_recv[pop_ref[mine] // (per_device * INNER)]

        def mid_start(s, carry):
            mid_copy(mine, lax.rem(outer + s, outers)).start()
            return carry
        lax.fori_loop(1, outers, mid_start, 0)
        three_stage[mine] = mid_stage[...]

    reply(cuts[2], cuts[3])
    arrivals(cuts[0], cuts[1])
    for k in range(pops):
        @pl.when(outer != k)
        def _():
            mid_copy(k, k).wait_recv()
    for s in range(1, INNER):
        three_copy(inner, lax.rem(inner + s, INNER)).start()
    for k in range(pops):
        popular[inner, k] = three_stage[k]
    arrivals(cuts[1], cuts[3])

    for s in range(1, INNER):
        j = lax.rem(inner + s, INNER)
        three_copy(j, j).wait_recv()

    def popular_fold(k, carry):
        block = jnp.concatenate([popular[j, k] for j in range(INNER)], axis=0)
        fold(block, k + 1, True)
        return carry
    lax.fori_loop(0, pops, popular_fold, 0)

    arrivals(cuts[3], cuts[4])

    for g in range(rows // tokens):
        at = pl.ds(g * tokens, tokens)
        out_ref[:, g * head:(g + 1) * head] = (
            total[:head, at] / total[head:head + 1, at]).T.astype(jnp.bfloat16)

    peers(lambda d: ask_copy(d, d).wait_send())
    peers(lambda d: rare_copy(d, d).wait_send())
    for s in range(1, INNER):
        j = lax.rem(inner + s, INNER)
        one_copy(j, j).wait_send()
        three_copy(j, j).wait_send()

    for k in range(pops):
        @pl.when(outer != k)
        def _():
            two_copy(k, k).wait_send()

    @pl.when(outer < pops)
    def _():
        def mid_done(s, carry):
            d = lax.rem(outer + s, outers)
            mid_copy(lax.rem(outer, pops), d).wait_send()
            return carry
        lax.fori_loop(1, outers, mid_done, 0)


def direct_body(queries, own_kv, store_kv, q_start, pop_ids, pop_pos, rare_ids, rare_count, rare_pos):
    n = lax.axis_size("store")
    tokens = queries.shape[0]
    head = own_kv.shape[1] // 2
    rows = tokens * (queries.shape[1] // head)
    per_device, span, width = store_kv.shape
    requests = rare_ids.shape[1]
    pops = pop_ids.shape[0]
    longest = max(span, tokens)
    lanes = -(-(requests + 1) // 128) * 128
    outers = n // INNER
    piece = span // INNER

    half = np.arange(head) % (head // 2)
    freq = 500000.0 ** (-(2.0 * half) / head)
    sign = np.where(np.arange(head) < head // 2, -1.0, 1.0)
    steps = np.arange(longest)[:, None] * freq[None, :]
    step_cos = np.cos(steps).astype(np.float32)
    step_sin = (np.sin(steps) * sign).astype(np.float32)
    base = jnp.concatenate([q_start, pop_pos[0], rare_pos[0]]).astype(jnp.float32)
    angles = base[:, None] * freq.astype(np.float32)[None, :]
    base_cos = jnp.cos(angles)
    base_sin = jnp.sin(angles) * sign.astype(np.float32)[None, :]
    table = jnp.concatenate([rare_ids[0], rare_count])
    table = jnp.pad(table, (0, lanes - requests - 1))

    vmem = pl.BlockSpec(memory_space=pltpu.VMEM)
    smem = pl.BlockSpec(memory_space=pltpu.SMEM)
    dma = pltpu.SemaphoreType.DMA
    bf16 = jnp.bfloat16
    chunk = min(rows, 512)
    return pl.pallas_call(
        functools.partial(direct_kernel, n, per_device, requests, pops, chunk, head ** -0.5 * np.log2(np.e).item()),
        out_shape=jax.ShapeDtypeStruct(queries.shape, bf16),
        in_specs=[smem, vmem, vmem, vmem, pl.BlockSpec(memory_space=pl.ANY)] + [vmem] * 4,
        out_specs=vmem,
        scratch_shapes=[
            pltpu.VMEM((per_device, span, width), bf16),
            pltpu.VMEM((n, 1, lanes), jnp.int32),
            pltpu.SMEM((n, 1, lanes), jnp.int32),
            pltpu.VMEM((n, span, width), bf16),
            pltpu.VMEM((n, span, width), bf16),
            pltpu.VMEM((rows, head), bf16),
            pltpu.VMEM((head + 16, rows), jnp.float32),
            pltpu.VMEM((1, rows), jnp.float32),
            pltpu.VMEM((INNER, pops, piece, width), bf16),
            pltpu.VMEM((INNER, pops, piece, width), bf16),
            pltpu.VMEM((pops, piece, width), bf16),
            pltpu.VMEM((outers, piece, width), bf16),
            pltpu.VMEM((piece, width), bf16),
            pltpu.VMEM((pops, piece, width), bf16),
            pltpu.VMEM((INNER, pops, piece, width), bf16),
            dma((2,)), dma((n,)), dma((n,)), dma((n,)), dma((n,)),
            dma((INNER,)), dma((INNER,)), dma((outers,)), dma((outers,)), dma((outers,)), dma((pops,)),
            dma((INNER,)), dma((INNER,)),
        ],
        compiler_params=pltpu.CompilerParams(
            collective_id=0, has_side_effects=True, vmem_limit_bytes=60 * 2**20),
    )(pop_ids, table.reshape(1, lanes), queries, own_kv, store_kv,
      base_cos, base_sin, step_cos, step_sin)


PLANES = 4
LANES = 4
PARTS = 2
STEPS = 4
COARSE = 128
PLACE = 64
LOWEST = -1e30
TINY = 1e-30


def plane_kernel(
    per_device, requests, pops, power,
    pop_ref, ids_ref, count_ref, rare_pos, pop_pos, start_ref,
    queries_hbm, own_hbm, store_hbm, trig_hbm, out_ref,
    store, queries_ref, own_ref, trig, row, asks, asks_s, info, rows_of, total, tops,
    stage, cand, part_out, part_in, log_out, log_in,
    zero_stage, zero_recv, one_stage, one_recv, two_stage, up_recv, merged, cross_recv, final, popular,
    local_sem, ask_send, ask_recv, query_send, query_sem, block_send, block_sem,
    part_send, part_sem, log_send, log_sem,
    pair_send, pair_sem, chain_send, chain_sem, three_send, three_sem,
):
    n = PLANES * LANES
    me = lax.axis_index("store")
    plane, lane = me // LANES, lax.rem(me, LANES)
    half = plane // 2
    near, across = plane ^ 1, plane ^ 3
    is_inner = (plane == 1) | (plane == 2)
    is_outer = jnp.logical_not(is_inner)
    far_inner, far_outer = 2 - half, 3 - 3 * half
    asker = (far_inner, far_outer, near, plane)
    head = trig.shape[1]
    longest = (trig.shape[0] - 2 * COARSE) // 2
    coarse_cos, coarse_sin = trig.at[pl.ds(0, COARSE)], trig.at[pl.ds(COARSE, COARSE)]
    step_cos = trig.at[pl.ds(2 * COARSE, longest)]
    step_sin = trig.at[pl.ds(2 * COARSE + longest, longest)]
    tokens = queries_ref.shape[0]
    rows = rows_of.shape[1]
    span = store.shape[1]
    piece = span // LANES
    part, step_rows = rows // PARTS, rows // STEPS
    pad = total.shape[1] - head

    def remote(src, dst, send, recv_at, target):
        return pltpu.make_async_remote_copy(
            src_ref=src, dst_ref=dst, send_sem=send, recv_sem=recv_at,
            device_id={"store": target}, device_id_type=MESH)

    def ask_copy(slot, target):
        return remote(row, asks.at[slot], ask_send.at[target], ask_recv.at[slot], target)

    def query_copy(number, src, dst, p, target_plane):
        at = pl.ds(p * step_rows, step_rows)
        return remote(
            rows_of.at[src, at], rows_of.at[dst, at], query_send.at[number * STEPS + p],
            query_sem.at[dst * STEPS + p], target_plane * LANES + lane)

    def own_to_near(p):
        return query_copy(0, 3, 2, p, near)

    def own_across(p):
        return query_copy(1, 3, 0, p, across)

    def near_across(p):
        return query_copy(2, 2, 1, p, across)

    def far_to_near(s, p):
        return query_copy(3 + s, s, s, p, near)

    def block_copy(i, d):
        at = i * LANES + d
        return remote(
            stage.at[at], cand.at[at], block_send.at[at], block_sem.at[at],
            plane * LANES + (lane ^ d))

    def part_copy(i, j, p, target_plane):
        return remote(
            part_out.at[i, p], part_in.at[j, p], part_send.at[i * PARTS + p],
            part_sem.at[j * PARTS + p], target_plane * LANES + lane)

    def log_copy(i, j, p, target_plane):
        return remote(
            log_out.at[i, p], log_in.at[j, p], log_send.at[i * PARTS + p],
            log_sem.at[j * PARTS + p], target_plane * LANES + lane)

    def zero_copy():
        return remote(zero_stage, zero_recv, pair_send.at[0], pair_sem.at[0], me ^ 1)

    def one_copy():
        return remote(one_stage, one_recv, pair_send.at[1], pair_sem.at[1], me ^ 2)

    def chain_copy(step, src, dst, target_plane):
        return remote(src, dst, chain_send.at[step], chain_sem.at[step], target_plane * LANES + lane)

    def up_copy():
        return chain_copy(0, two_stage, up_recv, near)

    def cross_copy():
        return chain_copy(1, merged, cross_recv, across)

    def down_copy():
        return chain_copy(2, final, final, near)

    def popular_at(t):
        begin = ((t & 1) * 2 + (t >> 1)) * piece
        return popular.at[:, pl.ds(pl.multiple_of(begin, piece), piece)]

    def three_copy():
        return remote(final, popular_at(lane), three_send.at[0], three_sem.at[0], me ^ 2)

    def four_copy(y):
        t = lane ^ (y * 2)
        return remote(popular_at(t), popular_at(t), three_send.at[1 + y], three_sem.at[1 + y], me ^ 1)

    def peers(act):
        def step(s, carry):
            act(lax.rem(me + s, n))
            return carry
        lax.fori_loop(1, n, step, 0)

    barrier = pltpu.get_barrier_semaphore()
    peers(lambda d: pl.semaphore_signal(
        barrier, inc=1, device_id={"store": d}, device_id_type=MESH))
    loads = [
        pltpu.make_async_copy(a, b, local_sem.at[2 + i])
        for i, (a, b) in enumerate(
            ((trig_hbm, trig), (queries_hbm, queries_ref), (own_hbm, own_ref), (store_hbm, store)))]
    for copy in loads:
        copy.start()

    spot = lax.broadcasted_iota(jnp.int32, row.shape, 1)
    wanted = jnp.full(row.shape, -1, jnp.int32)
    for r in range(requests):
        block_id = ids_ref[0, r]
        holder = jnp.where(r < count_ref[0], block_id // per_device, -1)
        wanted = jnp.where(spot == holder, lax.rem(block_id, per_device) + r * per_device, wanted)
        wanted = jnp.where(spot == PLACE + r, rare_pos[0, r], wanted)
    row[...] = wanted
    asks[me] = wanted

    def base_of(position):
        a, b = position // COARSE, lax.rem(position, COARSE)
        ca, sa = coarse_cos[pl.ds(a, 1), :], coarse_sin[pl.ds(a, 1), :]
        cb, sb = step_cos[pl.ds(b, 1), :], step_sin[pl.ds(b, 1), :]
        return ca * cb - sa * sb, sa * cb + ca * sb

    def table(position, count):
        cos_b, sin_b = base_of(position)
        cos_n, sin_n = step_cos[:count, :], step_sin[:count, :]
        return cos_b * cos_n - sin_b * sin_n, sin_b * cos_n + cos_b * sin_n

    def turn(x, cosine, sine):
        x = x.astype(jnp.float32)
        return (x * cosine + pltpu.roll(x, head // 2, 1) * sine).astype(jnp.bfloat16)

    def attend(i, keys, values, seen):
        scores = lax.dot_general(
            keys, rows_of[i], (((1,), (1,)), ((), ())),
            preferred_element_type=jnp.float32)
        if seen is not None:
            scores = jnp.where(seen, scores, -jnp.inf)
        top = jnp.max(scores, axis=0, keepdims=True)
        weights = jnp.exp2((scores - top) * power).astype(jnp.bfloat16)
        return top, jnp.dot(values, weights, preferred_element_type=jnp.float32)

    def flip(values):
        return jnp.concatenate(
            [values.T, jnp.ones((pad, values.shape[0]), jnp.bfloat16)], axis=0)

    def blend(i, at, top, mixed):
        old = tops[i, :, at]
        diff = top - old
        factor = jnp.exp2(-jnp.abs(diff) * power)
        rises = diff > 0.0
        tops[i, :, at] = jnp.maximum(old, top)
        total[i, :, at] = (
            total[i, :, at] * jnp.where(rises, factor, 1.0)
            + mixed * jnp.where(rises, 1.0, factor))

    def fold(i, block, position):
        keys = turn(block[:, :head], *table(jnp.maximum(position, 0), span))
        top, mixed = attend(i, keys, flip(block[:, head:]), None)
        blend(i, pl.ds(0, rows), jnp.where(position >= 0, top, -jnp.inf), mixed)

    core, y = lane & 1, lane >> 1

    def my_part(k, begin, size):
        return store[lax.rem(pop_ref[k], per_device), pl.ds(pl.multiple_of(begin, piece), size), :]

    pl.semaphore_wait(barrier, n - 1)
    peers(lambda d: ask_copy(me, d).start())
    for copy in loads[:2]:
        copy.wait()
    own_cos, own_sin = table(start_ref[0], tokens)
    for g in range(rows // tokens):
        rows_of[3, g * tokens:(g + 1) * tokens, :] = turn(
            queries_ref[:, g * head:(g + 1) * head], own_cos, own_sin)

    for p in range(STEPS):
        @pl.when(is_inner)
        def _():
            own_across(p).start()

        @pl.when(is_outer | (p < STEPS // 2))
        def _():
            own_to_near(p).start()

    loads[3].wait()
    for k in range(pops):
        zero_stage[k] = my_part(k, (1 - core) * 2 * piece, 2 * piece)
    zero_copy().start()

    def holder_lane(k):
        return lax.rem(pop_ref[k] // per_device, LANES)

    zero_copy().wait_recv()
    for k in range(pops):
        mine = (holder_lane(k) & 1) == core
        for to, t in ((one_stage, 1 - y), (two_stage, y)):
            other = zero_recv[k, pl.ds(pl.multiple_of(t * piece, piece), piece), :]
            to[k] = jnp.where(mine, my_part(k, (core * 2 + t) * piece, piece), other)
    one_copy().start()

    peers(lambda d: ask_copy(d, d).wait_recv())
    bring = pltpu.make_async_copy(asks, asks_s, local_sem.at[1])
    bring.start()
    bring.wait()

    def block_for(target):
        return store[lax.rem(jnp.maximum(asks_s[target, 0, me], 0), per_device)]

    def asker_at(i):
        return jnp.where(i == 0, asker[0], jnp.where(i == 1, asker[1], jnp.where(i == 2, asker[2], asker[3])))

    def send_blocks(i):
        for d in (2, 3, 1):
            stage[i * LANES + d] = block_for(asker_at(i) * LANES + (lane ^ d))
            block_copy(i, d).start()
        cand[i * LANES] = block_for(asker_at(i) * LANES + lane)

    order = [jnp.where(is_inner, a, b) for a, b in ((2, 0), (0, 1), (1, 2))] + [3]
    for i in order[:3]:
        send_blocks(i)

    def query_wait(s, p):
        at = pl.ds(p * step_rows, step_rows)
        remote(
            rows_of.at[s, at], rows_of.at[s, at], query_send.at[0],
            query_sem.at[s * STEPS + p], me ^ 1).wait_recv()

    @pl.when(is_inner)
    def _():
        for p in range(STEPS):
            query_wait(2, p)
            near_across(p).start()
            query_wait(0, p)
            far_to_near(0, p).start()

    for i in range(4):
        for d in range(LANES):
            requester = asker[i] * LANES + lane
            value = asks_s[requester, 0, plane * LANES + (lane ^ d)]
            position = asks_s[requester, 0, PLACE + jnp.maximum(value, 0) // per_device]
            info[i * LANES + d] = jnp.where(value >= 0, position, -1)

    loads[2].wait()
    token = lax.rem(lax.broadcasted_iota(jnp.int32, (tokens, rows), 1), tokens)
    seen = token >= lax.broadcasted_iota(jnp.int32, (tokens, rows), 0)
    top, mixed = attend(
        3, turn(own_ref[:, :head], own_cos, own_sin), flip(own_ref[:, head:]), seen)
    total[3] = mixed
    tops[3] = top
    for i in range(3):
        total[i] = jnp.zeros(total.shape[1:], jnp.float32)
        tops[i] = jnp.full(tops.shape[1:], LOWEST, jnp.float32)

    one_copy().wait_recv()
    for k in range(pops):
        two_stage[k] = jnp.where((holder_lane(k) >> 1) == y, two_stage[k], one_recv[k])

    def holder_plane(k):
        return pop_ref[k] // (per_device * LANES)

    @pl.when(is_inner)
    def _():
        for p in range(STEPS // 2):
            query_wait(1, p)
            far_to_near(1, p).start()
        up_copy().wait_recv()
        for k in range(pops):
            merged[k] = jnp.where(holder_plane(k) == plane, two_stage[k], up_recv[k])
        cross_copy().start()
        for p in range(STEPS // 2, STEPS):
            query_wait(1, p)
            far_to_near(1, p).start()
        for p in range(STEPS // 2, STEPS):
            own_to_near(p).start()

    @pl.when(is_outer)
    def _():
        up_copy().start()
        for p in range(STEPS):
            query_wait(0, p)

    def phase(i, first=0, last=LANES):
        def step(d, carry):
            at = i * LANES + d

            @pl.when(d > 0)
            def _():
                remote(
                    stage.at[0], cand.at[at], block_send.at[0], block_sem.at[at], me ^ 1).wait_recv()
            fold(i, cand[at], info[at])
            return carry
        lax.fori_loop(first, last, step, 0)

    def send_piece(i, j, p, target_plane):
        at = pl.ds(p * part, part)
        weight = jnp.maximum(total[i, head:head + 1, at], TINY)
        log_out[i, p] = tops[i, :, at] + jnp.log2(weight) * (1.0 / power)
        part_out[i, p] = (total[i, :head, at] / weight).astype(jnp.bfloat16)
        log_copy(i, j, p, target_plane).start()
        part_copy(i, j, p, target_plane).start()

    def take_piece(i, j, p):
        log_copy(0, j, p, near).wait_recv()
        part_copy(0, j, p, near).wait_recv()
        ones = jnp.ones((pad, part), jnp.float32)
        blend(
            i, pl.ds(p * part, part), log_in[j, p],
            jnp.concatenate([part_in[j, p].astype(jnp.float32), ones], axis=0))

    def send_part(i, j, target_plane):
        for p in range(PARTS):
            send_piece(i, j, p, target_plane)

    def pass_part(i, target_plane):
        for p in range(PARTS):
            take_piece(i, i, p)
            send_piece(i, 3, p, target_plane)

    def spread():
        three_copy().start()
        popular_at(lane)[...] = final[...]
        four_copy(0).start()
        send_blocks(3)

    phase(order[0])

    @pl.when(is_outer)
    def _():
        send_part(0, 0, near)
        for p in range(STEPS):
            query_wait(1, p)

    @pl.when(is_inner)
    def _():
        cross_copy().wait_recv()
        for k in range(pops):
            final[k] = jnp.where(holder_plane(k) // 2 == half, merged[k], cross_recv[k])
        down_copy().start()
        spread()
        send_part(2, 2, near)

    phase(order[1])

    @pl.when(is_outer)
    def _():
        send_part(1, 1, near)
        for p in range(STEPS):
            query_wait(2, p)
        down_copy().wait_recv()
        spread()

    @pl.when(is_inner)
    def _():
        pass_part(0, far_inner)

    phase(order[2])

    @pl.when(is_outer)
    def _():
        send_part(2, 2, near)

    @pl.when(is_inner)
    def _():
        pass_part(1, far_outer)

    phase(3, 0, 2)
    remote(final, popular_at(lane ^ 2), three_send.at[0], three_sem.at[0], me ^ 1).wait_recv()
    four_copy(1).start()
    for t in (0, 1):
        remote(
            final, popular_at(lane ^ (1 + 2 * t)), three_send.at[0], three_sem.at[1 + t], me ^ 1).wait_recv()

    def popular_fold(k, carry):
        fold(3, popular[k], pop_pos[0, k])
        return carry
    lax.fori_loop(0, pops, popular_fold, 0)

    phase(3, 2, 3)
    for p in range(PARTS):
        take_piece(3, 2, p)
        take_piece(3, 3, p)
    phase(3, 3, 4)

    for g in range(rows // tokens):
        at = pl.ds(g * tokens, tokens)
        out_ref[:, g * head:(g + 1) * head] = (
            total[3, :head, at] / total[3, head:head + 1, at]).T.astype(jnp.bfloat16)

    peers(lambda d: ask_copy(d, d).wait_send())
    for p in range(STEPS):
        own_to_near(p).wait_send()

        @pl.when(is_inner)
        def _():
            own_across(p).wait_send()
            near_across(p).wait_send()
            far_to_near(0, p).wait_send()
            far_to_near(1, p).wait_send()
    for i in range(4):
        for d in range(1, LANES):
            block_copy(i, d).wait_send()
    for copy in (zero_copy(), one_copy(), three_copy(), four_copy(0), four_copy(1)):
        copy.wait_send()
    for i in range(3):
        for p in range(PARTS):
            log_copy(i, i, p, near).wait_send()
            part_copy(i, i, p, near).wait_send()

    @pl.when(is_outer)
    def _():
        up_copy().wait_send()

    @pl.when(is_inner)
    def _():
        cross_copy().wait_send()
        down_copy().wait_send()


def plane_body(queries, own_kv, store_kv, q_start, pop_ids, pop_pos, rare_ids, rare_count, rare_pos):
    n = lax.axis_size("store")
    tokens = queries.shape[0]
    head = own_kv.shape[1] // 2
    rows = tokens * (queries.shape[1] // head)
    per_device, span, width = store_kv.shape
    requests = rare_ids.shape[1]
    pops = pop_ids.shape[0]
    longest = max(span, tokens, COARSE)
    piece = span // LANES

    half = np.arange(head) % (head // 2)
    freq = 500000.0 ** (-(2.0 * half) / head)
    sign = np.where(np.arange(head) < head // 2, -1.0, 1.0)

    def tables(positions):
        angles = positions[:, None] * freq[None, :]
        return np.cos(angles).astype(np.float32), (np.sin(angles) * sign).astype(np.float32)

    vmem = pl.BlockSpec(memory_space=pltpu.VMEM)
    smem = pl.BlockSpec(memory_space=pltpu.SMEM)
    dma = pltpu.SemaphoreType.DMA
    bf16, f32 = jnp.bfloat16, jnp.float32

    trig = np.concatenate([*tables(np.arange(COARSE) * float(COARSE)), *tables(np.arange(longest) * 1.0)])

    def blocks(count):
        return pltpu.VMEM((count, span, width), bf16)

    def pieces(*lead):
        return pltpu.VMEM((*lead, piece, width), bf16)

    return pl.pallas_call(
        functools.partial(plane_kernel, per_device, requests, pops, head ** -0.5 * np.log2(np.e).item()),
        out_shape=jax.ShapeDtypeStruct(queries.shape, bf16),
        in_specs=[smem] * 6 + [pl.BlockSpec(memory_space=pl.ANY)] * 4,
        out_specs=vmem,
        scratch_shapes=[
            blocks(per_device),
            pltpu.VMEM(queries.shape, bf16), pltpu.VMEM(own_kv.shape, bf16), pltpu.VMEM(trig.shape, f32),
            pltpu.VMEM((1, 128), jnp.int32),
            pltpu.VMEM((n, 1, 128), jnp.int32),
            pltpu.SMEM((n, 1, 128), jnp.int32),
            pltpu.SMEM((4 * LANES,), jnp.int32),
            pltpu.VMEM((4, rows, head), bf16),
            pltpu.VMEM((4, head + 16, rows), f32),
            pltpu.VMEM((4, 1, rows), f32),
            blocks(4 * LANES), blocks(4 * LANES),
            pltpu.VMEM((3, PARTS, head, rows // PARTS), bf16),
            pltpu.VMEM((4, PARTS, head, rows // PARTS), bf16),
            pltpu.VMEM((3, PARTS, 1, rows // PARTS), f32), pltpu.VMEM((4, PARTS, 1, rows // PARTS), f32),
            pltpu.VMEM((pops, 2 * piece, width), bf16), pltpu.VMEM((pops, 2 * piece, width), bf16),
            pieces(pops), pieces(pops), pieces(pops), pieces(pops),
            pieces(pops), pieces(pops), pieces(pops), blocks(pops),
            dma((6,)), dma((n,)), dma((n,)), dma((5 * STEPS,)), dma((3 * STEPS,)),
            dma((4 * LANES,)), dma((4 * LANES,)),
            dma((3 * PARTS,)), dma((4 * PARTS,)), dma((3 * PARTS,)), dma((4 * PARTS,)),
            dma((2,)), dma((2,)), dma((3,)), dma((3,)), dma((3,)), dma((3,)),
        ],
        compiler_params=pltpu.CompilerParams(
            collective_id=1, has_side_effects=True, vmem_limit_bytes=60 * 2**20),
    )(pop_ids, rare_ids, rare_count, rare_pos, pop_pos, q_start, queries, own_kv, store_kv,
      trig)


def body(*args):
    requests, pops = args[6].shape[1], args[4].shape[0]
    if lax.axis_size("store") == PLANES * LANES and requests <= PLACE and pops == 4:
        return plane_body(*args)
    return direct_body(*args)


def solution(mesh):
    both = ("tenant", "store")
    in_specs = (
        P(both, None), P(both, None), P(both, None, None), P(both), P("tenant"),
        P(both, None), P(both, None), P(both), P(both, None),
    )
    return jax.shard_map(
        body, mesh=mesh, in_specs=in_specs, out_specs=P(both, None), check_vma=False)
```

```python
import functools

import jax
import jax.numpy as jnp
import numpy as np
from jax import lax
from jax.experimental import pallas as pl
from jax.experimental.pallas import tpu as pltpu
from jax.sharding import PartitionSpec as P

MESH = pl.DeviceIdType.MESH
INNER = 4
STRIDE = 5
WINDOW = 7


def direct_kernel(
    n, per_device, requests, pops, chunk, power,
    pop_ref, request_ref, queries_ref, own_ref, store_hbm,
    base_cos, base_sin, step_cos, step_sin, out_ref,
    store, asks, asks_s, stage, recv, query_rows, total, tops,
    one_stage, one_recv, two_stage, two_recv, mid_stage, three_stage, popular,
    local_sem, ask_send, ask_recv, rare_send, rare_recv,
    one_send, one_sem, two_send, two_sem, mid_send, mid_sem, three_send, three_sem,
):
    me = lax.axis_index("store")
    inner, outer = lax.rem(me, INNER), me // INNER
    outers = n // INNER
    head = base_cos.shape[1]
    tokens = queries_ref.shape[0]
    rows = query_rows.shape[0]
    span = stage.shape[1]
    piece = span // INNER

    def ask_copy(slot, target):
        return pltpu.make_async_remote_copy(
            src_ref=request_ref, dst_ref=asks.at[slot],
            send_sem=ask_send.at[target], recv_sem=ask_recv.at[slot],
            device_id={"store": target}, device_id_type=MESH)

    def rare_copy(slot, target):
        return pltpu.make_async_remote_copy(
            src_ref=stage.at[target], dst_ref=recv.at[slot],
            send_sem=rare_send.at[target], recv_sem=rare_recv.at[slot],
            device_id={"store": target}, device_id_type=MESH)

    def one_copy(slot, target):
        return pltpu.make_async_remote_copy(
            src_ref=one_stage.at[target], dst_ref=one_recv.at[slot],
            send_sem=one_send.at[target], recv_sem=one_sem.at[slot],
            device_id={"store": outer * INNER + target}, device_id_type=MESH)

    def two_copy(slot, target):
        return pltpu.make_async_remote_copy(
            src_ref=two_stage.at[target], dst_ref=two_recv.at[slot],
            send_sem=two_send.at[target], recv_sem=two_sem.at[slot],
            device_id={"store": target * INNER + inner}, device_id_type=MESH)

    def mid_copy(slot, target):
        return pltpu.make_async_remote_copy(
            src_ref=mid_stage, dst_ref=three_stage.at[slot],
            send_sem=mid_send.at[target], recv_sem=mid_sem.at[slot],
            device_id={"store": target * INNER + inner}, device_id_type=MESH)

    def three_copy(slot, target):
        return pltpu.make_async_remote_copy(
            src_ref=three_stage, dst_ref=popular.at[slot],
            send_sem=three_send.at[target], recv_sem=three_sem.at[slot],
            device_id={"store": outer * INNER + target}, device_id_type=MESH)

    def peers(act):
        def step(s, carry):
            act(lax.rem(me + s, n))
            return carry
        lax.fori_loop(1, n, step, 0)

    load = pltpu.make_async_copy(store_hbm, store, local_sem.at[0])
    load.start()
    barrier = pltpu.get_barrier_semaphore()
    peers(lambda d: pl.semaphore_signal(
        barrier, inc=1, device_id={"store": d}, device_id_type=MESH))
    pl.semaphore_wait(barrier, n - 1)
    peers(lambda d: ask_copy(me, d).start())
    load.wait()

    for s in range(INNER):
        j = lax.rem(inner + s, INNER)
        begin = pl.multiple_of(j * piece, piece)
        for k in range(pops):
            part = store[lax.rem(pop_ref[k], per_device), pl.ds(begin, piece), :]
            if s == 0:
                one_recv[inner, k] = part
            else:
                one_stage[j, k] = part
        if s:
            one_copy(inner, j).start()

    cos0, sin0 = base_cos[0:1, :], base_sin[0:1, :]
    cos_n, sin_n = step_cos[:tokens, :], step_sin[:tokens, :]
    own_cos = cos0 * cos_n - sin0 * sin_n
    own_sin = sin0 * cos_n + cos0 * sin_n

    def turn(x, cosine, sine):
        x = x.astype(jnp.float32)
        return (x * cosine + pltpu.roll(x, head // 2, 1) * sine).astype(jnp.bfloat16)

    for g in range(rows // tokens):
        query_rows[g * tokens:(g + 1) * tokens, :] = turn(
            queries_ref[:, g * head:(g + 1) * head], own_cos, own_sin)

    pad = total.shape[0] - head

    def attend(keys, values, c, seen):
        at = pl.ds(c * chunk, chunk)
        scores = lax.dot_general(
            keys, query_rows[at, :], (((1,), (1,)), ((), ())),
            preferred_element_type=jnp.float32)
        if seen is not None:
            scores = jnp.where(seen, scores, -jnp.inf)
        top = jnp.max(scores, axis=0, keepdims=True)
        weights = jnp.exp2((scores - top) * power).astype(jnp.bfloat16)
        return top, jnp.dot(values, weights, preferred_element_type=jnp.float32)

    def flip(values):
        return jnp.concatenate(
            [values.T, jnp.ones((pad, values.shape[0]), jnp.bfloat16)], axis=0)

    def fold(block, base, live):
        cos_b, sin_b = base_cos[pl.ds(base, 1), :], base_sin[pl.ds(base, 1), :]
        cos_n, sin_n = step_cos[:span, :], step_sin[:span, :]
        keys = turn(
            block[:, :head], cos_b * cos_n - sin_b * sin_n, sin_b * cos_n + cos_b * sin_n)
        values = flip(block[:, head:])
        for c in range(rows // chunk):
            at = pl.ds(c * chunk, chunk)
            top, mixed = attend(keys, values, c, None)
            top = jnp.where(live, top, -jnp.inf)
            old = tops[:, at]
            diff = top - old
            factor = jnp.exp2(-jnp.abs(diff) * power)
            rises = diff > 0.0
            tops[:, at] = jnp.maximum(old, top)
            total[:, at] = (
                total[:, at] * jnp.where(rises, factor, 1.0)
                + mixed * jnp.where(rises, 1.0, factor))

    peers(lambda d: ask_copy(d, d).wait_recv())
    bring = pltpu.make_async_copy(asks, asks_s, local_sem.at[1])
    asks[me] = request_ref[...]
    bring.start()
    bring.wait()

    def slot_for(d):
        def look(r, slot):
            block_id = asks_s[d, 0, r]
            hit = (block_id // per_device == me) & (r < asks_s[d, 0, requests])
            return jnp.where(hit, lax.rem(block_id, per_device), slot)
        return lax.fori_loop(0, requests, look, jnp.int32(0), unroll=min(requests, 8))

    def reply(first, last):
        def step(s, carry):
            d = lax.rem(me + s * STRIDE, n)
            stage[d] = store[slot_for(d)]
            rare_copy(me, d).start()
            return carry
        lax.fori_loop(first, last, step, 0)

    cuts = [1, 3, 5, WINDOW + 1, n]
    reply(cuts[0], cuts[1])
    recv[me] = store[slot_for(me)]

    for s in range(1, INNER):
        j = lax.rem(inner + s, INNER)
        one_copy(j, j).wait_recv()
    for k in range(pops):
        two_stage[k] = one_recv[lax.rem(pop_ref[k] // per_device, INNER), k]
    for k in range(pops):
        @pl.when(outer != k)
        def _():
            two_copy(outer, k).start()

        @pl.when(outer == k)
        def _():
            two_recv[k] = two_stage[k]

    def rare_fold(h):
        def look(r, found):
            hit = (asks_s[me, 0, r] // per_device == h) & (r < asks_s[me, 0, requests])
            return jnp.where(hit, r, found)
        r = lax.fori_loop(0, requests, look, jnp.int32(-1), unroll=min(requests, 8))
        fold(recv[h], jnp.maximum(r, 0) + 1 + pops, r >= 0)

    def arrivals(first, last):
        def step(s, carry):
            h = lax.rem(me + (n - s) * STRIDE, n)
            rare_copy(h, h).wait_recv()
            rare_fold(h)

            @pl.when(s + WINDOW < n)
            def _():
                reply(s + WINDOW, s + WINDOW + 1)
            return carry
        lax.fori_loop(first, last, step, 0)

    reply(cuts[1], cuts[2])

    own_keys = turn(own_ref[:, :head], own_cos, own_sin)
    own_values = flip(own_ref[:, head:])
    for c in range(rows // chunk):
        at = pl.ds(c * chunk, chunk)
        token = lax.rem(
            lax.broadcasted_iota(jnp.int32, (tokens, chunk), 1) + c * chunk, tokens)
        seen = token >= lax.broadcasted_iota(jnp.int32, (tokens, chunk), 0)
        top, total[:, at] = attend(own_keys, own_values, c, seen)
        tops[:, at] = top

    rare_fold(me)

    @pl.when(outer < pops)
    def _():
        def two_wait(s, carry):
            d = lax.rem(outer + s, outers)
            pltpu.make_async_remote_copy(
                src_ref=mid_stage, dst_ref=two_recv.at[d],
                send_sem=mid_send.at[d], recv_sem=two_sem.at[d],
                device_id={"store": d * INNER + inner}, device_id_type=MESH).wait_recv()
            return carry
        lax.fori_loop(1, outers, two_wait, 0)
        mine = lax.rem(outer, pops)
        mid_stage[...] = two_recv[pop_ref[mine] // (per_device * INNER)]

        def mid_start(s, carry):
            mid_copy(mine, lax.rem(outer + s, outers)).start()
            return carry
        lax.fori_loop(1, outers, mid_start, 0)
        three_stage[mine] = mid_stage[...]

    reply(cuts[2], cuts[3])
    arrivals(cuts[0], cuts[1])
    for k in range(pops):
        @pl.when(outer != k)
        def _():
            mid_copy(k, k).wait_recv()
    for s in range(1, INNER):
        three_copy(inner, lax.rem(inner + s, INNER)).start()
    for k in range(pops):
        popular[inner, k] = three_stage[k]
    arrivals(cuts[1], cuts[3])

    for s in range(1, INNER):
        j = lax.rem(inner + s, INNER)
        three_copy(j, j).wait_recv()

    def popular_fold(k, carry):
        block = jnp.concatenate([popular[j, k] for j in range(INNER)], axis=0)
        fold(block, k + 1, True)
        return carry
    lax.fori_loop(0, pops, popular_fold, 0)

    arrivals(cuts[3], cuts[4])

    for g in range(rows // tokens):
        at = pl.ds(g * tokens, tokens)
        out_ref[:, g * head:(g + 1) * head] = (
            total[:head, at] / total[head:head + 1, at]).T.astype(jnp.bfloat16)

    peers(lambda d: ask_copy(d, d).wait_send())
    peers(lambda d: rare_copy(d, d).wait_send())
    for s in range(1, INNER):
        j = lax.rem(inner + s, INNER)
        one_copy(j, j).wait_send()
        three_copy(j, j).wait_send()

    for k in range(pops):
        @pl.when(outer != k)
        def _():
            two_copy(k, k).wait_send()

    @pl.when(outer < pops)
    def _():
        def mid_done(s, carry):
            d = lax.rem(outer + s, outers)
            mid_copy(lax.rem(outer, pops), d).wait_send()
            return carry
        lax.fori_loop(1, outers, mid_done, 0)


def direct_body(queries, own_kv, store_kv, q_start, pop_ids, pop_pos, rare_ids, rare_count, rare_pos):
    n = lax.axis_size("store")
    tokens = queries.shape[0]
    head = own_kv.shape[1] // 2
    rows = tokens * (queries.shape[1] // head)
    per_device, span, width = store_kv.shape
    requests = rare_ids.shape[1]
    pops = pop_ids.shape[0]
    longest = max(span, tokens)
    lanes = -(-(requests + 1) // 128) * 128
    outers = n // INNER
    piece = span // INNER

    half = np.arange(head) % (head // 2)
    freq = 500000.0 ** (-(2.0 * half) / head)
    sign = np.where(np.arange(head) < head // 2, -1.0, 1.0)
    steps = np.arange(longest)[:, None] * freq[None, :]
    step_cos = np.cos(steps).astype(np.float32)
    step_sin = (np.sin(steps) * sign).astype(np.float32)
    base = jnp.concatenate([q_start, pop_pos[0], rare_pos[0]]).astype(jnp.float32)
    angles = base[:, None] * freq.astype(np.float32)[None, :]
    base_cos = jnp.cos(angles)
    base_sin = jnp.sin(angles) * sign.astype(np.float32)[None, :]
    table = jnp.concatenate([rare_ids[0], rare_count])
    table = jnp.pad(table, (0, lanes - requests - 1))

    vmem = pl.BlockSpec(memory_space=pltpu.VMEM)
    smem = pl.BlockSpec(memory_space=pltpu.SMEM)
    dma = pltpu.SemaphoreType.DMA
    bf16 = jnp.bfloat16
    chunk = min(rows, 512)
    return pl.pallas_call(
        functools.partial(direct_kernel, n, per_device, requests, pops, chunk, head ** -0.5 * np.log2(np.e).item()),
        out_shape=jax.ShapeDtypeStruct(queries.shape, bf16),
        in_specs=[smem, vmem, vmem, vmem, pl.BlockSpec(memory_space=pl.ANY)] + [vmem] * 4,
        out_specs=vmem,
        scratch_shapes=[
            pltpu.VMEM((per_device, span, width), bf16),
            pltpu.VMEM((n, 1, lanes), jnp.int32),
            pltpu.SMEM((n, 1, lanes), jnp.int32),
            pltpu.VMEM((n, span, width), bf16),
            pltpu.VMEM((n, span, width), bf16),
            pltpu.VMEM((rows, head), bf16),
            pltpu.VMEM((head + 16, rows), jnp.float32),
            pltpu.VMEM((1, rows), jnp.float32),
            pltpu.VMEM((INNER, pops, piece, width), bf16),
            pltpu.VMEM((INNER, pops, piece, width), bf16),
            pltpu.VMEM((pops, piece, width), bf16),
            pltpu.VMEM((outers, piece, width), bf16),
            pltpu.VMEM((piece, width), bf16),
            pltpu.VMEM((pops, piece, width), bf16),
            pltpu.VMEM((INNER, pops, piece, width), bf16),
            dma((2,)), dma((n,)), dma((n,)), dma((n,)), dma((n,)),
            dma((INNER,)), dma((INNER,)), dma((outers,)), dma((outers,)), dma((outers,)), dma((pops,)),
            dma((INNER,)), dma((INNER,)),
        ],
        compiler_params=pltpu.CompilerParams(
            collective_id=0, has_side_effects=True, vmem_limit_bytes=60 * 2**20),
    )(pop_ids, table.reshape(1, lanes), queries, own_kv, store_kv,
      base_cos, base_sin, step_cos, step_sin)


PLANES = 4
LANES = 4
PARTS = 2
STEPS = 4
COARSE = 128
PLACE = 64
LOWEST = -1e30
TINY = 1e-30


def plane_kernel(
    per_device, requests, pops, power,
    pop_ref, ids_ref, count_ref, rare_pos, pop_pos, start_ref,
    queries_hbm, own_hbm, store_hbm, trig_hbm, out_ref,
    store, queries_ref, own_ref, trig, row, asks, asks_s, info, rows_of, total, tops,
    stage, cand, part_out, part_in, log_out, log_in,
    zero_stage, zero_recv, one_stage, one_recv, two_stage, up_recv, merged, cross_recv, final, popular,
    local_sem, ask_send, ask_recv, query_send, query_sem, block_send, block_sem,
    part_send, part_sem, log_send, log_sem,
    pair_send, pair_sem, chain_send, chain_sem, three_send, three_sem,
):
    n = PLANES * LANES
    me = lax.axis_index("store")
    plane, lane = me // LANES, lax.rem(me, LANES)
    half = plane // 2
    near, across = plane ^ 1, plane ^ 3
    is_inner = (plane == 1) | (plane == 2)
    is_outer = jnp.logical_not(is_inner)
    far_inner, far_outer = 2 - half, 3 - 3 * half
    asker = (far_inner, far_outer, near, plane)
    head = trig.shape[1]
    longest = (trig.shape[0] - 2 * COARSE) // 2
    coarse_cos, coarse_sin = trig.at[pl.ds(0, COARSE)], trig.at[pl.ds(COARSE, COARSE)]
    step_cos = trig.at[pl.ds(2 * COARSE, longest)]
    step_sin = trig.at[pl.ds(2 * COARSE + longest, longest)]
    tokens = queries_ref.shape[0]
    rows = rows_of.shape[1]
    span = store.shape[1]
    piece = span // LANES
    part, step_rows = rows // PARTS, rows // STEPS
    pad = total.shape[1] - head

    def remote(src, dst, send, recv_at, target):
        return pltpu.make_async_remote_copy(
            src_ref=src, dst_ref=dst, send_sem=send, recv_sem=recv_at,
            device_id={"store": target}, device_id_type=MESH)

    def ask_copy(slot, target):
        return remote(row, asks.at[slot], ask_send.at[target], ask_recv.at[slot], target)

    def query_copy(number, src, dst, p, target_plane):
        at = pl.ds(p * step_rows, step_rows)
        return remote(
            rows_of.at[src, at], rows_of.at[dst, at], query_send.at[number * STEPS + p],
            query_sem.at[dst * STEPS + p], target_plane * LANES + lane)

    def own_to_near(p):
        return query_copy(0, 3, 2, p, near)

    def own_across(p):
        return query_copy(1, 3, 0, p, across)

    def near_across(p):
        return query_copy(2, 2, 1, p, across)

    def far_to_near(s, p):
        return query_copy(3 + s, s, s, p, near)

    def block_copy(i, d):
        at = i * LANES + d
        return remote(
            stage.at[at], cand.at[at], block_send.at[at], block_sem.at[at],
            plane * LANES + (lane ^ d))

    def part_copy(i, j, p, target_plane):
        return remote(
            part_out.at[i, p], part_in.at[j, p], part_send.at[i * PARTS + p],
            part_sem.at[j * PARTS + p], target_plane * LANES + lane)

    def log_copy(i, j, p, target_plane):
        return remote(
            log_out.at[i, p], log_in.at[j, p], log_send.at[i * PARTS + p],
            log_sem.at[j * PARTS + p], target_plane * LANES + lane)

    def zero_copy():
        return remote(zero_stage, zero_recv, pair_send.at[0], pair_sem.at[0], me ^ 1)

    def one_copy():
        return remote(one_stage, one_recv, pair_send.at[1], pair_sem.at[1], me ^ 2)

    def chain_copy(step, src, dst, target_plane):
        return remote(src, dst, chain_send.at[step], chain_sem.at[step], target_plane * LANES + lane)

    def up_copy():
        return chain_copy(0, two_stage, up_recv, near)

    def cross_copy():
        return chain_copy(1, merged, cross_recv, across)

    def down_copy():
        return chain_copy(2, final, final, near)

    def popular_at(t):
        begin = ((t & 1) * 2 + (t >> 1)) * piece
        return popular.at[:, pl.ds(pl.multiple_of(begin, piece), piece)]

    def three_copy():
        return remote(final, popular_at(lane), three_send.at[0], three_sem.at[0], me ^ 2)

    def four_copy(y):
        t = lane ^ (y * 2)
        return remote(popular_at(t), popular_at(t), three_send.at[1 + y], three_sem.at[1 + y], me ^ 1)

    def peers(act):
        def step(s, carry):
            act(lax.rem(me + s, n))
            return carry
        lax.fori_loop(1, n, step, 0)

    barrier = pltpu.get_barrier_semaphore()
    peers(lambda d: pl.semaphore_signal(
        barrier, inc=1, device_id={"store": d}, device_id_type=MESH))
    loads = [
        pltpu.make_async_copy(a, b, local_sem.at[2 + i])
        for i, (a, b) in enumerate(
            ((trig_hbm, trig), (queries_hbm, queries_ref), (own_hbm, own_ref), (store_hbm, store)))]
    for copy in loads:
        copy.start()

    spot = lax.broadcasted_iota(jnp.int32, row.shape, 1)
    wanted = jnp.full(row.shape, -1, jnp.int32)
    for r in range(requests):
        block_id = ids_ref[0, r]
        holder = jnp.where(r < count_ref[0], block_id // per_device, -1)
        wanted = jnp.where(spot == holder, lax.rem(block_id, per_device) + r * per_device, wanted)
        wanted = jnp.where(spot == PLACE + r, rare_pos[0, r], wanted)
    row[...] = wanted
    asks[me] = wanted

    def base_of(position):
        a, b = position // COARSE, lax.rem(position, COARSE)
        ca, sa = coarse_cos[pl.ds(a, 1), :], coarse_sin[pl.ds(a, 1), :]
        cb, sb = step_cos[pl.ds(b, 1), :], step_sin[pl.ds(b, 1), :]
        return ca * cb - sa * sb, sa * cb + ca * sb

    def table(position, count):
        cos_b, sin_b = base_of(position)
        cos_n, sin_n = step_cos[:count, :], step_sin[:count, :]
        return cos_b * cos_n - sin_b * sin_n, sin_b * cos_n + cos_b * sin_n

    def turn(x, cosine, sine):
        x = x.astype(jnp.float32)
        return (x * cosine + pltpu.roll(x, head // 2, 1) * sine).astype(jnp.bfloat16)

    def attend(i, keys, values, seen):
        scores = lax.dot_general(
            keys, rows_of[i], (((1,), (1,)), ((), ())),
            preferred_element_type=jnp.float32)
        if seen is not None:
            scores = jnp.where(seen, scores, -jnp.inf)
        top = jnp.max(scores, axis=0, keepdims=True)
        weights = jnp.exp2((scores - top) * power).astype(jnp.bfloat16)
        return top, jnp.dot(values, weights, preferred_element_type=jnp.float32)

    def flip(values):
        return jnp.concatenate(
            [values.T, jnp.ones((pad, values.shape[0]), jnp.bfloat16)], axis=0)

    def blend(i, at, top, mixed):
        old = tops[i, :, at]
        diff = top - old
        factor = jnp.exp2(-jnp.abs(diff) * power)
        rises = diff > 0.0
        tops[i, :, at] = jnp.maximum(old, top)
        total[i, :, at] = (
            total[i, :, at] * jnp.where(rises, factor, 1.0)
            + mixed * jnp.where(rises, 1.0, factor))

    def fold(i, block, position):
        keys = turn(block[:, :head], *table(jnp.maximum(position, 0), span))
        top, mixed = attend(i, keys, flip(block[:, head:]), None)
        blend(i, pl.ds(0, rows), jnp.where(position >= 0, top, -jnp.inf), mixed)

    core, y = lane & 1, lane >> 1

    def my_part(k, begin, size):
        return store[lax.rem(pop_ref[k], per_device), pl.ds(pl.multiple_of(begin, piece), size), :]

    pl.semaphore_wait(barrier, n - 1)
    peers(lambda d: ask_copy(me, d).start())
    for copy in loads[:2]:
        copy.wait()
    own_cos, own_sin = table(start_ref[0], tokens)
    for g in range(rows // tokens):
        rows_of[3, g * tokens:(g + 1) * tokens, :] = turn(
            queries_ref[:, g * head:(g + 1) * head], own_cos, own_sin)

    for p in range(STEPS):
        @pl.when(is_inner)
        def _():
            own_across(p).start()

        @pl.when(is_outer | (p < STEPS // 2))
        def _():
            own_to_near(p).start()

    loads[3].wait()
    for k in range(pops):
        zero_stage[k] = my_part(k, (1 - core) * 2 * piece, 2 * piece)
    zero_copy().start()

    def holder_lane(k):
        return lax.rem(pop_ref[k] // per_device, LANES)

    zero_copy().wait_recv()
    for k in range(pops):
        mine = (holder_lane(k) & 1) == core
        for to, t in ((one_stage, 1 - y), (two_stage, y)):
            other = zero_recv[k, pl.ds(pl.multiple_of(t * piece, piece), piece), :]
            to[k] = jnp.where(mine, my_part(k, (core * 2 + t) * piece, piece), other)
    one_copy().start()

    peers(lambda d: ask_copy(d, d).wait_recv())
    bring = pltpu.make_async_copy(asks, asks_s, local_sem.at[1])
    bring.start()
    bring.wait()

    def block_for(target):
        return store[lax.rem(jnp.maximum(asks_s[target, 0, me], 0), per_device)]

    def asker_at(i):
        return jnp.where(i == 0, asker[0], jnp.where(i == 1, asker[1], jnp.where(i == 2, asker[2], asker[3])))

    def send_blocks(i):
        for d in (2, 3, 1):
            stage[i * LANES + d] = block_for(asker_at(i) * LANES + (lane ^ d))
            block_copy(i, d).start()
        cand[i * LANES] = block_for(asker_at(i) * LANES + lane)

    order = [jnp.where(is_inner, a, b) for a, b in ((2, 0), (0, 1), (1, 2))] + [3]
    for i in order[:3]:
        send_blocks(i)

    def query_wait(s, p):
        at = pl.ds(p * step_rows, step_rows)
        remote(
            rows_of.at[s, at], rows_of.at[s, at], query_send.at[0],
            query_sem.at[s * STEPS + p], me ^ 1).wait_recv()

    @pl.when(is_inner)
    def _():
        for p in range(STEPS):
            query_wait(2, p)
            near_across(p).start()
            query_wait(0, p)
            far_to_near(0, p).start()

    for i in range(4):
        for d in range(LANES):
            requester = asker[i] * LANES + lane
            value = asks_s[requester, 0, plane * LANES + (lane ^ d)]
            position = asks_s[requester, 0, PLACE + jnp.maximum(value, 0) // per_device]
            info[i * LANES + d] = jnp.where(value >= 0, position, -1)

    loads[2].wait()
    token = lax.rem(lax.broadcasted_iota(jnp.int32, (tokens, rows), 1), tokens)
    seen = token >= lax.broadcasted_iota(jnp.int32, (tokens, rows), 0)
    top, mixed = attend(
        3, turn(own_ref[:, :head], own_cos, own_sin), flip(own_ref[:, head:]), seen)
    total[3] = mixed
    tops[3] = top
    for i in range(3):
        total[i] = jnp.zeros(total.shape[1:], jnp.float32)
        tops[i] = jnp.full(tops.shape[1:], LOWEST, jnp.float32)

    one_copy().wait_recv()
    for k in range(pops):
        two_stage[k] = jnp.where((holder_lane(k) >> 1) == y, two_stage[k], one_recv[k])

    def holder_plane(k):
        return pop_ref[k] // (per_device * LANES)

    @pl.when(is_inner)
    def _():
        for p in range(STEPS // 2):
            query_wait(1, p)
            far_to_near(1, p).start()
        up_copy().wait_recv()
        for k in range(pops):
            merged[k] = jnp.where(holder_plane(k) == plane, two_stage[k], up_recv[k])
        cross_copy().start()
        for p in range(STEPS // 2, STEPS):
            query_wait(1, p)
            far_to_near(1, p).start()
        for p in range(STEPS // 2, STEPS):
            own_to_near(p).start()

    @pl.when(is_outer)
    def _():
        up_copy().start()
        for p in range(STEPS):
            query_wait(0, p)

    def phase(i, first=0, last=LANES):
        def step(d, carry):
            at = i * LANES + d

            @pl.when(d > 0)
            def _():
                remote(
                    stage.at[0], cand.at[at], block_send.at[0], block_sem.at[at], me ^ 1).wait_recv()
            fold(i, cand[at], info[at])
            return carry
        lax.fori_loop(first, last, step, 0)

    def send_piece(i, j, p, target_plane):
        at = pl.ds(p * part, part)
        weight = jnp.maximum(total[i, head:head + 1, at], TINY)
        log_out[i, p] = tops[i, :, at] + jnp.log2(weight) * (1.0 / power)
        part_out[i, p] = (total[i, :head, at] / weight).astype(jnp.bfloat16)
        log_copy(i, j, p, target_plane).start()
        part_copy(i, j, p, target_plane).start()

    def take_piece(i, j, p):
        log_copy(0, j, p, near).wait_recv()
        part_copy(0, j, p, near).wait_recv()
        ones = jnp.ones((pad, part), jnp.float32)
        blend(
            i, pl.ds(p * part, part), log_in[j, p],
            jnp.concatenate([part_in[j, p].astype(jnp.float32), ones], axis=0))

    def send_part(i, j, target_plane):
        for p in range(PARTS):
            send_piece(i, j, p, target_plane)

    def pass_part(i, target_plane):
        for p in range(PARTS):
            take_piece(i, i, p)
            send_piece(i, 3, p, target_plane)

    def spread():
        three_copy().start()
        popular_at(lane)[...] = final[...]
        four_copy(0).start()
        send_blocks(3)

    phase(order[0])

    @pl.when(is_outer)
    def _():
        send_part(0, 0, near)
        for p in range(STEPS):
            query_wait(1, p)

    @pl.when(is_inner)
    def _():
        cross_copy().wait_recv()
        for k in range(pops):
            final[k] = jnp.where(holder_plane(k) // 2 == half, merged[k], cross_recv[k])
        down_copy().start()
        spread()
        send_part(2, 2, near)

    phase(order[1])

    @pl.when(is_outer)
    def _():
        send_part(1, 1, near)
        for p in range(STEPS):
            query_wait(2, p)
        down_copy().wait_recv()
        spread()

    @pl.when(is_inner)
    def _():
        pass_part(0, far_inner)

    phase(order[2])

    @pl.when(is_outer)
    def _():
        send_part(2, 2, near)

    @pl.when(is_inner)
    def _():
        pass_part(1, far_outer)

    phase(3, 0, 2)
    remote(final, popular_at(lane ^ 2), three_send.at[0], three_sem.at[0], me ^ 1).wait_recv()
    four_copy(1).start()
    for t in (0, 1):
        remote(
            final, popular_at(lane ^ (1 + 2 * t)), three_send.at[0], three_sem.at[1 + t], me ^ 1).wait_recv()

    def popular_fold(k, carry):
        fold(3, popular[k], pop_pos[0, k])
        return carry
    lax.fori_loop(0, pops, popular_fold, 0)

    phase(3, 2, 3)
    for p in range(PARTS):
        take_piece(3, 2, p)
    phase(3, 3, 4)
    for p in range(PARTS):
        take_piece(3, 3, p)

    for g in range(rows // tokens):
        at = pl.ds(g * tokens, tokens)
        out_ref[:, g * head:(g + 1) * head] = (
            total[3, :head, at] / total[3, head:head + 1, at]).T.astype(jnp.bfloat16)

    peers(lambda d: ask_copy(d, d).wait_send())
    for p in range(STEPS):
        own_to_near(p).wait_send()

        @pl.when(is_inner)
        def _():
            own_across(p).wait_send()
            near_across(p).wait_send()
            far_to_near(0, p).wait_send()
            far_to_near(1, p).wait_send()
    for i in range(4):
        for d in range(1, LANES):
            block_copy(i, d).wait_send()
    for copy in (zero_copy(), one_copy(), three_copy(), four_copy(0), four_copy(1)):
        copy.wait_send()
    for i in range(3):
        for p in range(PARTS):
            log_copy(i, i, p, near).wait_send()
            part_copy(i, i, p, near).wait_send()

    @pl.when(is_outer)
    def _():
        up_copy().wait_send()

    @pl.when(is_inner)
    def _():
        cross_copy().wait_send()
        down_copy().wait_send()


def plane_body(queries, own_kv, store_kv, q_start, pop_ids, pop_pos, rare_ids, rare_count, rare_pos):
    n = lax.axis_size("store")
    tokens = queries.shape[0]
    head = own_kv.shape[1] // 2
    rows = tokens * (queries.shape[1] // head)
    per_device, span, width = store_kv.shape
    requests = rare_ids.shape[1]
    pops = pop_ids.shape[0]
    longest = max(span, tokens, COARSE)
    piece = span // LANES

    half = np.arange(head) % (head // 2)
    freq = 500000.0 ** (-(2.0 * half) / head)
    sign = np.where(np.arange(head) < head // 2, -1.0, 1.0)

    def tables(positions):
        angles = positions[:, None] * freq[None, :]
        return np.cos(angles).astype(np.float32), (np.sin(angles) * sign).astype(np.float32)

    vmem = pl.BlockSpec(memory_space=pltpu.VMEM)
    smem = pl.BlockSpec(memory_space=pltpu.SMEM)
    dma = pltpu.SemaphoreType.DMA
    bf16, f32 = jnp.bfloat16, jnp.float32

    trig = np.concatenate([*tables(np.arange(COARSE) * float(COARSE)), *tables(np.arange(longest) * 1.0)])

    def blocks(count):
        return pltpu.VMEM((count, span, width), bf16)

    def pieces(*lead):
        return pltpu.VMEM((*lead, piece, width), bf16)

    return pl.pallas_call(
        functools.partial(plane_kernel, per_device, requests, pops, head ** -0.5 * np.log2(np.e).item()),
        out_shape=pltpu.VMEM(queries.shape, bf16),
        in_specs=[smem] * 6 + [pl.BlockSpec(memory_space=pl.ANY)] * 4,
        out_specs=vmem,
        scratch_shapes=[
            blocks(per_device),
            pltpu.VMEM(queries.shape, bf16), pltpu.VMEM(own_kv.shape, bf16), pltpu.VMEM(trig.shape, f32),
            pltpu.VMEM((1, 128), jnp.int32),
            pltpu.VMEM((n, 1, 128), jnp.int32),
            pltpu.SMEM((n, 1, 128), jnp.int32),
            pltpu.SMEM((4 * LANES,), jnp.int32),
            pltpu.VMEM((4, rows, head), bf16),
            pltpu.VMEM((4, head + 16, rows), f32),
            pltpu.VMEM((4, 1, rows), f32),
            blocks(4 * LANES), blocks(4 * LANES),
            pltpu.VMEM((3, PARTS, head, rows // PARTS), bf16),
            pltpu.VMEM((4, PARTS, head, rows // PARTS), bf16),
            pltpu.VMEM((3, PARTS, 1, rows // PARTS), f32), pltpu.VMEM((4, PARTS, 1, rows // PARTS), f32),
            pltpu.VMEM((pops, 2 * piece, width), bf16), pltpu.VMEM((pops, 2 * piece, width), bf16),
            pieces(pops), pieces(pops), pieces(pops), pieces(pops),
            pieces(pops), pieces(pops), pieces(pops), blocks(pops),
            dma((6,)), dma((n,)), dma((n,)), dma((5 * STEPS,)), dma((3 * STEPS,)),
            dma((4 * LANES,)), dma((4 * LANES,)),
            dma((3 * PARTS,)), dma((4 * PARTS,)), dma((3 * PARTS,)), dma((4 * PARTS,)),
            dma((2,)), dma((2,)), dma((3,)), dma((3,)), dma((3,)), dma((3,)),
        ],
        compiler_params=pltpu.CompilerParams(
            collective_id=1, has_side_effects=True, vmem_limit_bytes=60 * 2**20),
    )(pop_ids, rare_ids, rare_count, rare_pos, pop_pos, q_start, queries, own_kv, store_kv,
      trig)


def body(*args):
    requests, pops = args[6].shape[1], args[4].shape[0]
    if lax.axis_size("store") == PLANES * LANES and requests <= PLACE and pops == 4:
        return plane_body(*args)
    return direct_body(*args)


def solution(mesh):
    both = ("tenant", "store")
    in_specs = (
        P(both, None), P(both, None), P(both, None, None), P(both), P("tenant"),
        P(both, None), P(both, None), P(both), P(both, None),
    )
    return jax.shard_map(
        body, mesh=mesh, in_specs=in_specs, out_specs=P(both, None), check_vma=False)
```

```python
import functools

import jax
import jax.numpy as jnp
import numpy as np
from jax import lax
from jax.experimental import pallas as pl
from jax.experimental.pallas import tpu as pltpu
from jax.sharding import PartitionSpec as P

MESH = pl.DeviceIdType.MESH
INNER = 4
STRIDE = 5
WINDOW = 7


def direct_kernel(
    n, per_device, requests, pops, chunk, power,
    pop_ref, request_ref, queries_ref, own_ref, store_hbm,
    base_cos, base_sin, step_cos, step_sin, out_ref,
    store, asks, asks_s, stage, recv, query_rows, total, tops,
    one_stage, one_recv, two_stage, two_recv, mid_stage, three_stage, popular,
    local_sem, ask_send, ask_recv, rare_send, rare_recv,
    one_send, one_sem, two_send, two_sem, mid_send, mid_sem, three_send, three_sem,
):
    me = lax.axis_index("store")
    inner, outer = lax.rem(me, INNER), me // INNER
    outers = n // INNER
    head = base_cos.shape[1]
    tokens = queries_ref.shape[0]
    rows = query_rows.shape[0]
    span = stage.shape[1]
    piece = span // INNER

    def ask_copy(slot, target):
        return pltpu.make_async_remote_copy(
            src_ref=request_ref, dst_ref=asks.at[slot],
            send_sem=ask_send.at[target], recv_sem=ask_recv.at[slot],
            device_id={"store": target}, device_id_type=MESH)

    def rare_copy(slot, target):
        return pltpu.make_async_remote_copy(
            src_ref=stage.at[target], dst_ref=recv.at[slot],
            send_sem=rare_send.at[target], recv_sem=rare_recv.at[slot],
            device_id={"store": target}, device_id_type=MESH)

    def one_copy(slot, target):
        return pltpu.make_async_remote_copy(
            src_ref=one_stage.at[target], dst_ref=one_recv.at[slot],
            send_sem=one_send.at[target], recv_sem=one_sem.at[slot],
            device_id={"store": outer * INNER + target}, device_id_type=MESH)

    def two_copy(slot, target):
        return pltpu.make_async_remote_copy(
            src_ref=two_stage.at[target], dst_ref=two_recv.at[slot],
            send_sem=two_send.at[target], recv_sem=two_sem.at[slot],
            device_id={"store": target * INNER + inner}, device_id_type=MESH)

    def mid_copy(slot, target):
        return pltpu.make_async_remote_copy(
            src_ref=mid_stage, dst_ref=three_stage.at[slot],
            send_sem=mid_send.at[target], recv_sem=mid_sem.at[slot],
            device_id={"store": target * INNER + inner}, device_id_type=MESH)

    def three_copy(slot, target):
        return pltpu.make_async_remote_copy(
            src_ref=three_stage, dst_ref=popular.at[slot],
            send_sem=three_send.at[target], recv_sem=three_sem.at[slot],
            device_id={"store": outer * INNER + target}, device_id_type=MESH)

    def peers(act):
        def step(s, carry):
            act(lax.rem(me + s, n))
            return carry
        lax.fori_loop(1, n, step, 0)

    load = pltpu.make_async_copy(store_hbm, store, local_sem.at[0])
    load.start()
    barrier = pltpu.get_barrier_semaphore()
    peers(lambda d: pl.semaphore_signal(
        barrier, inc=1, device_id={"store": d}, device_id_type=MESH))
    pl.semaphore_wait(barrier, n - 1)
    peers(lambda d: ask_copy(me, d).start())
    load.wait()

    for s in range(INNER):
        j = lax.rem(inner + s, INNER)
        begin = pl.multiple_of(j * piece, piece)
        for k in range(pops):
            part = store[lax.rem(pop_ref[k], per_device), pl.ds(begin, piece), :]
            if s == 0:
                one_recv[inner, k] = part
            else:
                one_stage[j, k] = part
        if s:
            one_copy(inner, j).start()

    cos0, sin0 = base_cos[0:1, :], base_sin[0:1, :]
    cos_n, sin_n = step_cos[:tokens, :], step_sin[:tokens, :]
    own_cos = cos0 * cos_n - sin0 * sin_n
    own_sin = sin0 * cos_n + cos0 * sin_n

    def turn(x, cosine, sine):
        x = x.astype(jnp.float32)
        return (x * cosine + pltpu.roll(x, head // 2, 1) * sine).astype(jnp.bfloat16)

    for g in range(rows // tokens):
        query_rows[g * tokens:(g + 1) * tokens, :] = turn(
            queries_ref[:, g * head:(g + 1) * head], own_cos, own_sin)

    pad = total.shape[0] - head

    def attend(keys, values, c, seen):
        at = pl.ds(c * chunk, chunk)
        scores = lax.dot_general(
            keys, query_rows[at, :], (((1,), (1,)), ((), ())),
            preferred_element_type=jnp.float32)
        if seen is not None:
            scores = jnp.where(seen, scores, -jnp.inf)
        top = jnp.max(scores, axis=0, keepdims=True)
        weights = jnp.exp2((scores - top) * power).astype(jnp.bfloat16)
        return top, jnp.dot(values, weights, preferred_element_type=jnp.float32)

    def flip(values):
        return jnp.concatenate(
            [values.T, jnp.ones((pad, values.shape[0]), jnp.bfloat16)], axis=0)

    def fold(block, base, live):
        cos_b, sin_b = base_cos[pl.ds(base, 1), :], base_sin[pl.ds(base, 1), :]
        cos_n, sin_n = step_cos[:span, :], step_sin[:span, :]
        keys = turn(
            block[:, :head], cos_b * cos_n - sin_b * sin_n, sin_b * cos_n + cos_b * sin_n)
        values = flip(block[:, head:])
        for c in range(rows // chunk):
            at = pl.ds(c * chunk, chunk)
            top, mixed = attend(keys, values, c, None)
            top = jnp.where(live, top, -jnp.inf)
            old = tops[:, at]
            diff = top - old
            factor = jnp.exp2(-jnp.abs(diff) * power)
            rises = diff > 0.0
            tops[:, at] = jnp.maximum(old, top)
            total[:, at] = (
                total[:, at] * jnp.where(rises, factor, 1.0)
                + mixed * jnp.where(rises, 1.0, factor))

    peers(lambda d: ask_copy(d, d).wait_recv())
    bring = pltpu.make_async_copy(asks, asks_s, local_sem.at[1])
    asks[me] = request_ref[...]
    bring.start()
    bring.wait()

    def slot_for(d):
        def look(r, slot):
            block_id = asks_s[d, 0, r]
            hit = (block_id // per_device == me) & (r < asks_s[d, 0, requests])
            return jnp.where(hit, lax.rem(block_id, per_device), slot)
        return lax.fori_loop(0, requests, look, jnp.int32(0), unroll=min(requests, 8))

    def reply(first, last):
        def step(s, carry):
            d = lax.rem(me + s * STRIDE, n)
            stage[d] = store[slot_for(d)]
            rare_copy(me, d).start()
            return carry
        lax.fori_loop(first, last, step, 0)

    cuts = [1, 3, 5, WINDOW + 1, n]
    reply(cuts[0], cuts[1])
    recv[me] = store[slot_for(me)]

    for s in range(1, INNER):
        j = lax.rem(inner + s, INNER)
        one_copy(j, j).wait_recv()
    for k in range(pops):
        two_stage[k] = one_recv[lax.rem(pop_ref[k] // per_device, INNER), k]
    for k in range(pops):
        @pl.when(outer != k)
        def _():
            two_copy(outer, k).start()

        @pl.when(outer == k)
        def _():
            two_recv[k] = two_stage[k]

    def rare_fold(h):
        def look(r, found):
            hit = (asks_s[me, 0, r] // per_device == h) & (r < asks_s[me, 0, requests])
            return jnp.where(hit, r, found)
        r = lax.fori_loop(0, requests, look, jnp.int32(-1), unroll=min(requests, 8))
        fold(recv[h], jnp.maximum(r, 0) + 1 + pops, r >= 0)

    def arrivals(first, last):
        def step(s, carry):
            h = lax.rem(me + (n - s) * STRIDE, n)
            rare_copy(h, h).wait_recv()
            rare_fold(h)

            @pl.when(s + WINDOW < n)
            def _():
                reply(s + WINDOW, s + WINDOW + 1)
            return carry
        lax.fori_loop(first, last, step, 0)

    reply(cuts[1], cuts[2])

    own_keys = turn(own_ref[:, :head], own_cos, own_sin)
    own_values = flip(own_ref[:, head:])
    for c in range(rows // chunk):
        at = pl.ds(c * chunk, chunk)
        token = lax.rem(
            lax.broadcasted_iota(jnp.int32, (tokens, chunk), 1) + c * chunk, tokens)
        seen = token >= lax.broadcasted_iota(jnp.int32, (tokens, chunk), 0)
        top, total[:, at] = attend(own_keys, own_values, c, seen)
        tops[:, at] = top

    rare_fold(me)

    @pl.when(outer < pops)
    def _():
        def two_wait(s, carry):
            d = lax.rem(outer + s, outers)
            pltpu.make_async_remote_copy(
                src_ref=mid_stage, dst_ref=two_recv.at[d],
                send_sem=mid_send.at[d], recv_sem=two_sem.at[d],
                device_id={"store": d * INNER + inner}, device_id_type=MESH).wait_recv()
            return carry
        lax.fori_loop(1, outers, two_wait, 0)
        mine = lax.rem(outer, pops)
        mid_stage[...] = two_recv[pop_ref[mine] // (per_device * INNER)]

        def mid_start(s, carry):
            mid_copy(mine, lax.rem(outer + s, outers)).start()
            return carry
        lax.fori_loop(1, outers, mid_start, 0)
        three_stage[mine] = mid_stage[...]

    reply(cuts[2], cuts[3])
    arrivals(cuts[0], cuts[1])
    for k in range(pops):
        @pl.when(outer != k)
        def _():
            mid_copy(k, k).wait_recv()
    for s in range(1, INNER):
        three_copy(inner, lax.rem(inner + s, INNER)).start()
    for k in range(pops):
        popular[inner, k] = three_stage[k]
    arrivals(cuts[1], cuts[3])

    for s in range(1, INNER):
        j = lax.rem(inner + s, INNER)
        three_copy(j, j).wait_recv()

    def popular_fold(k, carry):
        block = jnp.concatenate([popular[j, k] for j in range(INNER)], axis=0)
        fold(block, k + 1, True)
        return carry
    lax.fori_loop(0, pops, popular_fold, 0)

    arrivals(cuts[3], cuts[4])

    for g in range(rows // tokens):
        at = pl.ds(g * tokens, tokens)
        out_ref[:, g * head:(g + 1) * head] = (
            total[:head, at] / total[head:head + 1, at]).T.astype(jnp.bfloat16)

    peers(lambda d: ask_copy(d, d).wait_send())
    peers(lambda d: rare_copy(d, d).wait_send())
    for s in range(1, INNER):
        j = lax.rem(inner + s, INNER)
        one_copy(j, j).wait_send()
        three_copy(j, j).wait_send()

    for k in range(pops):
        @pl.when(outer != k)
        def _():
            two_copy(k, k).wait_send()

    @pl.when(outer < pops)
    def _():
        def mid_done(s, carry):
            d = lax.rem(outer + s, outers)
            mid_copy(lax.rem(outer, pops), d).wait_send()
            return carry
        lax.fori_loop(1, outers, mid_done, 0)


def direct_body(queries, own_kv, store_kv, q_start, pop_ids, pop_pos, rare_ids, rare_count, rare_pos):
    n = lax.axis_size("store")
    tokens = queries.shape[0]
    head = own_kv.shape[1] // 2
    rows = tokens * (queries.shape[1] // head)
    per_device, span, width = store_kv.shape
    requests = rare_ids.shape[1]
    pops = pop_ids.shape[0]
    longest = max(span, tokens)
    lanes = -(-(requests + 1) // 128) * 128
    outers = n // INNER
    piece = span // INNER

    half = np.arange(head) % (head // 2)
    freq = 500000.0 ** (-(2.0 * half) / head)
    sign = np.where(np.arange(head) < head // 2, -1.0, 1.0)
    steps = np.arange(longest)[:, None] * freq[None, :]
    step_cos = np.cos(steps).astype(np.float32)
    step_sin = (np.sin(steps) * sign).astype(np.float32)
    base = jnp.concatenate([q_start, pop_pos[0], rare_pos[0]]).astype(jnp.float32)
    angles = base[:, None] * freq.astype(np.float32)[None, :]
    base_cos = jnp.cos(angles)
    base_sin = jnp.sin(angles) * sign.astype(np.float32)[None, :]
    table = jnp.concatenate([rare_ids[0], rare_count])
    table = jnp.pad(table, (0, lanes - requests - 1))

    vmem = pl.BlockSpec(memory_space=pltpu.VMEM)
    smem = pl.BlockSpec(memory_space=pltpu.SMEM)
    dma = pltpu.SemaphoreType.DMA
    bf16 = jnp.bfloat16
    chunk = min(rows, 512)
    return pl.pallas_call(
        functools.partial(direct_kernel, n, per_device, requests, pops, chunk, head ** -0.5 * np.log2(np.e).item()),
        out_shape=jax.ShapeDtypeStruct(queries.shape, bf16),
        in_specs=[smem, vmem, vmem, vmem, pl.BlockSpec(memory_space=pl.ANY)] + [vmem] * 4,
        out_specs=vmem,
        scratch_shapes=[
            pltpu.VMEM((per_device, span, width), bf16),
            pltpu.VMEM((n, 1, lanes), jnp.int32),
            pltpu.SMEM((n, 1, lanes), jnp.int32),
            pltpu.VMEM((n, span, width), bf16),
            pltpu.VMEM((n, span, width), bf16),
            pltpu.VMEM((rows, head), bf16),
            pltpu.VMEM((head + 16, rows), jnp.float32),
            pltpu.VMEM((1, rows), jnp.float32),
            pltpu.VMEM((INNER, pops, piece, width), bf16),
            pltpu.VMEM((INNER, pops, piece, width), bf16),
            pltpu.VMEM((pops, piece, width), bf16),
            pltpu.VMEM((outers, piece, width), bf16),
            pltpu.VMEM((piece, width), bf16),
            pltpu.VMEM((pops, piece, width), bf16),
            pltpu.VMEM((INNER, pops, piece, width), bf16),
            dma((2,)), dma((n,)), dma((n,)), dma((n,)), dma((n,)),
            dma((INNER,)), dma((INNER,)), dma((outers,)), dma((outers,)), dma((outers,)), dma((pops,)),
            dma((INNER,)), dma((INNER,)),
        ],
        compiler_params=pltpu.CompilerParams(
            collective_id=0, has_side_effects=True, vmem_limit_bytes=60 * 2**20),
    )(pop_ids, table.reshape(1, lanes), queries, own_kv, store_kv,
      base_cos, base_sin, step_cos, step_sin)


PLANES = 4
LANES = 4
PARTS = 2
STEPS = 4
COARSE = 128
PLACE = 64
LOWEST = -1e30
TINY = 1e-30


def plane_kernel(
    per_device, requests, pops, power,
    pop_ref, ids_ref, count_ref, rare_pos, pop_pos, start_ref,
    queries_hbm, own_hbm, store_hbm, trig_hbm, out_ref,
    store, queries_ref, own_ref, trig, row, asks, asks_s, info, rows_of, total, tops,
    stage, cand, part_out, part_in, log_out, log_in,
    zero_stage, zero_recv, one_stage, one_recv, two_stage, up_recv, merged, cross_recv, final, popular,
    local_sem, ask_send, ask_recv, query_send, query_sem, block_send, block_sem,
    part_send, part_sem, log_send, log_sem,
    pair_send, pair_sem, chain_send, chain_sem, three_send, three_sem,
):
    n = PLANES * LANES
    me = lax.axis_index("store")
    plane, lane = me // LANES, lax.rem(me, LANES)
    half = plane // 2
    near, across = plane ^ 1, plane ^ 3
    is_inner = (plane == 1) | (plane == 2)
    is_outer = jnp.logical_not(is_inner)
    far_inner, far_outer = 2 - half, 3 - 3 * half
    asker = (far_inner, far_outer, near, plane)
    head = trig.shape[1]
    longest = (trig.shape[0] - 2 * COARSE) // 2
    coarse_cos, coarse_sin = trig.at[pl.ds(0, COARSE)], trig.at[pl.ds(COARSE, COARSE)]
    step_cos = trig.at[pl.ds(2 * COARSE, longest)]
    step_sin = trig.at[pl.ds(2 * COARSE + longest, longest)]
    tokens = queries_ref.shape[0]
    rows = rows_of.shape[1]
    span = store.shape[1]
    piece = span // LANES
    part, step_rows = rows // PARTS, rows // STEPS
    pad = total.shape[1] - head

    def remote(src, dst, send, recv_at, target):
        return pltpu.make_async_remote_copy(
            src_ref=src, dst_ref=dst, send_sem=send, recv_sem=recv_at,
            device_id={"store": target}, device_id_type=MESH)

    def ask_copy(slot, target):
        return remote(row, asks.at[slot], ask_send.at[target], ask_recv.at[slot], target)

    def query_copy(number, src, dst, p, target_plane):
        at = pl.ds(p * step_rows, step_rows)
        return remote(
            rows_of.at[src, at], rows_of.at[dst, at], query_send.at[number * STEPS + p],
            query_sem.at[dst * STEPS + p], target_plane * LANES + lane)

    def own_to_near(p):
        return query_copy(0, 3, 2, p, near)

    def own_across(p):
        return query_copy(1, 3, 0, p, across)

    def near_across(p):
        return query_copy(2, 2, 1, p, across)

    def far_to_near(s, p):
        return query_copy(3 + s, s, s, p, near)

    def block_copy(i, d):
        at = i * LANES + d
        return remote(
            stage.at[at], cand.at[at], block_send.at[at], block_sem.at[at],
            plane * LANES + (lane ^ d))

    def part_copy(i, j, p, target_plane):
        return remote(
            part_out.at[i, p], part_in.at[j, p], part_send.at[i * PARTS + p],
            part_sem.at[j * PARTS + p], target_plane * LANES + lane)

    def log_copy(i, j, p, target_plane):
        return remote(
            log_out.at[i, p], log_in.at[j, p], log_send.at[i * PARTS + p],
            log_sem.at[j * PARTS + p], target_plane * LANES + lane)

    def zero_copy():
        return remote(zero_stage, zero_recv, pair_send.at[0], pair_sem.at[0], me ^ 1)

    def one_copy():
        return remote(one_stage, one_recv, pair_send.at[1], pair_sem.at[1], me ^ 2)

    def chain_copy(step, src, dst, target_plane):
        return remote(src, dst, chain_send.at[step], chain_sem.at[step], target_plane * LANES + lane)

    def up_copy():
        return chain_copy(0, two_stage, up_recv, near)

    def cross_copy():
        return chain_copy(1, merged, cross_recv, across)

    def down_copy():
        return chain_copy(2, final, final, near)

    def popular_at(t):
        begin = ((t & 1) * 2 + (t >> 1)) * piece
        return popular.at[:, pl.ds(pl.multiple_of(begin, piece), piece)]

    def three_copy():
        return remote(final, popular_at(lane), three_send.at[0], three_sem.at[0], me ^ 2)

    def four_copy(y):
        t = lane ^ (y * 2)
        return remote(popular_at(t), popular_at(t), three_send.at[1 + y], three_sem.at[1 + y], me ^ 1)

    def peers(act):
        def step(s, carry):
            act(lax.rem(me + s, n))
            return carry
        lax.fori_loop(1, n, step, 0)

    barrier = pltpu.get_barrier_semaphore()
    peers(lambda d: pl.semaphore_signal(
        barrier, inc=1, device_id={"store": d}, device_id_type=MESH))
    loads = [
        pltpu.make_async_copy(a, b, local_sem.at[2 + i])
        for i, (a, b) in enumerate(
            ((trig_hbm, trig), (queries_hbm, queries_ref), (own_hbm, own_ref), (store_hbm, store)))]
    for copy in loads:
        copy.start()

    spot = lax.broadcasted_iota(jnp.int32, row.shape, 1)
    wanted = jnp.full(row.shape, -1, jnp.int32)
    for r in range(requests):
        block_id = ids_ref[0, r]
        holder = jnp.where(r < count_ref[0], block_id // per_device, -1)
        wanted = jnp.where(spot == holder, lax.rem(block_id, per_device) + r * per_device, wanted)
        wanted = jnp.where(spot == PLACE + r, rare_pos[0, r], wanted)
    row[...] = wanted
    asks[me] = wanted

    def base_of(position):
        a, b = position // COARSE, lax.rem(position, COARSE)
        ca, sa = coarse_cos[pl.ds(a, 1), :], coarse_sin[pl.ds(a, 1), :]
        cb, sb = step_cos[pl.ds(b, 1), :], step_sin[pl.ds(b, 1), :]
        return ca * cb - sa * sb, sa * cb + ca * sb

    def table(position, count):
        cos_b, sin_b = base_of(position)
        cos_n, sin_n = step_cos[:count, :], step_sin[:count, :]
        return cos_b * cos_n - sin_b * sin_n, sin_b * cos_n + cos_b * sin_n

    def turn(x, cosine, sine):
        x = x.astype(jnp.float32)
        return (x * cosine + pltpu.roll(x, head // 2, 1) * sine).astype(jnp.bfloat16)

    def attend(i, keys, values, seen):
        scores = lax.dot_general(
            keys, rows_of[i], (((1,), (1,)), ((), ())),
            preferred_element_type=jnp.float32)
        if seen is not None:
            scores = jnp.where(seen, scores, -jnp.inf)
        top = jnp.max(scores, axis=0, keepdims=True)
        weights = jnp.exp2((scores - top) * power).astype(jnp.bfloat16)
        return top, jnp.dot(values, weights, preferred_element_type=jnp.float32)

    def flip(values):
        return jnp.concatenate(
            [values.T, jnp.ones((pad, values.shape[0]), jnp.bfloat16)], axis=0)

    def blend(i, at, top, mixed):
        old = tops[i, :, at]
        diff = top - old
        factor = jnp.exp2(-jnp.abs(diff) * power)
        rises = diff > 0.0
        tops[i, :, at] = jnp.maximum(old, top)
        total[i, :, at] = (
            total[i, :, at] * jnp.where(rises, factor, 1.0)
            + mixed * jnp.where(rises, 1.0, factor))

    def fold(i, block, position):
        keys = turn(block[:, :head], *table(jnp.maximum(position, 0), span))
        top, mixed = attend(i, keys, flip(block[:, head:]), None)
        blend(i, pl.ds(0, rows), jnp.where(position >= 0, top, -jnp.inf), mixed)

    core, y = lane & 1, lane >> 1

    def my_part(k, begin, size):
        return store[lax.rem(pop_ref[k], per_device), pl.ds(pl.multiple_of(begin, piece), size), :]

    pl.semaphore_wait(barrier, n - 1)
    peers(lambda d: ask_copy(me, d).start())
    loads[3].wait()
    for k in range(pops):
        zero_stage[k] = my_part(k, (1 - core) * 2 * piece, 2 * piece)
    zero_copy().start()
    for copy in loads[:2]:
        copy.wait()
    own_cos, own_sin = table(start_ref[0], tokens)
    for g in range(rows // tokens):
        rows_of[3, g * tokens:(g + 1) * tokens, :] = turn(
            queries_ref[:, g * head:(g + 1) * head], own_cos, own_sin)

    for p in range(STEPS):
        @pl.when(is_inner)
        def _():
            own_across(p).start()

        @pl.when(is_outer | (p < STEPS * 3 // 4))
        def _():
            own_to_near(p).start()


    def holder_lane(k):
        return lax.rem(pop_ref[k] // per_device, LANES)

    zero_copy().wait_recv()
    for k in range(pops):
        mine = (holder_lane(k) & 1) == core
        for to, t in ((one_stage, 1 - y), (two_stage, y)):
            other = zero_recv[k, pl.ds(pl.multiple_of(t * piece, piece), piece), :]
            to[k] = jnp.where(mine, my_part(k, (core * 2 + t) * piece, piece), other)
    one_copy().start()

    peers(lambda d: ask_copy(d, d).wait_recv())
    bring = pltpu.make_async_copy(asks, asks_s, local_sem.at[1])
    bring.start()
    bring.wait()

    def block_for(target):
        return store[lax.rem(jnp.maximum(asks_s[target, 0, me], 0), per_device)]

    def asker_at(i):
        return jnp.where(i == 0, asker[0], jnp.where(i == 1, asker[1], jnp.where(i == 2, asker[2], asker[3])))

    def send_blocks(i):
        for d in (2, 3, 1):
            stage[i * LANES + d] = block_for(asker_at(i) * LANES + (lane ^ d))
            block_copy(i, d).start()
        cand[i * LANES] = block_for(asker_at(i) * LANES + lane)

    order = [jnp.where(is_inner, a, b) for a, b in ((2, 0), (0, 1), (1, 2))] + [3]
    for i in order[:3]:
        send_blocks(i)

    def query_wait(s, p):
        at = pl.ds(p * step_rows, step_rows)
        remote(
            rows_of.at[s, at], rows_of.at[s, at], query_send.at[0],
            query_sem.at[s * STEPS + p], me ^ 1).wait_recv()

    @pl.when(is_inner)
    def _():
        for p in range(STEPS):
            query_wait(2, p)
            near_across(p).start()
            query_wait(0, p)
            far_to_near(0, p).start()

    one_copy().wait_recv()
    for k in range(pops):
        two_stage[k] = jnp.where((holder_lane(k) >> 1) == y, two_stage[k], one_recv[k])

    @pl.when(is_outer)
    def _():
        up_copy().start()

    for i in range(4):
        for d in range(LANES):
            requester = asker[i] * LANES + lane
            value = asks_s[requester, 0, plane * LANES + (lane ^ d)]
            position = asks_s[requester, 0, PLACE + jnp.maximum(value, 0) // per_device]
            info[i * LANES + d] = jnp.where(value >= 0, position, -1)

    loads[2].wait()
    token = lax.rem(lax.broadcasted_iota(jnp.int32, (tokens, rows), 1), tokens)
    seen = token >= lax.broadcasted_iota(jnp.int32, (tokens, rows), 0)
    top, mixed = attend(
        3, turn(own_ref[:, :head], own_cos, own_sin), flip(own_ref[:, head:]), seen)
    total[3] = mixed
    tops[3] = top
    for i in range(3):
        total[i] = jnp.zeros(total.shape[1:], jnp.float32)
        tops[i] = jnp.full(tops.shape[1:], LOWEST, jnp.float32)

    def holder_plane(k):
        return pop_ref[k] // (per_device * LANES)

    @pl.when(is_inner)
    def _():
        for p in range(STEPS // 2):
            query_wait(1, p)
            far_to_near(1, p).start()
        up_copy().wait_recv()
        for k in range(pops):
            merged[k] = jnp.where(holder_plane(k) == plane, two_stage[k], up_recv[k])
        cross_copy().start()
        for p in range(STEPS // 2, STEPS):
            query_wait(1, p)
            far_to_near(1, p).start()
        for p in range(STEPS * 3 // 4, STEPS):
            own_to_near(p).start()

    @pl.when(is_outer)
    def _():
        for p in range(STEPS):
            query_wait(0, p)

    def phase(i, first=0, last=LANES):
        def step(d, carry):
            at = i * LANES + d

            @pl.when(d > 0)
            def _():
                remote(
                    stage.at[0], cand.at[at], block_send.at[0], block_sem.at[at], me ^ 1).wait_recv()
            fold(i, cand[at], info[at])
            return carry
        lax.fori_loop(first, last, step, 0)

    def send_piece(i, j, p, target_plane):
        at = pl.ds(p * part, part)
        weight = jnp.maximum(total[i, head:head + 1, at], TINY)
        log_out[i, p] = tops[i, :, at] + jnp.log2(weight) * (1.0 / power)
        part_out[i, p] = (total[i, :head, at] * (1.0 / weight)).astype(jnp.bfloat16)
        log_copy(i, j, p, target_plane).start()
        part_copy(i, j, p, target_plane).start()

    def take_piece(i, j, p):
        log_copy(0, j, p, near).wait_recv()
        part_copy(0, j, p, near).wait_recv()
        ones = jnp.ones((pad, part), jnp.float32)
        blend(
            i, pl.ds(p * part, part), log_in[j, p],
            jnp.concatenate([part_in[j, p].astype(jnp.float32), ones], axis=0))

    def send_part(i, j, target_plane):
        for p in range(PARTS):
            send_piece(i, j, p, target_plane)

    def pass_part(i, target_plane):
        for p in range(PARTS):
            take_piece(i, i, p)
            send_piece(i, 3, p, target_plane)

    def spread():
        three_copy().start()
        popular_at(lane)[...] = final[...]
        four_copy(0).start()
        send_blocks(3)

    phase(order[0])

    @pl.when(is_outer)
    def _():
        send_part(0, 0, near)
        for p in range(STEPS):
            query_wait(1, p)

    @pl.when(is_inner)
    def _():
        cross_copy().wait_recv()
        for k in range(pops):
            final[k] = jnp.where(holder_plane(k) // 2 == half, merged[k], cross_recv[k])
        down_copy().start()
        spread()
        send_part(2, 2, near)

    phase(order[1])

    @pl.when(is_outer)
    def _():
        send_part(1, 1, near)
        down_copy().wait_recv()
        spread()
        for p in range(STEPS):
            query_wait(2, p)

    @pl.when(is_inner)
    def _():
        pass_part(0, far_inner)

    phase(order[2])

    @pl.when(is_outer)
    def _():
        send_part(2, 2, near)

    @pl.when(is_inner)
    def _():
        pass_part(1, far_outer)

    phase(3, 0, 2)
    remote(final, popular_at(lane ^ 2), three_send.at[0], three_sem.at[0], me ^ 1).wait_recv()
    four_copy(1).start()
    for t in (0, 1):
        remote(
            final, popular_at(lane ^ (1 + 2 * t)), three_send.at[0], three_sem.at[1 + t], me ^ 1).wait_recv()

    def popular_fold(k, carry):
        fold(3, popular[k], pop_pos[0, k])
        return carry
    lax.fori_loop(0, pops, popular_fold, 0)

    phase(3, 2, 3)
    for p in range(PARTS):
        take_piece(3, 2, p)
    phase(3, 3, 4)
    for p in range(PARTS):
        take_piece(3, 3, p)

    for g in range(rows // tokens):
        at = pl.ds(g * tokens, tokens)
        out_ref[:, g * head:(g + 1) * head] = (
            total[3, :head, at] * (1.0 / total[3, head:head + 1, at])).astype(jnp.bfloat16).T

    peers(lambda d: ask_copy(d, d).wait_send())
    for p in range(STEPS):
        own_to_near(p).wait_send()

        @pl.when(is_inner)
        def _():
            own_across(p).wait_send()
            near_across(p).wait_send()
            far_to_near(0, p).wait_send()
            far_to_near(1, p).wait_send()
    for i in range(4):
        for d in range(1, LANES):
            block_copy(i, d).wait_send()
    for copy in (zero_copy(), one_copy(), three_copy(), four_copy(0), four_copy(1)):
        copy.wait_send()
    for i in range(3):
        for p in range(PARTS):
            log_copy(i, i, p, near).wait_send()
            part_copy(i, i, p, near).wait_send()

    @pl.when(is_outer)
    def _():
        up_copy().wait_send()

    @pl.when(is_inner)
    def _():
        cross_copy().wait_send()
        down_copy().wait_send()


def plane_body(queries, own_kv, store_kv, q_start, pop_ids, pop_pos, rare_ids, rare_count, rare_pos):
    n = lax.axis_size("store")
    tokens = queries.shape[0]
    head = own_kv.shape[1] // 2
    rows = tokens * (queries.shape[1] // head)
    per_device, span, width = store_kv.shape
    requests = rare_ids.shape[1]
    pops = pop_ids.shape[0]
    longest = max(span, tokens, COARSE)
    piece = span // LANES

    half = np.arange(head) % (head // 2)
    freq = 500000.0 ** (-(2.0 * half) / head)
    sign = np.where(np.arange(head) < head // 2, -1.0, 1.0)

    def tables(positions):
        angles = positions[:, None] * freq[None, :]
        return np.cos(angles).astype(np.float32), (np.sin(angles) * sign).astype(np.float32)

    vmem = pl.BlockSpec(memory_space=pltpu.VMEM)
    smem = pl.BlockSpec(memory_space=pltpu.SMEM)
    dma = pltpu.SemaphoreType.DMA
    bf16, f32 = jnp.bfloat16, jnp.float32

    trig = np.concatenate([*tables(np.arange(COARSE) * float(COARSE)), *tables(np.arange(longest) * 1.0)])

    def blocks(count):
        return pltpu.VMEM((count, span, width), bf16)

    def pieces(*lead):
        return pltpu.VMEM((*lead, piece, width), bf16)

    return pl.pallas_call(
        functools.partial(plane_kernel, per_device, requests, pops, head ** -0.5 * np.log2(np.e).item()),
        out_shape=pltpu.VMEM(queries.shape, bf16),
        in_specs=[smem] * 6 + [pl.BlockSpec(memory_space=pl.ANY)] * 4,
        out_specs=vmem,
        scratch_shapes=[
            blocks(per_device),
            pltpu.VMEM(queries.shape, bf16), pltpu.VMEM(own_kv.shape, bf16), pltpu.VMEM(trig.shape, f32),
            pltpu.VMEM((1, 128), jnp.int32),
            pltpu.VMEM((n, 1, 128), jnp.int32),
            pltpu.SMEM((n, 1, 128), jnp.int32),
            pltpu.SMEM((4 * LANES,), jnp.int32),
            pltpu.VMEM((4, rows, head), bf16),
            pltpu.VMEM((4, head + 16, rows), f32),
            pltpu.VMEM((4, 1, rows), f32),
            blocks(4 * LANES), blocks(4 * LANES),
            pltpu.VMEM((3, PARTS, head, rows // PARTS), bf16),
            pltpu.VMEM((4, PARTS, head, rows // PARTS), bf16),
            pltpu.VMEM((3, PARTS, 1, rows // PARTS), f32), pltpu.VMEM((4, PARTS, 1, rows // PARTS), f32),
            pltpu.VMEM((pops, 2 * piece, width), bf16), pltpu.VMEM((pops, 2 * piece, width), bf16),
            pieces(pops), pieces(pops), pieces(pops), pieces(pops),
            pieces(pops), pieces(pops), pieces(pops), blocks(pops),
            dma((6,)), dma((n,)), dma((n,)), dma((5 * STEPS,)), dma((3 * STEPS,)),
            dma((4 * LANES,)), dma((4 * LANES,)),
            dma((3 * PARTS,)), dma((4 * PARTS,)), dma((3 * PARTS,)), dma((4 * PARTS,)),
            dma((2,)), dma((2,)), dma((3,)), dma((3,)), dma((3,)), dma((3,)),
        ],
        compiler_params=pltpu.CompilerParams(
            collective_id=1, has_side_effects=True, vmem_limit_bytes=60 * 2**20),
    )(pop_ids, rare_ids, rare_count, rare_pos, pop_pos, q_start, queries, own_kv, store_kv,
      trig)


def body(*args):
    requests, pops = args[6].shape[1], args[4].shape[0]
    if lax.axis_size("store") == PLANES * LANES and requests <= PLACE and pops == 4:
        return plane_body(*args)
    return direct_body(*args)


def solution(mesh):
    both = ("tenant", "store")
    in_specs = (
        P(both, None), P(both, None), P(both, None, None), P(both), P("tenant"),
        P(both, None), P(both, None), P(both), P(both, None),
    )
    return jax.shard_map(
        body, mesh=mesh, in_specs=in_specs, out_specs=P(both, None), check_vma=False)
```

```python
import functools

import jax
import jax.numpy as jnp
import numpy as np
from jax import lax
from jax.experimental import pallas as pl
from jax.experimental.pallas import tpu as pltpu
from jax.sharding import PartitionSpec as P

MESH = pl.DeviceIdType.MESH
INNER = 4
STRIDE = 5
WINDOW = 7


def direct_kernel(
    n, per_device, requests, pops, chunk, power,
    pop_ref, request_ref, queries_ref, own_ref, store_hbm,
    base_cos, base_sin, step_cos, step_sin, out_ref,
    store, asks, asks_s, stage, recv, query_rows, total, tops,
    one_stage, one_recv, two_stage, two_recv, mid_stage, three_stage, popular,
    local_sem, ask_send, ask_recv, rare_send, rare_recv,
    one_send, one_sem, two_send, two_sem, mid_send, mid_sem, three_send, three_sem,
):
    me = lax.axis_index("store")
    inner, outer = lax.rem(me, INNER), me // INNER
    outers = n // INNER
    head = base_cos.shape[1]
    tokens = queries_ref.shape[0]
    rows = query_rows.shape[0]
    span = stage.shape[1]
    piece = span // INNER

    def ask_copy(slot, target):
        return pltpu.make_async_remote_copy(
            src_ref=request_ref, dst_ref=asks.at[slot],
            send_sem=ask_send.at[target], recv_sem=ask_recv.at[slot],
            device_id={"store": target}, device_id_type=MESH)

    def rare_copy(slot, target):
        return pltpu.make_async_remote_copy(
            src_ref=stage.at[target], dst_ref=recv.at[slot],
            send_sem=rare_send.at[target], recv_sem=rare_recv.at[slot],
            device_id={"store": target}, device_id_type=MESH)

    def one_copy(slot, target):
        return pltpu.make_async_remote_copy(
            src_ref=one_stage.at[target], dst_ref=one_recv.at[slot],
            send_sem=one_send.at[target], recv_sem=one_sem.at[slot],
            device_id={"store": outer * INNER + target}, device_id_type=MESH)

    def two_copy(slot, target):
        return pltpu.make_async_remote_copy(
            src_ref=two_stage.at[target], dst_ref=two_recv.at[slot],
            send_sem=two_send.at[target], recv_sem=two_sem.at[slot],
            device_id={"store": target * INNER + inner}, device_id_type=MESH)

    def mid_copy(slot, target):
        return pltpu.make_async_remote_copy(
            src_ref=mid_stage, dst_ref=three_stage.at[slot],
            send_sem=mid_send.at[target], recv_sem=mid_sem.at[slot],
            device_id={"store": target * INNER + inner}, device_id_type=MESH)

    def three_copy(slot, target):
        return pltpu.make_async_remote_copy(
            src_ref=three_stage, dst_ref=popular.at[slot],
            send_sem=three_send.at[target], recv_sem=three_sem.at[slot],
            device_id={"store": outer * INNER + target}, device_id_type=MESH)

    def peers(act):
        def step(s, carry):
            act(lax.rem(me + s, n))
            return carry
        lax.fori_loop(1, n, step, 0)

    load = pltpu.make_async_copy(store_hbm, store, local_sem.at[0])
    load.start()
    barrier = pltpu.get_barrier_semaphore()
    peers(lambda d: pl.semaphore_signal(
        barrier, inc=1, device_id={"store": d}, device_id_type=MESH))
    pl.semaphore_wait(barrier, n - 1)
    peers(lambda d: ask_copy(me, d).start())
    load.wait()

    for s in range(INNER):
        j = lax.rem(inner + s, INNER)
        begin = pl.multiple_of(j * piece, piece)
        for k in range(pops):
            part = store[lax.rem(pop_ref[k], per_device), pl.ds(begin, piece), :]
            if s == 0:
                one_recv[inner, k] = part
            else:
                one_stage[j, k] = part
        if s:
            one_copy(inner, j).start()

    cos0, sin0 = base_cos[0:1, :], base_sin[0:1, :]
    cos_n, sin_n = step_cos[:tokens, :], step_sin[:tokens, :]
    own_cos = cos0 * cos_n - sin0 * sin_n
    own_sin = sin0 * cos_n + cos0 * sin_n

    def turn(x, cosine, sine):
        x = x.astype(jnp.float32)
        return (x * cosine + pltpu.roll(x, head // 2, 1) * sine).astype(jnp.bfloat16)

    for g in range(rows // tokens):
        query_rows[g * tokens:(g + 1) * tokens, :] = turn(
            queries_ref[:, g * head:(g + 1) * head], own_cos, own_sin)

    pad = total.shape[0] - head

    def attend(keys, values, c, seen):
        at = pl.ds(c * chunk, chunk)
        scores = lax.dot_general(
            keys, query_rows[at, :], (((1,), (1,)), ((), ())),
            preferred_element_type=jnp.float32)
        if seen is not None:
            scores = jnp.where(seen, scores, -jnp.inf)
        top = jnp.max(scores, axis=0, keepdims=True)
        weights = jnp.exp2((scores - top) * power).astype(jnp.bfloat16)
        return top, jnp.dot(values, weights, preferred_element_type=jnp.float32)

    def flip(values):
        return jnp.concatenate(
            [values.T, jnp.ones((pad, values.shape[0]), jnp.bfloat16)], axis=0)

    def fold(block, base, live):
        cos_b, sin_b = base_cos[pl.ds(base, 1), :], base_sin[pl.ds(base, 1), :]
        cos_n, sin_n = step_cos[:span, :], step_sin[:span, :]
        keys = turn(
            block[:, :head], cos_b * cos_n - sin_b * sin_n, sin_b * cos_n + cos_b * sin_n)
        values = flip(block[:, head:])
        for c in range(rows // chunk):
            at = pl.ds(c * chunk, chunk)
            top, mixed = attend(keys, values, c, None)
            top = jnp.where(live, top, -jnp.inf)
            old = tops[:, at]
            diff = top - old
            factor = jnp.exp2(-jnp.abs(diff) * power)
            rises = diff > 0.0
            tops[:, at] = jnp.maximum(old, top)
            total[:, at] = (
                total[:, at] * jnp.where(rises, factor, 1.0)
                + mixed * jnp.where(rises, 1.0, factor))

    peers(lambda d: ask_copy(d, d).wait_recv())
    bring = pltpu.make_async_copy(asks, asks_s, local_sem.at[1])
    asks[me] = request_ref[...]
    bring.start()
    bring.wait()

    def slot_for(d):
        def look(r, slot):
            block_id = asks_s[d, 0, r]
            hit = (block_id // per_device == me) & (r < asks_s[d, 0, requests])
            return jnp.where(hit, lax.rem(block_id, per_device), slot)
        return lax.fori_loop(0, requests, look, jnp.int32(0), unroll=min(requests, 8))

    def reply(first, last):
        def step(s, carry):
            d = lax.rem(me + s * STRIDE, n)
            stage[d] = store[slot_for(d)]
            rare_copy(me, d).start()
            return carry
        lax.fori_loop(first, last, step, 0)

    cuts = [1, 3, 5, WINDOW + 1, n]
    reply(cuts[0], cuts[1])
    recv[me] = store[slot_for(me)]

    for s in range(1, INNER):
        j = lax.rem(inner + s, INNER)
        one_copy(j, j).wait_recv()
    for k in range(pops):
        two_stage[k] = one_recv[lax.rem(pop_ref[k] // per_device, INNER), k]
    for k in range(pops):
        @pl.when(outer != k)
        def _():
            two_copy(outer, k).start()

        @pl.when(outer == k)
        def _():
            two_recv[k] = two_stage[k]

    def rare_fold(h):
        def look(r, found):
            hit = (asks_s[me, 0, r] // per_device == h) & (r < asks_s[me, 0, requests])
            return jnp.where(hit, r, found)
        r = lax.fori_loop(0, requests, look, jnp.int32(-1), unroll=min(requests, 8))
        fold(recv[h], jnp.maximum(r, 0) + 1 + pops, r >= 0)

    def arrivals(first, last):
        def step(s, carry):
            h = lax.rem(me + (n - s) * STRIDE, n)
            rare_copy(h, h).wait_recv()
            rare_fold(h)

            @pl.when(s + WINDOW < n)
            def _():
                reply(s + WINDOW, s + WINDOW + 1)
            return carry
        lax.fori_loop(first, last, step, 0)

    reply(cuts[1], cuts[2])

    own_keys = turn(own_ref[:, :head], own_cos, own_sin)
    own_values = flip(own_ref[:, head:])
    for c in range(rows // chunk):
        at = pl.ds(c * chunk, chunk)
        token = lax.rem(
            lax.broadcasted_iota(jnp.int32, (tokens, chunk), 1) + c * chunk, tokens)
        seen = token >= lax.broadcasted_iota(jnp.int32, (tokens, chunk), 0)
        top, total[:, at] = attend(own_keys, own_values, c, seen)
        tops[:, at] = top

    rare_fold(me)

    @pl.when(outer < pops)
    def _():
        def two_wait(s, carry):
            d = lax.rem(outer + s, outers)
            pltpu.make_async_remote_copy(
                src_ref=mid_stage, dst_ref=two_recv.at[d],
                send_sem=mid_send.at[d], recv_sem=two_sem.at[d],
                device_id={"store": d * INNER + inner}, device_id_type=MESH).wait_recv()
            return carry
        lax.fori_loop(1, outers, two_wait, 0)
        mine = lax.rem(outer, pops)
        mid_stage[...] = two_recv[pop_ref[mine] // (per_device * INNER)]

        def mid_start(s, carry):
            mid_copy(mine, lax.rem(outer + s, outers)).start()
            return carry
        lax.fori_loop(1, outers, mid_start, 0)
        three_stage[mine] = mid_stage[...]

    reply(cuts[2], cuts[3])
    arrivals(cuts[0], cuts[1])
    for k in range(pops):
        @pl.when(outer != k)
        def _():
            mid_copy(k, k).wait_recv()
    for s in range(1, INNER):
        three_copy(inner, lax.rem(inner + s, INNER)).start()
    for k in range(pops):
        popular[inner, k] = three_stage[k]
    arrivals(cuts[1], cuts[3])

    for s in range(1, INNER):
        j = lax.rem(inner + s, INNER)
        three_copy(j, j).wait_recv()

    def popular_fold(k, carry):
        block = jnp.concatenate([popular[j, k] for j in range(INNER)], axis=0)
        fold(block, k + 1, True)
        return carry
    lax.fori_loop(0, pops, popular_fold, 0)

    arrivals(cuts[3], cuts[4])

    for g in range(rows // tokens):
        at = pl.ds(g * tokens, tokens)
        out_ref[:, g * head:(g + 1) * head] = (
            total[:head, at] / total[head:head + 1, at]).T.astype(jnp.bfloat16)

    peers(lambda d: ask_copy(d, d).wait_send())
    peers(lambda d: rare_copy(d, d).wait_send())
    for s in range(1, INNER):
        j = lax.rem(inner + s, INNER)
        one_copy(j, j).wait_send()
        three_copy(j, j).wait_send()

    for k in range(pops):
        @pl.when(outer != k)
        def _():
            two_copy(k, k).wait_send()

    @pl.when(outer < pops)
    def _():
        def mid_done(s, carry):
            d = lax.rem(outer + s, outers)
            mid_copy(lax.rem(outer, pops), d).wait_send()
            return carry
        lax.fori_loop(1, outers, mid_done, 0)


def direct_body(queries, own_kv, store_kv, q_start, pop_ids, pop_pos, rare_ids, rare_count, rare_pos):
    n = lax.axis_size("store")
    tokens = queries.shape[0]
    head = own_kv.shape[1] // 2
    rows = tokens * (queries.shape[1] // head)
    per_device, span, width = store_kv.shape
    requests = rare_ids.shape[1]
    pops = pop_ids.shape[0]
    longest = max(span, tokens)
    lanes = -(-(requests + 1) // 128) * 128
    outers = n // INNER
    piece = span // INNER

    half = np.arange(head) % (head // 2)
    freq = 500000.0 ** (-(2.0 * half) / head)
    sign = np.where(np.arange(head) < head // 2, -1.0, 1.0)
    steps = np.arange(longest)[:, None] * freq[None, :]
    step_cos = np.cos(steps).astype(np.float32)
    step_sin = (np.sin(steps) * sign).astype(np.float32)
    base = jnp.concatenate([q_start, pop_pos[0], rare_pos[0]]).astype(jnp.float32)
    angles = base[:, None] * freq.astype(np.float32)[None, :]
    base_cos = jnp.cos(angles)
    base_sin = jnp.sin(angles) * sign.astype(np.float32)[None, :]
    table = jnp.concatenate([rare_ids[0], rare_count])
    table = jnp.pad(table, (0, lanes - requests - 1))

    vmem = pl.BlockSpec(memory_space=pltpu.VMEM)
    smem = pl.BlockSpec(memory_space=pltpu.SMEM)
    dma = pltpu.SemaphoreType.DMA
    bf16 = jnp.bfloat16
    chunk = min(rows, 512)
    return pl.pallas_call(
        functools.partial(direct_kernel, n, per_device, requests, pops, chunk, head ** -0.5 * np.log2(np.e).item()),
        out_shape=jax.ShapeDtypeStruct(queries.shape, bf16),
        in_specs=[smem, vmem, vmem, vmem, pl.BlockSpec(memory_space=pl.ANY)] + [vmem] * 4,
        out_specs=vmem,
        scratch_shapes=[
            pltpu.VMEM((per_device, span, width), bf16),
            pltpu.VMEM((n, 1, lanes), jnp.int32),
            pltpu.SMEM((n, 1, lanes), jnp.int32),
            pltpu.VMEM((n, span, width), bf16),
            pltpu.VMEM((n, span, width), bf16),
            pltpu.VMEM((rows, head), bf16),
            pltpu.VMEM((head + 16, rows), jnp.float32),
            pltpu.VMEM((1, rows), jnp.float32),
            pltpu.VMEM((INNER, pops, piece, width), bf16),
            pltpu.VMEM((INNER, pops, piece, width), bf16),
            pltpu.VMEM((pops, piece, width), bf16),
            pltpu.VMEM((outers, piece, width), bf16),
            pltpu.VMEM((piece, width), bf16),
            pltpu.VMEM((pops, piece, width), bf16),
            pltpu.VMEM((INNER, pops, piece, width), bf16),
            dma((2,)), dma((n,)), dma((n,)), dma((n,)), dma((n,)),
            dma((INNER,)), dma((INNER,)), dma((outers,)), dma((outers,)), dma((outers,)), dma((pops,)),
            dma((INNER,)), dma((INNER,)),
        ],
        compiler_params=pltpu.CompilerParams(
            collective_id=0, has_side_effects=True, vmem_limit_bytes=60 * 2**20),
    )(pop_ids, table.reshape(1, lanes), queries, own_kv, store_kv,
      base_cos, base_sin, step_cos, step_sin)


PLANES = 4
LANES = 4
PARTS = 2
STEPS = 4
COARSE = 128
PLACE = 64
LOWEST = -1e30
TINY = 1e-30


def plane_kernel(
    per_device, requests, pops, power,
    pop_ref, ids_ref, count_ref, rare_pos, pop_pos, start_ref,
    queries_hbm, own_hbm, store_hbm, trig_hbm, out_ref,
    store, queries_ref, own_ref, trig, row, asks, asks_s, info, rows_of, total, tops,
    stage, cand, part_out, part_in, log_out, log_in,
    zero_stage, zero_recv, one_stage, one_recv, two_stage, up_recv, merged, cross_recv, final, popular,
    local_sem, ask_send, ask_recv, query_send, query_sem, block_send, block_sem,
    part_send, part_sem, log_send, log_sem,
    pair_send, pair_sem, chain_send, chain_sem, three_send, three_sem,
):
    n = PLANES * LANES
    me = lax.axis_index("store")
    plane, lane = me // LANES, lax.rem(me, LANES)
    half = plane // 2
    near, across = plane ^ 1, plane ^ 3
    is_inner = (plane == 1) | (plane == 2)
    is_outer = jnp.logical_not(is_inner)
    far_inner, far_outer = 2 - half, 3 - 3 * half
    asker = (far_inner, far_outer, near, plane)
    head = trig.shape[1]
    longest = (trig.shape[0] - 2 * COARSE) // 2
    coarse_cos, coarse_sin = trig.at[pl.ds(0, COARSE)], trig.at[pl.ds(COARSE, COARSE)]
    step_cos = trig.at[pl.ds(2 * COARSE, longest)]
    step_sin = trig.at[pl.ds(2 * COARSE + longest, longest)]
    tokens = queries_ref.shape[0]
    rows = rows_of.shape[1]
    span = store.shape[1]
    piece = span // LANES
    part, step_rows = rows // PARTS, rows // STEPS
    pad = total.shape[1] - head

    def remote(src, dst, send, recv_at, target):
        return pltpu.make_async_remote_copy(
            src_ref=src, dst_ref=dst, send_sem=send, recv_sem=recv_at,
            device_id={"store": target}, device_id_type=MESH)

    def ask_copy(slot, target):
        return remote(row, asks.at[slot], ask_send.at[target], ask_recv.at[slot], target)

    def query_copy(number, src, dst, p, target_plane):
        at = pl.ds(p * step_rows, step_rows)
        return remote(
            rows_of.at[src, at], rows_of.at[dst, at], query_send.at[number * STEPS + p],
            query_sem.at[dst * STEPS + p], target_plane * LANES + lane)

    def own_to_near(p):
        return query_copy(0, 3, 2, p, near)

    def own_across(p):
        return query_copy(1, 3, 0, p, across)

    def near_across(p):
        return query_copy(2, 2, 1, p, across)

    def far_to_near(s, p):
        return query_copy(3 + s, s, s, p, near)

    def block_copy(i, d):
        at = i * LANES + d
        return remote(
            stage.at[at], cand.at[at], block_send.at[at], block_sem.at[at],
            plane * LANES + (lane ^ d))

    def part_copy(i, j, p, target_plane):
        return remote(
            part_out.at[i, p], part_in.at[j, p], part_send.at[i * PARTS + p],
            part_sem.at[j * PARTS + p], target_plane * LANES + lane)

    def log_copy(i, j, p, target_plane):
        return remote(
            log_out.at[i, p], log_in.at[j, p], log_send.at[i * PARTS + p],
            log_sem.at[j * PARTS + p], target_plane * LANES + lane)

    def zero_copy():
        return remote(zero_stage, zero_recv, pair_send.at[0], pair_sem.at[0], me ^ 1)

    def one_copy():
        return remote(one_stage, one_recv, pair_send.at[1], pair_sem.at[1], me ^ 2)

    def chain_copy(step, src, dst, target_plane):
        return remote(src, dst, chain_send.at[step], chain_sem.at[step], target_plane * LANES + lane)

    def up_copy():
        return chain_copy(0, two_stage, up_recv, near)

    def cross_copy():
        return chain_copy(1, merged, cross_recv, across)

    def down_copy():
        return chain_copy(2, final, final, near)

    def popular_at(t):
        begin = ((t & 1) * 2 + (t >> 1)) * piece
        return popular.at[:, pl.ds(pl.multiple_of(begin, piece), piece)]

    def three_copy():
        return remote(final, popular_at(lane), three_send.at[0], three_sem.at[0], me ^ 2)

    def four_copy(y):
        t = lane ^ (y * 2)
        return remote(popular_at(t), popular_at(t), three_send.at[1 + y], three_sem.at[1 + y], me ^ 1)

    def peers(act):
        def step(s, carry):
            act(lax.rem(me + s, n))
            return carry
        lax.fori_loop(1, n, step, 0)

    barrier = pltpu.get_barrier_semaphore()
    peers(lambda d: pl.semaphore_signal(
        barrier, inc=1, device_id={"store": d}, device_id_type=MESH))
    loads = [
        pltpu.make_async_copy(a, b, local_sem.at[2 + i])
        for i, (a, b) in enumerate(
            ((trig_hbm, trig), (queries_hbm, queries_ref), (own_hbm, own_ref), (store_hbm, store)))]
    for copy in loads:
        copy.start()

    spot = lax.broadcasted_iota(jnp.int32, row.shape, 1)
    wanted = jnp.full(row.shape, -1, jnp.int32)
    for r in range(requests):
        block_id = ids_ref[0, r]
        holder = jnp.where(r < count_ref[0], block_id // per_device, -1)
        wanted = jnp.where(spot == holder, lax.rem(block_id, per_device) + r * per_device, wanted)
        wanted = jnp.where(spot == PLACE + r, rare_pos[0, r], wanted)
    row[...] = wanted
    asks[me] = wanted

    def base_of(position):
        a, b = position // COARSE, lax.rem(position, COARSE)
        ca, sa = coarse_cos[pl.ds(a, 1), :], coarse_sin[pl.ds(a, 1), :]
        cb, sb = step_cos[pl.ds(b, 1), :], step_sin[pl.ds(b, 1), :]
        return ca * cb - sa * sb, sa * cb + ca * sb

    def table(position, count):
        cos_b, sin_b = base_of(position)
        cos_n, sin_n = step_cos[:count, :], step_sin[:count, :]
        return cos_b * cos_n - sin_b * sin_n, sin_b * cos_n + cos_b * sin_n

    def turn(x, cosine, sine):
        x = x.astype(jnp.float32)
        return (x * cosine + pltpu.roll(x, head // 2, 1) * sine).astype(jnp.bfloat16)

    def attend(i, keys, values, seen):
        scores = lax.dot_general(
            keys, rows_of[i], (((1,), (1,)), ((), ())),
            preferred_element_type=jnp.float32)
        if seen is not None:
            scores = jnp.where(seen, scores, -jnp.inf)
        top = jnp.max(scores, axis=0, keepdims=True)
        weights = jnp.exp2((scores - top) * power).astype(jnp.bfloat16)
        return top, jnp.dot(values, weights, preferred_element_type=jnp.float32)

    def flip(values):
        return jnp.concatenate(
            [values.T, jnp.ones((pad, values.shape[0]), jnp.bfloat16)], axis=0)

    def blend(i, at, top, mixed):
        old = tops[i, :, at]
        diff = top - old
        factor = jnp.exp2(-jnp.abs(diff) * power)
        rises = diff > 0.0
        tops[i, :, at] = jnp.maximum(old, top)
        total[i, :, at] = (
            total[i, :, at] * jnp.where(rises, factor, 1.0)
            + mixed * jnp.where(rises, 1.0, factor))

    def fold(i, block, position):
        keys = turn(block[:, :head], *table(jnp.maximum(position, 0), span))
        top, mixed = attend(i, keys, flip(block[:, head:]), None)
        blend(i, pl.ds(0, rows), jnp.where(position >= 0, top, -jnp.inf), mixed)

    core, y = lane & 1, lane >> 1

    def my_part(k, begin, size):
        return store[lax.rem(pop_ref[k], per_device), pl.ds(pl.multiple_of(begin, piece), size), :]

    pl.semaphore_wait(barrier, n - 1)
    peers(lambda d: ask_copy(me, d).start())
    loads[3].wait()
    for k in range(pops):
        zero_stage[k] = my_part(k, (1 - core) * 2 * piece, 2 * piece)
    zero_copy().start()
    for copy in loads[:2]:
        copy.wait()
    own_cos, own_sin = table(start_ref[0], tokens)
    for g in range(rows // tokens):
        rows_of[3, g * tokens:(g + 1) * tokens, :] = turn(
            queries_ref[:, g * head:(g + 1) * head], own_cos, own_sin)

    for p in range(STEPS):
        @pl.when(is_inner)
        def _():
            own_across(p).start()

        @pl.when(is_outer | (p < STEPS * 3 // 4))
        def _():
            own_to_near(p).start()


    def holder_lane(k):
        return lax.rem(pop_ref[k] // per_device, LANES)

    zero_copy().wait_recv()
    for k in range(pops):
        mine = (holder_lane(k) & 1) == core
        for to, t in ((one_stage, 1 - y), (two_stage, y)):
            other = zero_recv[k, pl.ds(pl.multiple_of(t * piece, piece), piece), :]
            to[k] = jnp.where(mine, my_part(k, (core * 2 + t) * piece, piece), other)
    one_copy().start()

    peers(lambda d: ask_copy(d, d).wait_recv())
    bring = pltpu.make_async_copy(asks, asks_s, local_sem.at[1])
    bring.start()
    bring.wait()

    def block_for(target):
        return store[lax.rem(jnp.maximum(asks_s[target, 0, me], 0), per_device)]

    def asker_at(i):
        return jnp.where(i == 0, asker[0], jnp.where(i == 1, asker[1], jnp.where(i == 2, asker[2], asker[3])))

    def send_blocks(i):
        for d in (2, 3, 1):
            stage[i * LANES + d] = block_for(asker_at(i) * LANES + (lane ^ d))
            block_copy(i, d).start()
        cand[i * LANES] = block_for(asker_at(i) * LANES + lane)

    order = [jnp.where(is_inner, a, b) for a, b in ((2, 0), (0, 1), (1, 2))] + [3]
    for i in order[:3]:
        send_blocks(i)

    def query_wait(s, p):
        at = pl.ds(p * step_rows, step_rows)
        remote(
            rows_of.at[s, at], rows_of.at[s, at], query_send.at[0],
            query_sem.at[s * STEPS + p], me ^ 1).wait_recv()

    @pl.when(is_inner)
    def _():
        for p in range(STEPS):
            query_wait(2, p)
            near_across(p).start()
            query_wait(0, p)
            far_to_near(0, p).start()

    one_copy().wait_recv()
    for k in range(pops):
        two_stage[k] = jnp.where((holder_lane(k) >> 1) == y, two_stage[k], one_recv[k])

    @pl.when(is_outer)
    def _():
        up_copy().start()

    for i in range(4):
        for d in range(LANES):
            requester = asker[i] * LANES + lane
            value = asks_s[requester, 0, plane * LANES + (lane ^ d)]
            position = asks_s[requester, 0, PLACE + jnp.maximum(value, 0) // per_device]
            info[i * LANES + d] = jnp.where(value >= 0, position, -1)

    loads[2].wait()
    token = lax.rem(lax.broadcasted_iota(jnp.int32, (tokens, rows), 1), tokens)
    seen = token >= lax.broadcasted_iota(jnp.int32, (tokens, rows), 0)
    top, mixed = attend(
        3, turn(own_ref[:, :head], own_cos, own_sin), flip(own_ref[:, head:]), seen)
    total[3] = mixed
    tops[3] = top
    for i in range(3):
        total[i] = jnp.zeros(total.shape[1:], jnp.float32)
        tops[i] = jnp.full(tops.shape[1:], LOWEST, jnp.float32)

    def holder_plane(k):
        return pop_ref[k] // (per_device * LANES)

    @pl.when(is_inner)
    def _():
        for p in range(STEPS // 2):
            query_wait(1, p)
            far_to_near(1, p).start()
        up_copy().wait_recv()
        for k in range(pops):
            merged[k] = jnp.where(holder_plane(k) == plane, two_stage[k], up_recv[k])
        cross_copy().start()
        for p in range(STEPS // 2, STEPS):
            query_wait(1, p)
            far_to_near(1, p).start()

    @pl.when(is_outer)
    def _():
        for p in range(STEPS):
            query_wait(0, p)

    def phase(i, first=0, last=LANES):
        def step(d, carry):
            at = i * LANES + d

            @pl.when(d > 0)
            def _():
                remote(
                    stage.at[0], cand.at[at], block_send.at[0], block_sem.at[at], me ^ 1).wait_recv()
            fold(i, cand[at], info[at])
            return carry
        lax.fori_loop(first, last, step, 0)

    def send_piece(i, j, p, target_plane):
        at = pl.ds(p * part, part)
        weight = jnp.maximum(total[i, head:head + 1, at], TINY)
        log_out[i, p] = tops[i, :, at] + jnp.log2(weight) * (1.0 / power)
        part_out[i, p] = (total[i, :head, at] * (1.0 / weight)).astype(jnp.bfloat16)
        log_copy(i, j, p, target_plane).start()
        part_copy(i, j, p, target_plane).start()

    def take_piece(i, j, p):
        log_copy(0, j, p, near).wait_recv()
        part_copy(0, j, p, near).wait_recv()
        ones = jnp.ones((pad, part), jnp.float32)
        blend(
            i, pl.ds(p * part, part), log_in[j, p],
            jnp.concatenate([part_in[j, p].astype(jnp.float32), ones], axis=0))

    def send_part(i, j, target_plane):
        for p in range(PARTS):
            send_piece(i, j, p, target_plane)

    def pass_part(i, target_plane):
        for p in range(PARTS):
            take_piece(i, i, p)
            send_piece(i, 3, p, target_plane)

    def spread():
        three_copy().start()
        popular_at(lane)[...] = final[...]
        four_copy(0).start()
        send_blocks(3)

    phase(order[0])

    @pl.when(is_outer)
    def _():
        send_part(0, 0, near)
        for p in range(STEPS):
            query_wait(1, p)

    @pl.when(is_inner)
    def _():
        cross_copy().wait_recv()
        for k in range(pops):
            final[k] = jnp.where(holder_plane(k) // 2 == half, merged[k], cross_recv[k])
        down_copy().start()
        for p in range(STEPS * 3 // 4, STEPS):
            own_to_near(p).start()
        spread()
        send_part(2, 2, near)

    phase(order[1])

    @pl.when(is_outer)
    def _():
        send_part(1, 1, near)
        down_copy().wait_recv()
        spread()
        for p in range(STEPS):
            query_wait(2, p)

    @pl.when(is_inner)
    def _():
        pass_part(0, far_inner)

    phase(order[2])

    @pl.when(is_outer)
    def _():
        send_part(2, 2, near)

    @pl.when(is_inner)
    def _():
        pass_part(1, far_outer)

    phase(3, 0, 2)
    remote(final, popular_at(lane ^ 2), three_send.at[0], three_sem.at[0], me ^ 1).wait_recv()
    four_copy(1).start()
    for t in (0, 1):
        remote(
            final, popular_at(lane ^ (1 + 2 * t)), three_send.at[0], three_sem.at[1 + t], me ^ 1).wait_recv()

    def popular_fold(k, carry):
        fold(3, popular[k], pop_pos[0, k])
        return carry
    lax.fori_loop(0, pops, popular_fold, 0)

    phase(3, 2, 3)
    for p in range(PARTS):
        take_piece(3, 2, p)
    phase(3, 3, 4)
    for p in range(PARTS):
        take_piece(3, 3, p)

    for g in range(rows // tokens):
        at = pl.ds(g * tokens, tokens)
        out_ref[:, g * head:(g + 1) * head] = (
            total[3, :head, at] * (1.0 / total[3, head:head + 1, at])).astype(jnp.bfloat16).T

    peers(lambda d: ask_copy(d, d).wait_send())
    for p in range(STEPS):
        own_to_near(p).wait_send()

        @pl.when(is_inner)
        def _():
            own_across(p).wait_send()
            near_across(p).wait_send()
            far_to_near(0, p).wait_send()
            far_to_near(1, p).wait_send()
    for i in range(4):
        for d in range(1, LANES):
            block_copy(i, d).wait_send()
    for copy in (zero_copy(), one_copy(), three_copy(), four_copy(0), four_copy(1)):
        copy.wait_send()
    for i in range(3):
        for p in range(PARTS):
            log_copy(i, i, p, near).wait_send()
            part_copy(i, i, p, near).wait_send()

    @pl.when(is_outer)
    def _():
        up_copy().wait_send()

    @pl.when(is_inner)
    def _():
        cross_copy().wait_send()
        down_copy().wait_send()


def plane_body(queries, own_kv, store_kv, q_start, pop_ids, pop_pos, rare_ids, rare_count, rare_pos):
    n = lax.axis_size("store")
    tokens = queries.shape[0]
    head = own_kv.shape[1] // 2
    rows = tokens * (queries.shape[1] // head)
    per_device, span, width = store_kv.shape
    requests = rare_ids.shape[1]
    pops = pop_ids.shape[0]
    longest = max(span, tokens, COARSE)
    piece = span // LANES

    half = np.arange(head) % (head // 2)
    freq = 500000.0 ** (-(2.0 * half) / head)
    sign = np.where(np.arange(head) < head // 2, -1.0, 1.0)

    def tables(positions):
        angles = positions[:, None] * freq[None, :]
        return np.cos(angles).astype(np.float32), (np.sin(angles) * sign).astype(np.float32)

    vmem = pl.BlockSpec(memory_space=pltpu.VMEM)
    smem = pl.BlockSpec(memory_space=pltpu.SMEM)
    dma = pltpu.SemaphoreType.DMA
    bf16, f32 = jnp.bfloat16, jnp.float32

    trig = np.concatenate([*tables(np.arange(COARSE) * float(COARSE)), *tables(np.arange(longest) * 1.0)])

    def blocks(count):
        return pltpu.VMEM((count, span, width), bf16)

    def pieces(*lead):
        return pltpu.VMEM((*lead, piece, width), bf16)

    return pl.pallas_call(
        functools.partial(plane_kernel, per_device, requests, pops, head ** -0.5 * np.log2(np.e).item()),
        out_shape=pltpu.VMEM(queries.shape, bf16),
        in_specs=[smem] * 6 + [pl.BlockSpec(memory_space=pl.ANY)] * 4,
        out_specs=vmem,
        scratch_shapes=[
            blocks(per_device),
            pltpu.VMEM(queries.shape, bf16), pltpu.VMEM(own_kv.shape, bf16), pltpu.VMEM(trig.shape, f32),
            pltpu.VMEM((1, 128), jnp.int32),
            pltpu.VMEM((n, 1, 128), jnp.int32),
            pltpu.SMEM((n, 1, 128), jnp.int32),
            pltpu.SMEM((4 * LANES,), jnp.int32),
            pltpu.VMEM((4, rows, head), bf16),
            pltpu.VMEM((4, head + 16, rows), f32),
            pltpu.VMEM((4, 1, rows), f32),
            blocks(4 * LANES), blocks(4 * LANES),
            pltpu.VMEM((3, PARTS, head, rows // PARTS), bf16),
            pltpu.VMEM((4, PARTS, head, rows // PARTS), bf16),
            pltpu.VMEM((3, PARTS, 1, rows // PARTS), f32), pltpu.VMEM((4, PARTS, 1, rows // PARTS), f32),
            pltpu.VMEM((pops, 2 * piece, width), bf16), pltpu.VMEM((pops, 2 * piece, width), bf16),
            pieces(pops), pieces(pops), pieces(pops), pieces(pops),
            pieces(pops), pieces(pops), pieces(pops), blocks(pops),
            dma((6,)), dma((n,)), dma((n,)), dma((5 * STEPS,)), dma((3 * STEPS,)),
            dma((4 * LANES,)), dma((4 * LANES,)),
            dma((3 * PARTS,)), dma((4 * PARTS,)), dma((3 * PARTS,)), dma((4 * PARTS,)),
            dma((2,)), dma((2,)), dma((3,)), dma((3,)), dma((3,)), dma((3,)),
        ],
        compiler_params=pltpu.CompilerParams(
            collective_id=1, has_side_effects=True, vmem_limit_bytes=60 * 2**20),
    )(pop_ids, rare_ids, rare_count, rare_pos, pop_pos, q_start, queries, own_kv, store_kv,
      trig)


def body(*args):
    requests, pops = args[6].shape[1], args[4].shape[0]
    if lax.axis_size("store") == PLANES * LANES and requests <= PLACE and pops == 4:
        return plane_body(*args)
    return direct_body(*args)


def solution(mesh):
    both = ("tenant", "store")
    in_specs = (
        P(both, None), P(both, None), P(both, None, None), P(both), P("tenant"),
        P(both, None), P(both, None), P(both), P(both, None),
    )
    return jax.shard_map(
        body, mesh=mesh, in_specs=in_specs, out_specs=P(both, None), check_vma=False)
```
